32 devices in a mesh: row: 4 (over x, core), col: 2 (over y), fiber: 4 (over z).
Axes of the slice: x: 2, y: 2, z: 4, core: 2. Of those that a mesh axis runs over, the one named last changes fastest.
Arguments:
- values: float32 [3072, 3072], P('row', ('col', 'fiber')), may hold values from -6 to 6
- tile_mask: int32 [24, 24], P('row', ('col', 'fiber')), may hold values from 0 to 1, as said below
- keep_mask: int32 [24, 24], P('row', ('col', 'fiber')), may hold values 0 or 1
Outputs:
- flows: float32 [3072, 3072], P('row', ('col', 'fiber'))
The draws below stay inside these ranges and needn't reach their ends.
Inputs may be any that keep to these rules, and one draw needn't show every extreme that they name: `tile_mask`: 1 marks a tile that holds entries; every diagonal tile is 1, and tiles with low indices are denser.
All inputs are finite; a program needn't handle non-finite values. No bound on the sum of `keep_mask` on one device may be relied on, other than what follows from the above.
Results may differ from the reference program's by a relative error of at most 0.017.
Values may be sent and summed in bfloat16 or wider, within the bound.
A program may use at most 64 MiB of HBM per device.

```python
import jax
import jax.numpy as jnp
from jax import lax

UNIT = 384
N = 3072
NTILES = 24
N_FIBER = 4


def draw_tile_mask(key, part):
    indices = jnp.arange(NTILES, dtype=jnp.int32)
    row_ids = indices[:, None]
    col_ids = indices[None, :]
    levels = max(1, (NTILES - 1).bit_length())
    agreement = jnp.zeros((NTILES, NTILES), jnp.int32)
    both_low = jnp.zeros((NTILES, NTILES), jnp.int32)
    for level in range(levels):
        row_bit = row_ids >> level & 1
        col_bit = col_ids >> level & 1
        agreement = agreement + (row_bit == col_bit).astype(jnp.int32)
        both_low = both_low + ((row_bit == 0) & (col_bit == 0)).astype(jnp.int32)
    ticket = jax.random.randint(jax.random.fold_in(key, 17), (NTILES, NTILES), 0, 2 * levels + 1)
    kept_tiles = (ticket <= agreement + both_low) | (row_ids == col_ids)
    return kept_tiles.astype(jnp.int32)


def place_ends(values, stream_key, smallest, largest):
    longest = values.shape.index(max(values.shape))
    spots = []
    for shift in (0, 1):
        where = [jax.random.randint(jax.random.fold_in(stream_key, axis), (), 0, length) for axis, length in enumerate(values.shape)]
        where[longest] = (where[longest] + shift) % values.shape[longest]
        spots.append(tuple(where))
    return values.at[spots[0]].set(smallest).at[spots[1]].set(largest)


def steps_of(stream_key, extent, cuts, low, top_value):
    gain, own = 1.0, jax.random.fold_in(stream_key, 6)
    for axis_at, parts in cuts:
        draws = jnp.exp(jax.random.uniform(jax.random.fold_in(own, axis_at), (parts,), jnp.float32, low / len(cuts), top_value / len(cuts)))
        gain = gain * jnp.repeat(draws, extent[axis_at] // parts).reshape([-1 if axis == axis_at else 1 for axis in range(len(extent))])
    return gain


def scatter_about(rng, dims, spread, most, split=(), held_as=jnp.bfloat16):
    level = steps_of(rng, dims, split, -0.22, 0.18) if split else 1.0
    result = jax.random.normal(rng, dims, jnp.float32) * spread * level
    return jnp.minimum(jnp.maximum(result, -most), most).astype(held_as)


def setup_inputs(seed: int = 0) -> dict:
    seeds = jax.random.split(jax.random.key(seed), 4)
    return {
        "values": scatter_about(seeds[0], (N, N), 1.0, 6.0, ((0, 4), (1, 8)), jnp.float32),
        "tile_mask": draw_tile_mask(jax.random.fold_in(seeds[3], 71), 0),
        "keep_mask": place_ends((jax.random.randint(seeds[2], (NTILES, NTILES), 0, 4) < 3).astype(jnp.int32), jax.random.fold_in(seeds[2], 1), 0, 1),
    }


def spread_tiles(mask, tile_size):
    count_rows, count_cols = mask.shape
    wide = jnp.broadcast_to(mask.astype(jnp.float32)[:, None, :, None], (count_rows, tile_size, count_cols, tile_size))
    return wide.reshape(count_rows * tile_size, count_cols * tile_size)


def reference(values, tile_mask, keep_mask):
    tile_size = values.shape[0] // tile_mask.shape[0]
    total = values.shape[0]
    sub_width = UNIT // N_FIBER
    weighted = (values * spread_tiles(tile_mask, tile_size)).astype(jnp.bfloat16)
    layer_cols = weighted.reshape(total, total // UNIT, N_FIBER, sub_width)
    layer_rows = weighted.reshape(total // UNIT, N_FIBER, sub_width, total)

    def add_layer(layer, running):
        left_part = lax.dynamic_index_in_dim(layer_cols, layer, 2, keepdims=False).reshape(total, (total // UNIT) * sub_width)
        right_part = lax.dynamic_index_in_dim(layer_rows, layer, 1, keepdims=False).reshape((total // UNIT) * sub_width, total)
        product = jnp.dot(left_part, right_part, preferred_element_type=jnp.float32)
        return running + product.astype(jnp.bfloat16).astype(jnp.float32)

    expanded = lax.fori_loop(0, N_FIBER, add_layer, jnp.zeros((total, total), jnp.float32))
    squared = expanded * expanded
    col_scale = jnp.mean(squared, axis=0) + 1e-6
    return spread_tiles(keep_mask, tile_size) * squared / col_scale[None, :]
```

```python
import functools

import jax
import jax.numpy as jnp
from jax import lax
from jax.experimental import pallas as pl
from jax.experimental.pallas import tpu as pltpu
from jax.sharding import PartitionSpec as P

MESH = pl.DeviceIdType.MESH
CHUNKS = 8
HELP = 2
FETCH = 6
ANSWER = 7
LAG = 2
VMEM_LIMIT = 62 * 1024 * 1024


def kernel(
    n_row, n_col, n_fib, helps, tile_hbm, values_hbm, own, inverse_ref,
    tile_ref, values_ref, left, right, ahead, part_out, part_in, sums,
    right_far, help_own, help_out, help_in, helped, load_sem,
    send_up, send_down, recv_left, send_right, recv_right, send_pair, recv_pair,
    send_part, recv_part, send_sum, recv_sum,
    send_far, send_side, recv_far, send_far_pair, recv_far_pair,
    send_help, recv_help, send_done, recv_done,
):
    r, c, f = lax.axis_index("row"), lax.axis_index("col"), lax.axis_index("fiber")
    rows, unit = values_ref.shape
    tile = unit // tile_ref.shape[0]
    step = rows // CHUNKS
    parts = rows // unit
    group = n_row // n_col
    owner, seat = r // group, lax.rem(r, group)

    load = pltpu.make_async_copy(values_hbm, values_ref, load_sem.at[0])
    load.start()
    load_tile = pltpu.make_async_copy(tile_hbm, tile_ref, load_sem.at[1])
    load_tile.start()

    barrier = pltpu.get_barrier_semaphore()
    for dr in range(n_row):
        for dc in range(n_col):
            if dr or dc:
                pl.semaphore_signal(
                    barrier, inc=1, device_id_type=MESH,
                    device_id=(lax.rem(r + dr, n_row), lax.rem(c + dc, n_col), f),
                )

    has_down, has_up = f > 0, f < n_fib - 1
    outer = jnp.logical_not(has_down & has_up)
    helper = (f == 1) | (f == n_fib - 2)
    mate = jnp.where(outer, jnp.where(has_down, f - 1, 1), jnp.where(f == 1, 0, n_fib - 1))
    mine = owner == c

    @pl.when(has_down)
    def _():
        pl.semaphore_signal(barrier, inc=1, device_id=(r, c, f - 1), device_id_type=MESH)

    @pl.when(has_up)
    def _():
        pl.semaphore_signal(barrier, inc=1, device_id=(r, c, f + 1), device_id_type=MESH)

    load_tile.wait()
    load.wait()

    for i in range(rows // tile):
        for j in range(unit // tile):
            at = (pl.ds(i * tile, tile), pl.ds(j * tile, tile))
            masked = values_ref[at] * tile_ref[j, i].astype(jnp.float32)
            left[f, i * tile:(i + 1) * tile, j * tile:(j + 1) * tile] = masked.astype(jnp.bfloat16)

    neighbours = has_down.astype(jnp.int32) + has_up.astype(jnp.int32)
    pl.semaphore_wait(barrier, n_row * n_col - 1 + neighbours)

    def chunk(i):
        return pl.ds(pl.multiple_of(i * step, step), step)

    def along(source, i, up):
        part = left.at[source, chunk(i)]
        return pltpu.make_async_remote_copy(
            src_ref=part, dst_ref=part,
            send_sem=(send_up if up else send_down).at[source, i],
            recv_sem=recv_left.at[source, i],
            device_id=(r, c, f + 1 if up else f - 1), device_id_type=MESH,
        )

    def sends_up(i):
        return has_up & ((i >= helps) | (f + 1 < n_fib - 1))

    def sends_down(i):
        return has_down & ((i >= helps) | (f - 1 > 0))

    def gets_up(i):
        return (i >= helps) | has_up

    def gets_down(i):
        return (i >= helps) | has_down

    def right_at(ref, col, place, b):
        return ref.at[
            pl.ds(pl.multiple_of(place * rows + b * unit, unit), unit),
            pl.ds(pl.multiple_of(col * unit, unit), unit),
        ]

    def block(source, b):
        return left.at[source, pl.ds(b * unit, unit)]

    def to_right(t, b):
        return pltpu.make_async_remote_copy(
            src_ref=block(f, b), dst_ref=right_at(right, c, seat, b),
            send_sem=send_right.at[t, b], recv_sem=recv_right.at[c, b],
            device_id=(t * group + seat, owner, f), device_id_type=MESH,
        )

    def came_right(col, b):
        return pltpu.make_async_remote_copy(
            src_ref=block(f, b), dst_ref=right_at(right, col, seat, b),
            send_sem=send_right.at[0, b], recv_sem=recv_right.at[col, b],
            device_id=(r, c, f), device_id_type=MESH,
        )

    def to_far(col, b):
        return pltpu.make_async_remote_copy(
            src_ref=right_at(right, col, seat, b), dst_ref=right_at(right_far, col, seat, b),
            send_sem=send_far.at[col, b], recv_sem=recv_far.at[col, b],
            device_id=(r, c, mate), device_id_type=MESH,
        )

    def to_side(t, b):
        return pltpu.make_async_remote_copy(
            src_ref=block(mate, b), dst_ref=right_at(right_far, c, seat, b),
            send_sem=send_side.at[t, b], recv_sem=recv_far.at[c, b],
            device_id=(t * group + seat, c, f), device_id_type=MESH,
        )

    def came_far(col, b):
        return pltpu.make_async_remote_copy(
            src_ref=block(f, b), dst_ref=right_at(right_far, col, seat, b),
            send_sem=send_far.at[col, b], recv_sem=recv_far.at[col, b],
            device_id=(r, c, f), device_id_type=MESH,
        )

    def pairing(ref, sends, recvs):
        def to_pair(col, b, other):
            return pltpu.make_async_remote_copy(
                src_ref=right_at(ref, col, seat, b), dst_ref=right_at(ref, col, seat, b),
                send_sem=sends.at[col, b, other], recv_sem=recvs.at[col, b, seat],
                device_id=(owner * group + other, c, f), device_id_type=MESH,
            )

        def came_pair(col, b, other):
            return pltpu.make_async_remote_copy(
                src_ref=right_at(ref, col, other, b), dst_ref=right_at(ref, col, other, b),
                send_sem=sends.at[col, b, other], recv_sem=recvs.at[col, b, other],
                device_id=(r, c, f), device_id_type=MESH,
            )

        return to_pair, came_pair

    to_pair, came_pair = pairing(right, send_pair, recv_pair)
    to_far_pair, came_far_pair = pairing(right_far, send_far_pair, recv_far_pair)

    def crossing(out, into, sends, recvs):
        def to_col(col, i):
            return pltpu.make_async_remote_copy(
                src_ref=out.at[col, chunk(i)], dst_ref=into.at[c, chunk(i)],
                send_sem=sends.at[col, i], recv_sem=recvs.at[c, i],
                device_id=(r, col, f), device_id_type=MESH,
            )

        def came_col(col, i):
            return pltpu.make_async_remote_copy(
                src_ref=out.at[col, chunk(i)], dst_ref=into.at[col, chunk(i)],
                send_sem=sends.at[col, i], recv_sem=recvs.at[col, i],
                device_id=(r, col, f), device_id_type=MESH,
            )

        return to_col, came_col

    to_col, came_col = crossing(part_out, part_in, send_part, recv_part)
    to_help, came_help = crossing(help_out, help_in, send_help, recv_help)

    def to_done(i):
        return pltpu.make_async_remote_copy(
            src_ref=helped.at[chunk(i)], dst_ref=helped.at[chunk(i)],
            send_sem=send_done.at[i], recv_sem=recv_done.at[i],
            device_id=(r, c, mate), device_id_type=MESH,
        )

    def served(place, b):
        return place * parts + b != mate

    def to_serve(b):
        return seat * parts + b != f

    @pl.loop(0, CHUNKS)
    def _(i):
        @pl.when(sends_down(i))
        def _():
            along(f, i, False).start()

        @pl.when(sends_up(i))
        def _():
            along(f, i, True).start()

    for b in range(parts):
        for t in range(n_row // group):
            @pl.when(jnp.logical_not(mine & (owner == t)))
            def _():
                to_right(t, b).start()

    @pl.when(mine)
    def _():
        for b in range(parts):
            spot = right_at(right, c, seat, b)
            spot[...] = left[f, b * unit:(b + 1) * unit]

    def relay(d, i):
        @pl.when((f - d >= 0) & gets_up(i))
        def _():
            along(f - d, i, True).wait_recv()

            @pl.when(sends_up(i))
            def _():
                along(f - d, i, True).start()

        @pl.when((f + d < n_fib) & gets_down(i))
        def _():
            along(f + d, i, False).wait_recv()

            @pl.when(sends_down(i))
            def _():
                along(f + d, i, False).start()

    @pl.loop(0, CHUNKS)
    def _(i):
        relay(1, i)

    if helps:
        @pl.when(helper & mine)
        def _():
            for b in range(parts):
                @pl.when(served(seat, b))
                def _():
                    for t in range(n_row // group):
                        @pl.when(owner != t)
                        def _():
                            to_side(t, b).start()

                    spot = right_at(right_far, c, seat, b)
                    spot[...] = left[mate, b * unit:(b + 1) * unit]

    for b in range(parts):
        for col in range(n_col):
            @pl.when(jnp.logical_not(mine & (c == col)))
            def _():
                came_right(col, b).wait_recv()

            if helps:
                @pl.when(outer & (c != col) & to_serve(b))
                def _():
                    to_far(col, b).start()

            for other in range(group):
                @pl.when(seat != other)
                def _():
                    to_pair(col, b, other).start()

    for b in range(parts):
        for col in range(n_col):
            for other in range(group):
                @pl.when(seat != other)
                def _():
                    came_pair(col, b, other).wait_recv()

    near = jnp.where(has_down, f - 1, 1)
    first = jnp.where(has_down, f - 1, 0)
    ready = min(n_fib, 2)

    def product(ref, part, col, k):
        return jnp.dot(
            left[k, part, :],
            ref[
                pl.ds(pl.multiple_of(k * unit, unit), unit),
                pl.ds(pl.multiple_of(col * unit, unit), unit),
            ],
            preferred_element_type=jnp.float32,
        )

    def col_at(shift):
        return lax.rem(c + shift, n_col)

    def total_at(shift):
        return own if shift == 0 else ahead.at[shift - 1]

    wide = step * HELP

    @pl.loop(0, CHUNKS // HELP)
    def _(i):
        part = pl.ds(pl.multiple_of(i * wide, wide), wide)
        for shift in range(n_col):
            total_at(shift)[part, :] = product(right, part, col_at(shift), f)
        if ready > 1:
            @pl.when(jnp.logical_not(outer & (i * HELP < helps)))
            def _():
                for shift in range(n_col):
                    total_at(shift)[part, :] += product(right, part, col_at(shift), near)

    sums[r] = jnp.zeros((8, unit), jnp.float32)

    def combine(i, answered=False):
        part = chunk(i)
        expanded = own[part, :]
        for shift in range(1, n_col):
            came_col(col_at(shift), i).wait_recv()
            expanded += part_in[col_at(shift), part, :].astype(jnp.float32)
        if answered:
            to_done(i).wait_recv()
            expanded += helped[part, :].astype(jnp.float32)
        squared = expanded * expanded
        own[part, :] = squared
        sums[r] += jnp.sum(squared.reshape(step // 8, 8, unit), axis=0)

    def fetch():
        for b in range(parts):
            @pl.when(served(seat, b))
            def _():
                for col in range(n_col):
                    @pl.when(jnp.logical_not(mine & (c == col)))
                    def _():
                        came_far(col, b).wait_recv()

                    for other in range(group):
                        @pl.when(seat != other)
                        def _():
                            to_far_pair(col, b, other).start()

    def answer():
        for b in range(parts):
            for other in range(group):
                @pl.when((seat != other) & served(other, b))
                def _():
                    for col in range(n_col):
                        came_far_pair(col, b, other).wait_recv()

        part = pl.ds(0, helps * step)
        for shift in list(range(1, n_col)) + [0]:
            col = col_at(shift)
            total = product(right_far, part, col, lax.rem(mate + 1, n_fib))
            for k in range(2, n_fib):
                total += product(right_far, part, col, lax.rem(mate + k, n_fib))
            if shift:
                help_out[col, :, :] = total.astype(jnp.bfloat16)
                for i in range(helps):
                    to_help(col, i).start()
            else:
                help_own[...] = total

    @pl.loop(0, CHUNKS)
    def _(i):
        for d in range(2, n_fib):
            relay(d, i)

        if helps:
            @pl.when(helper & (i == FETCH))
            def _():
                fetch()

            @pl.when(helper & (i == ANSWER))
            def _():
                answer()

        part = chunk(i)
        full = jnp.logical_not(outer & (i < helps))

        @pl.when(full)
        def _():
            for shift in range(1, n_col):
                total = ahead[shift - 1, part, :]
                for k in range(ready, n_fib):
                    total += product(right, part, col_at(shift), lax.rem(first + k, n_fib))
                ahead[shift - 1, part, :] = total

        for shift in range(1, n_col):
            col = col_at(shift)
            part_out[col, part, :] = ahead[shift - 1, part, :].astype(jnp.bfloat16)
            to_col(col, i).start()

        @pl.when(full)
        def _():
            total = own[part, :]
            for k in range(ready, n_fib):
                total += product(right, part, c, lax.rem(first + k, n_fib))
            own[part, :] = total

        @pl.when((i >= LAG) & jnp.logical_not(outer & (i - LAG < helps)))
        def _():
            combine(i - LAG)

    @pl.loop(CHUNKS - LAG, CHUNKS - 1)
    def _(i):
        combine(i)

    if helps:
        @pl.when(helper)
        def _():
            @pl.loop(0, helps)
            def _(i):
                part = chunk(i)
                total = help_own[part, :]
                for shift in range(1, n_col):
                    came_help(col_at(shift), i).wait_recv()
                    total += help_in[col_at(shift), part, :].astype(jnp.float32)
                helped[part, :] = total.astype(jnp.bfloat16)
                to_done(i).start()

    combine(CHUNKS - 1)

    if helps:
        @pl.when(outer)
        def _():
            @pl.loop(0, helps)
            def _(i):
                combine(i, True)

    def to_row(shift):
        return pltpu.make_async_remote_copy(
            src_ref=sums.at[r], dst_ref=sums.at[r],
            send_sem=send_sum.at[shift], recv_sem=recv_sum.at[r],
            device_id=(lax.rem(r + shift, n_row), c, f), device_id_type=MESH,
        )

    def came_row(other):
        return pltpu.make_async_remote_copy(
            src_ref=sums.at[r], dst_ref=sums.at[other],
            send_sem=send_sum.at[0], recv_sem=recv_sum.at[other],
            device_id=(other, c, f), device_id_type=MESH,
        )

    for shift in range(1, n_row):
        to_row(shift).start()
    for shift in range(1, n_row):
        came_row(lax.rem(r + shift, n_row)).wait_recv()
    total = sums[0]
    for other in range(1, n_row):
        total += sums[other]
    scale = jnp.sum(total, axis=0, keepdims=True) / (rows * n_row) + 1e-6
    inverse_ref[...] = jnp.broadcast_to(1.0 / scale, inverse_ref.shape)

    @pl.loop(0, CHUNKS)
    def _(i):
        for source in range(n_fib):
            @pl.when(sends_up(i) & (source <= f))
            def _():
                along(source, i, True).wait_send()

            @pl.when(sends_down(i) & (source >= f))
            def _():
                along(source, i, False).wait_send()

        for shift in range(1, n_col):
            to_col(col_at(shift), i).wait_send()

    for b in range(parts):
        for t in range(n_row // group):
            @pl.when(jnp.logical_not(mine & (owner == t)))
            def _():
                to_right(t, b).wait_send()

        for col in range(n_col):
            for other in range(group):
                @pl.when(seat != other)
                def _():
                    to_pair(col, b, other).wait_send()

    if helps:
        @pl.when(helper)
        def _():
            for b in range(parts):
                @pl.when(served(seat, b))
                def _():
                    for t in range(n_row // group):
                        @pl.when(mine & (owner != t))
                        def _():
                            to_side(t, b).wait_send()

                    for col in range(n_col):
                        for other in range(group):
                            @pl.when(seat != other)
                            def _():
                                to_far_pair(col, b, other).wait_send()

            for i in range(helps):
                for shift in range(1, n_col):
                    to_help(col_at(shift), i).wait_send()
                to_done(i).wait_send()

        @pl.when(outer)
        def _():
            for b in range(parts):
                for col in range(n_col):
                    @pl.when((c != col) & to_serve(b))
                    def _():
                        to_far(col, b).wait_send()

    for shift in range(1, n_row):
        to_row(shift).wait_send()


def prune(keep_ref, squared_ref, inverse_ref, out_hbm, out_vmem, sem):
    tile = out_vmem.shape[1] // keep_ref.shape[0]
    copies = []
    for i in range(keep_ref.shape[1]):
        down = slice(i * tile, (i + 1) * tile)
        for j in range(keep_ref.shape[0]):
            across = slice(j * tile, (j + 1) * tile)
            factor = inverse_ref[0:1, across] * keep_ref[j, i].astype(jnp.float32)
            out_vmem[down, across] = squared_ref[down, across] * factor
        copy = pltpu.make_async_copy(out_vmem.at[down], out_hbm.at[down], sem.at[i])
        copy.start()
        copies.append(copy)
    for copy in copies:
        copy.wait()


def solution(mesh):
    n_row, n_col, n_fib = (mesh.shape[name] for name in ("row", "col", "fiber"))
    group = n_row // n_col
    helps = HELP if n_fib > 3 else 0

    def local(values, tile_mask, keep_mask):
        rows, unit = values.shape
        dma = pltpu.SemaphoreType.DMA
        parts = rows // unit
        few = rows // CHUNKS * HELP
        squared, inverse = pl.pallas_call(
            functools.partial(kernel, n_row, n_col, n_fib, helps),
            out_shape=(
                pltpu.VMEM((rows, unit), jnp.float32),
                pltpu.VMEM((8, unit), jnp.float32),
            ),
            in_specs=[
                pl.BlockSpec(memory_space=pltpu.HBM),
                pl.BlockSpec(memory_space=pltpu.HBM),
            ],
            out_specs=(
                pl.BlockSpec(memory_space=pltpu.VMEM),
                pl.BlockSpec(memory_space=pltpu.VMEM),
            ),
            scratch_shapes=[
                pltpu.SMEM(tile_mask.shape[::-1], jnp.int32),
                pltpu.VMEM((rows, unit), jnp.float32),
                pltpu.VMEM((n_fib, rows, unit), jnp.bfloat16),
                pltpu.VMEM((group * rows, n_col * unit), jnp.bfloat16),
                pltpu.VMEM((n_col - 1, rows, unit), jnp.float32),
                pltpu.VMEM((n_col, rows, unit), jnp.bfloat16),
                pltpu.VMEM((n_col, rows, unit), jnp.bfloat16),
                pltpu.VMEM((n_row, 8, unit), jnp.float32),
                pltpu.VMEM((group * rows, n_col * unit), jnp.bfloat16),
                pltpu.VMEM((few, unit), jnp.float32),
                pltpu.VMEM((n_col, few, unit), jnp.bfloat16),
                pltpu.VMEM((n_col, few, unit), jnp.bfloat16),
                pltpu.VMEM((few, unit), jnp.bfloat16),
                dma((2,)),
                dma((n_fib, CHUNKS)),
                dma((n_fib, CHUNKS)),
                dma((n_fib, CHUNKS)),
                dma((n_row // group, parts)),
                dma((n_col, parts)),
                dma((n_col, parts, group)),
                dma((n_col, parts, group)),
                dma((n_col, CHUNKS)),
                dma((n_col, CHUNKS)),
                dma((n_row,)),
                dma((n_row,)),
                dma((n_col, parts)),
                dma((n_row // group, parts)),
                dma((n_col, parts)),
                dma((n_col, parts, group)),
                dma((n_col, parts, group)),
                dma((n_col, HELP)),
                dma((n_col, HELP)),
                dma((HELP,)),
                dma((HELP,)),
            ],
            compiler_params=pltpu.CompilerParams(
                collective_id=0, has_side_effects=True, vmem_limit_bytes=VMEM_LIMIT
            ),
            name="expand",
        )(tile_mask.T, values)
        return pl.pallas_call(
            prune,
            out_shape=jax.ShapeDtypeStruct((rows, unit), jnp.float32),
            in_specs=[
                pl.BlockSpec(memory_space=pltpu.SMEM),
                pl.BlockSpec(memory_space=pltpu.VMEM),
                pl.BlockSpec(memory_space=pltpu.VMEM),
            ],
            out_specs=pl.BlockSpec(memory_space=pl.ANY),
            scratch_shapes=[
                pltpu.VMEM((rows, unit), jnp.float32),
                dma((keep_mask.shape[0],)),
            ],
            compiler_params=pltpu.CompilerParams(vmem_limit_bytes=8 * 1024 * 1024),
            name="prune",
        )(keep_mask.T, squared, inverse)

    spec = P("row", ("col", "fiber"))
    return jax.shard_map(
        local, mesh=mesh, in_specs=(spec, spec, spec), out_specs=spec, check_vma=False
    )
```

```python
import functools

import jax
import jax.numpy as jnp
from jax import lax
from jax.experimental import pallas as pl
from jax.experimental.pallas import tpu as pltpu
from jax.sharding import PartitionSpec as P

MESH = pl.DeviceIdType.MESH
CHUNKS = 8
HELP = 2
AHEAD = 3
FETCH = 4
ANSWER = 5
LAG = 3
VMEM_LIMIT = 62 * 1024 * 1024


def kernel(
    n_row, n_col, n_fib, helps, tile_hbm, values_hbm, own, inverse_ref,
    tile_ref, values_ref, left, right, part_out, part_in, sums,
    right_far, help_own, help_out, help_in, helped, load_sem,
    sent_left, sent_right, sent_pair, sent_part, sent_sum, sent_far, sent_far_pair, sent_help, sent_done,
    recv_left, recv_right, recv_pair, recv_part, recv_sum,
    recv_far, recv_far_pair, recv_help, recv_done,
):
    r, c, f = lax.axis_index("row"), lax.axis_index("col"), lax.axis_index("fiber")
    rows, unit = values_ref.shape
    tile = unit // tile_ref.shape[0]
    step = rows // CHUNKS
    parts = rows // unit
    group = n_row // n_col
    owner, seat = r // group, lax.rem(r, group)

    load = pltpu.make_async_copy(values_hbm, values_ref, load_sem.at[0])
    load.start()
    load_tile = pltpu.make_async_copy(tile_hbm, tile_ref, load_sem.at[1])
    load_tile.start()

    barrier = pltpu.get_barrier_semaphore()
    for dr in range(n_row):
        for dc in range(n_col):
            if dr or dc:
                pl.semaphore_signal(
                    barrier, inc=1, device_id_type=MESH,
                    device_id=(lax.rem(r + dr, n_row), lax.rem(c + dc, n_col), f),
                )

    has_down, has_up = f > 0, f < n_fib - 1
    outer = jnp.logical_not(has_down & has_up)
    helper = (f == 1) | (f == n_fib - 2)
    mate = jnp.where(outer, jnp.where(has_down, f - 1, 1), jnp.where(f == 1, 0, n_fib - 1))
    mine = owner == c

    @pl.when(has_down)
    def _():
        pl.semaphore_signal(barrier, inc=1, device_id=(r, c, f - 1), device_id_type=MESH)

    @pl.when(has_up)
    def _():
        pl.semaphore_signal(barrier, inc=1, device_id=(r, c, f + 1), device_id_type=MESH)

    load_tile.wait()
    load.wait()

    for i in range(rows // tile):
        for j in range(unit // tile):
            at = (pl.ds(i * tile, tile), pl.ds(j * tile, tile))
            masked = values_ref[at] * tile_ref[j, i].astype(jnp.float32)
            left[f, i * tile:(i + 1) * tile, j * tile:(j + 1) * tile] = masked.astype(jnp.bfloat16)

    neighbours = has_down.astype(jnp.int32) + has_up.astype(jnp.int32)
    pl.semaphore_wait(barrier, n_row * n_col - 1 + neighbours)

    def chunk(i):
        return pl.ds(pl.multiple_of(i * step, step), step)

    def along(source, i, up):
        part = left.at[source, chunk(i)]
        return pltpu.make_async_remote_copy(
            src_ref=part, dst_ref=part,
            send_sem=sent_left.at[int(up)], recv_sem=recv_left.at[source if up else source - 1, i],
            device_id=(r, c, f + 1 if up else f - 1), device_id_type=MESH,
        )

    def sends_up(i):
        return has_up & ((i >= helps) | (f + 1 < n_fib - 1))

    def sends_down(i):
        return has_down & ((i >= helps) | (f - 1 > 0))

    def gets_up(i):
        return (i >= helps) | has_up

    def gets_down(i):
        return (i >= helps) | has_down

    def right_at(ref, col, place, b):
        return ref.at[
            pl.ds(pl.multiple_of(place * rows + b * unit, unit), unit),
            pl.ds(pl.multiple_of(col * unit, unit), unit),
        ]

    def block(source, b):
        return left.at[source, pl.ds(b * unit, unit)]

    def to_right(t, b):
        return pltpu.make_async_remote_copy(
            src_ref=block(f, b), dst_ref=right_at(right, c, seat, b),
            send_sem=sent_right.at[0], recv_sem=recv_right.at[c, b],
            device_id=(t * group + seat, owner, f), device_id_type=MESH,
        )

    def came_right(col, b):
        return pltpu.make_async_remote_copy(
            src_ref=block(f, b), dst_ref=right_at(right, col, seat, b),
            send_sem=sent_right.at[0], recv_sem=recv_right.at[col, b],
            device_id=(r, c, f), device_id_type=MESH,
        )

    def to_far(col, b):
        return pltpu.make_async_remote_copy(
            src_ref=right_at(right, col, seat, b), dst_ref=right_at(right_far, col, seat, b),
            send_sem=sent_far.at[0], recv_sem=recv_far.at[col, b],
            device_id=(r, c, mate), device_id_type=MESH,
        )

    def to_side(t, b):
        return pltpu.make_async_remote_copy(
            src_ref=block(mate, b), dst_ref=right_at(right_far, c, seat, b),
            send_sem=sent_far.at[0], recv_sem=recv_far.at[c, b],
            device_id=(t * group + seat, c, f), device_id_type=MESH,
        )

    def came_far(col, b):
        return pltpu.make_async_remote_copy(
            src_ref=block(f, b), dst_ref=right_at(right_far, col, seat, b),
            send_sem=sent_far.at[0], recv_sem=recv_far.at[col, b],
            device_id=(r, c, f), device_id_type=MESH,
        )

    def pairing(ref, send, recv):
        def to_pair(col, b, other):
            return pltpu.make_async_remote_copy(
                src_ref=right_at(ref, col, seat, b), dst_ref=right_at(ref, col, seat, b),
                send_sem=send.at[0], recv_sem=recv.at[seat],
                device_id=(owner * group + other, c, f), device_id_type=MESH,
            )

        def came_pair(other, blocks):
            theirs = ref.at[pl.ds(other * rows, blocks * unit)]
            return pltpu.make_async_remote_copy(
                src_ref=theirs, dst_ref=theirs, send_sem=send.at[0], recv_sem=recv.at[other],
                device_id=(r, c, f), device_id_type=MESH,
            )

        return to_pair, came_pair

    to_pair, came_pair = pairing(right, sent_pair, recv_pair)
    to_far_pair, came_far_pair = pairing(right_far, sent_far_pair, recv_far_pair)

    def crossing(out, into, send, recv):
        def to_col(col, i):
            return pltpu.make_async_remote_copy(
                src_ref=out.at[col, chunk(i)], dst_ref=into.at[c, chunk(i)],
                send_sem=send.at[0], recv_sem=recv.at[lax.rem(c - col + n_col, n_col) - 1, i],
                device_id=(r, col, f), device_id_type=MESH,
            )

        def came_col(col, i):
            return pltpu.make_async_remote_copy(
                src_ref=out.at[col, chunk(i)], dst_ref=into.at[col, chunk(i)],
                send_sem=send.at[0], recv_sem=recv.at[lax.rem(col - c + n_col, n_col) - 1, i],
                device_id=(r, col, f), device_id_type=MESH,
            )

        return to_col, came_col

    to_col, came_col = crossing(part_out, part_in, sent_part, recv_part)
    to_help, came_help = crossing(help_out, help_in, sent_help, recv_help)

    def to_done(i):
        return pltpu.make_async_remote_copy(
            src_ref=helped.at[chunk(i)], dst_ref=helped.at[chunk(i)],
            send_sem=sent_done.at[0], recv_sem=recv_done.at[i],
            device_id=(r, c, mate), device_id_type=MESH,
        )

    def skips(place, far):
        return (far >= place * parts) & (far < (place + 1) * parts)

    def served(place, b):
        return place * parts + b != mate

    def to_serve(b):
        return seat * parts + b != f

    def send_own(i, now_down, now_up):
        @pl.when(sends_down(i) & now_down)
        def _():
            along(f, i, False).start()

        @pl.when(sends_up(i) & now_up)
        def _():
            along(f, i, True).start()

    last = max(n_fib - 3, 0) * AHEAD
    before = last + 2
    direct_down = outer | (f == 1)
    direct_up = outer | (f == n_fib - 2)

    @pl.loop(0, CHUNKS)
    def _(i):
        send_own(i, direct_down | (i < AHEAD), direct_up | (i < AHEAD))

    for b in range(parts):
        for t in range(n_row // group):
            @pl.when(jnp.logical_not(mine & (owner == t)))
            def _():
                to_right(t, b).start()

    @pl.when(mine)
    def _():
        for b in range(parts):
            spot = right_at(right, c, seat, b)
            spot[...] = left[f, b * unit:(b + 1) * unit]

    def pass_up(d, i):
        @pl.when((f - d >= 0) & gets_up(i))
        def _():
            along(f - d, i, True).wait_recv()

            @pl.when(sends_up(i))
            def _():
                along(f - d, i, True).start()

    def pass_down(d, i):
        @pl.when((f + d < n_fib) & gets_down(i))
        def _():
            along(f + d, i, False).wait_recv()

            @pl.when(sends_down(i))
            def _():
                along(f + d, i, False).start()

    def relay(s):
        @pl.when(s < CHUNKS - AHEAD)
        def _():
            send_own(s + AHEAD, jnp.logical_not(direct_down), jnp.logical_not(direct_up))

        @pl.when((s < CHUNKS) & ((s < before) | (f != 1)))
        def _():
            pass_up(1, s)

        @pl.when((s < CHUNKS) & ((s < before) | (f != n_fib - 2)))
        def _():
            pass_down(1, s)

        for d in range(2, n_fib - 1):
            i = s - (d - 1) * AHEAD

            @pl.when((i >= 0) & (i < CHUNKS))
            def _():
                pass_up(d, i)
                pass_down(d, i)

    def side(b):
        @pl.when(helper & mine & served(seat, b))
        def _():
            for t in range(n_row // group):
                @pl.when(owner != t)
                def _():
                    to_side(t, b).start()

            spot = right_at(right_far, c, seat, b)
            spot[...] = left[mate, b * unit:(b + 1) * unit]

    early = [b for b in range(parts) if (b + 1) * unit <= before * step]

    @pl.when(jnp.logical_not(outer))
    def _():
        @pl.loop(0, before)
        def _(s):
            relay(s)

        if helps:
            for b in early:
                side(b)

        @pl.loop(before, CHUNKS)
        def _(i):
            @pl.when(f == 1)
            def _():
                pass_up(1, i)

            @pl.when(f == n_fib - 2)
            def _():
                pass_down(1, i)

        if helps:
            for b in range(len(early), parts):
                side(b)

    for b in range(parts):
        for col in range(n_col):
            @pl.when(jnp.logical_not(mine & (c == col)))
            def _():
                came_right(col, b).wait_recv()

            if helps:
                @pl.when(outer & (c != col) & to_serve(b))
                def _():
                    to_far(col, b).start()

            for other in range(group):
                @pl.when(seat != other)
                def _():
                    to_pair(col, b, other).start()

    for other in range(group):
        @pl.when(seat != other)
        def _():
            came_pair(other, parts).wait_recv()

    def product(ref, part, col, k):
        return jnp.dot(
            left[k, part, :],
            ref[
                pl.ds(pl.multiple_of(k * unit, unit), unit),
                pl.ds(pl.multiple_of(col * unit, unit), unit),
            ],
            preferred_element_type=jnp.float32,
        )

    def all_products(part, col):
        total = product(right, part, col, 0)
        for k in range(1, n_fib):
            total += product(right, part, col, k)
        return total

    def col_at(shift):
        return lax.rem(c + shift, n_col)

    sums[r] = jnp.zeros((8, unit), jnp.float32)

    def combine(i, answered=False):
        part = chunk(i)
        expanded = own[part, :]
        for shift in range(1, n_col):
            came_col(col_at(shift), i).wait_recv()
            expanded += part_in[col_at(shift), part, :].astype(jnp.float32)
        if answered:
            to_done(i).wait_recv()
            expanded += helped[part, :].astype(jnp.float32)
        squared = expanded * expanded
        own[part, :] = squared
        sums[r] += jnp.sum(squared.reshape(step // 8, 8, unit), axis=0)

    def fetch():
        for b in range(parts):
            @pl.when(served(seat, b))
            def _():
                for col in range(n_col):
                    @pl.when(jnp.logical_not(mine & (c == col)))
                    def _():
                        came_far(col, b).wait_recv()

                    for other in range(group):
                        @pl.when(seat != other)
                        def _():
                            to_far_pair(col, b, other).start()

    def answer():
        for other in range(group):
            for skipped in range(2):
                @pl.when((seat != other) & (skips(other, mate) == bool(skipped)))
                def _():
                    came_far_pair(other, parts - skipped).wait_recv()

        part = pl.ds(0, helps * step)
        for shift in list(range(1, n_col)) + [0]:
            col = col_at(shift)
            total = product(right_far, part, col, lax.rem(mate + 1, n_fib))
            for k in range(2, n_fib):
                total += product(right_far, part, col, lax.rem(mate + k, n_fib))
            if shift:
                help_out[col, :, :] = total.astype(jnp.bfloat16)
                for i in range(helps):
                    to_help(col, i).start()
            else:
                help_own[...] = total

    @pl.loop(0, CHUNKS)
    def _(i):
        part = chunk(i)
        full = jnp.logical_not(outer & (i < helps))

        @pl.when(outer & full)
        def _():
            for d in range(1, n_fib):
                pass_up(d, i)
                pass_down(d, i)

        if helps:
            @pl.when(helper & (i == FETCH))
            def _():
                fetch()

            @pl.when(helper & (i == ANSWER))
            def _():
                answer()

        @pl.when(full)
        def _():
            for shift in range(1, n_col):
                col = col_at(shift)
                part_out[col, part, :] = all_products(part, col).astype(jnp.bfloat16)

        @pl.when(jnp.logical_not(full))
        def _():
            for shift in range(1, n_col):
                col = col_at(shift)
                part_out[col, part, :] = product(right, part, col, f).astype(jnp.bfloat16)

        for shift in range(1, n_col):
            to_col(col_at(shift), i).start()

        @pl.when(full)
        def _():
            own[part, :] = all_products(part, c)

        @pl.when(jnp.logical_not(full))
        def _():
            own[part, :] = product(right, part, c, f)

        @pl.when(jnp.logical_not(outer) & (i + before < CHUNKS + last))
        def _():
            relay(i + before)

        @pl.when((i >= LAG) & jnp.logical_not(outer & (i - LAG < helps)))
        def _():
            combine(i - LAG)

    @pl.loop(CHUNKS - LAG, CHUNKS - 1)
    def _(i):
        combine(i)

    if helps:
        @pl.when(helper)
        def _():
            @pl.loop(0, helps)
            def _(i):
                part = chunk(i)
                total = help_own[part, :]
                for shift in range(1, n_col):
                    came_help(col_at(shift), i).wait_recv()
                    total += help_in[col_at(shift), part, :].astype(jnp.float32)
                helped[part, :] = total.astype(jnp.bfloat16)
                to_done(i).start()

    combine(CHUNKS - 1)

    if helps:
        @pl.when(outer)
        def _():
            @pl.loop(0, helps)
            def _(i):
                combine(i, True)

    def to_row(shift):
        return pltpu.make_async_remote_copy(
            src_ref=sums.at[r], dst_ref=sums.at[r],
            send_sem=sent_sum.at[0], recv_sem=recv_sum.at[0],
            device_id=(lax.rem(r + shift, n_row), c, f), device_id_type=MESH,
        )

    def came_rows():
        return pltpu.make_async_remote_copy(
            src_ref=sums.at[pl.ds(0, n_row - 1)], dst_ref=sums.at[pl.ds(0, n_row - 1)],
            send_sem=sent_sum.at[0], recv_sem=recv_sum.at[0],
            device_id=(r, c, f), device_id_type=MESH,
        )

    for shift in range(1, n_row):
        to_row(shift).start()
    came_rows().wait_recv()
    total = sums[0]
    for other in range(1, n_row):
        total += sums[other]
    scale = jnp.sum(total, axis=0, keepdims=True) / (rows * n_row) + 1e-6
    inverse_ref[...] = jnp.broadcast_to(1.0 / scale, inverse_ref.shape)

    def left_behind(sem, ref):
        pltpu.make_async_remote_copy(
            src_ref=ref, dst_ref=ref, send_sem=sem, recv_sem=recv_sum.at[0],
            device_id=(r, c, f), device_id_type=MESH,
        ).wait_send()

    few = helps * step
    for at in range(n_fib):
        @pl.when(f == at)
        def _():
            if at < n_fib - 1:
                less = few if at == n_fib - 2 else 0
                left_behind(sent_left.at[1], left.at[pl.ds(0, at + 1), pl.ds(0, rows - less)])
            if at > 0:
                less = few if at == 1 else 0
                left_behind(sent_left.at[0], left.at[pl.ds(0, n_fib - at), pl.ds(0, rows - less)])

    for less in range(2):
        if n_col > less:
            @pl.when(mine == bool(less))
            def _():
                left_behind(sent_right.at[0], part_out.at[pl.ds(0, n_col - less)])

    if group > 1:
        left_behind(sent_pair.at[0], right.at[pl.ds(0, (group - 1) * rows)])
    if n_col > 1:
        left_behind(sent_part.at[0], part_out.at[pl.ds(0, n_col - 1)])
    if n_row > 1:
        left_behind(sent_sum.at[0], sums.at[pl.ds(0, n_row - 1)])

    if helps:
        for less in range(2):
            size = (parts - less) * unit
            across = pl.ds(0, (n_col - 1) * unit)
            if size and n_col > 1:
                @pl.when(skips(seat, jnp.where(outer, f, mate)) == bool(less))
                def _():
                    @pl.when(outer | (helper & mine))
                    def _():
                        left_behind(sent_far.at[0], right.at[pl.ds(0, size), across])

            if size and group > 1:
                @pl.when(helper & (skips(seat, mate) == bool(less)))
                def _():
                    left_behind(sent_far_pair.at[0], right.at[pl.ds(0, (group - 1) * size)])

        @pl.when(helper)
        def _():
            if n_col > 1:
                left_behind(sent_help.at[0], help_out.at[pl.ds(0, n_col - 1)])
            left_behind(sent_done.at[0], helped)


def prune(keep_ref, squared_ref, inverse_ref, out_hbm, out_vmem, sem):
    tile = out_vmem.shape[1] // keep_ref.shape[0]
    copies = []
    for i in range(keep_ref.shape[1]):
        down = slice(i * tile, (i + 1) * tile)
        for j in range(keep_ref.shape[0]):
            across = slice(j * tile, (j + 1) * tile)
            factor = inverse_ref[0:1, across] * keep_ref[j, i].astype(jnp.float32)
            out_vmem[down, across] = squared_ref[down, across] * factor
        copy = pltpu.make_async_copy(out_vmem.at[down], out_hbm.at[down], sem.at[i])
        copy.start()
        copies.append(copy)
    for copy in copies:
        copy.wait()


def solution(mesh):
    n_row, n_col, n_fib = (mesh.shape[name] for name in ("row", "col", "fiber"))
    group = n_row // n_col
    helps = HELP if n_fib > 3 else 0

    def local(values, tile_mask, keep_mask):
        rows, unit = values.shape
        dma = pltpu.SemaphoreType.DMA
        parts = rows // unit
        few = rows // CHUNKS * HELP
        squared, inverse = pl.pallas_call(
            functools.partial(kernel, n_row, n_col, n_fib, helps),
            out_shape=(
                pltpu.VMEM((rows, unit), jnp.float32),
                pltpu.VMEM((8, unit), jnp.float32),
            ),
            in_specs=[
                pl.BlockSpec(memory_space=pltpu.HBM),
                pl.BlockSpec(memory_space=pltpu.HBM),
            ],
            out_specs=(
                pl.BlockSpec(memory_space=pltpu.VMEM),
                pl.BlockSpec(memory_space=pltpu.VMEM),
            ),
            scratch_shapes=[
                pltpu.SMEM(tile_mask.shape[::-1], jnp.int32),
                pltpu.VMEM((rows, unit), jnp.float32),
                pltpu.VMEM((n_fib, rows, unit), jnp.bfloat16),
                pltpu.VMEM((group * rows, n_col * unit), jnp.bfloat16),
                pltpu.VMEM((n_col, rows, unit), jnp.bfloat16),
                pltpu.VMEM((n_col, rows, unit), jnp.bfloat16),
                pltpu.VMEM((n_row, 8, unit), jnp.float32),
                pltpu.VMEM((group * rows, n_col * unit), jnp.bfloat16),
                pltpu.VMEM((few, unit), jnp.float32),
                pltpu.VMEM((n_col, few, unit), jnp.bfloat16),
                pltpu.VMEM((n_col, few, unit), jnp.bfloat16),
                pltpu.VMEM((few, unit), jnp.bfloat16),
                dma((2,)),
                dma((2,)),
                dma((1,)),
                dma((1,)),
                dma((1,)),
                dma((1,)),
                dma((1,)),
                dma((1,)),
                dma((1,)),
                dma((1,)),
                dma((n_fib - 1, CHUNKS)),
                dma((n_col, parts)),
                dma((group,)),
                dma((n_col - 1, CHUNKS)),
                dma((1,)),
                dma((n_col, parts)),
                dma((group,)),
                dma((n_col - 1, HELP)),
                dma((HELP,)),
            ],
            compiler_params=pltpu.CompilerParams(
                collective_id=0, has_side_effects=True, vmem_limit_bytes=VMEM_LIMIT
            ),
            name="expand",
        )(tile_mask.T, values)
        return pl.pallas_call(
            prune,
            out_shape=jax.ShapeDtypeStruct((rows, unit), jnp.float32),
            in_specs=[
                pl.BlockSpec(memory_space=pltpu.SMEM),
                pl.BlockSpec(memory_space=pltpu.VMEM),
                pl.BlockSpec(memory_space=pltpu.VMEM),
            ],
            out_specs=pl.BlockSpec(memory_space=pl.ANY),
            scratch_shapes=[
                pltpu.VMEM((rows, unit), jnp.float32),
                dma((keep_mask.shape[0],)),
            ],
            compiler_params=pltpu.CompilerParams(vmem_limit_bytes=8 * 1024 * 1024),
            name="prune",
        )(keep_mask.T, squared, inverse)

    spec = P("row", ("col", "fiber"))
    return jax.shard_map(
        local, mesh=mesh, in_specs=(spec, spec, spec), out_specs=spec, check_vma=False
    )
```

```python
import functools

import jax
import jax.numpy as jnp
from jax import lax
from jax.experimental import pallas as pl
from jax.experimental.pallas import tpu as pltpu
from jax.sharding import PartitionSpec as P

MESH = pl.DeviceIdType.MESH
CHUNKS = 12
HELP = 3
TRAIL = 1
AHEAD = 5
FETCH = 7
ANSWER = 8
LAG = 4
VMEM_LIMIT = 62 * 1024 * 1024


def kernel(
    n_row, n_col, n_fib, helps, tile_hbm, values_hbm, own, inverse_ref,
    tile_ref, values_ref, left, right, part_out, part_in, sums,
    right_far, help_own, help_out, help_in, helped, load_sem,
    sent_left, sent_right, sent_pair, sent_part, sent_sum, sent_far, sent_far_pair, sent_help, sent_done,
    recv_left, recv_right, recv_pair, recv_part, recv_sum,
    recv_far, recv_far_pair, recv_help, recv_done,
):
    r, c, f = lax.axis_index("row"), lax.axis_index("col"), lax.axis_index("fiber")
    rows, unit = values_ref.shape
    tile = unit // tile_ref.shape[0]
    step = rows // CHUNKS
    parts = rows // unit
    group = n_row // n_col
    owner, seat = r // group, lax.rem(r, group)

    load = pltpu.make_async_copy(values_hbm, values_ref, load_sem.at[0])
    load.start()
    load_tile = pltpu.make_async_copy(tile_hbm, tile_ref, load_sem.at[1])
    load_tile.start()

    barrier = pltpu.get_barrier_semaphore()
    for dr in range(n_row):
        for dc in range(n_col):
            if dr or dc:
                pl.semaphore_signal(
                    barrier, inc=1, device_id_type=MESH,
                    device_id=(lax.rem(r + dr, n_row), lax.rem(c + dc, n_col), f),
                )

    has_down, has_up = f > 0, f < n_fib - 1
    outer = jnp.logical_not(has_down & has_up)
    helper = (f == 1) | (f == n_fib - 2)
    mate = jnp.where(outer, jnp.where(has_down, f - 1, 1), jnp.where(f == 1, 0, n_fib - 1))
    mine = owner == c

    @pl.when(has_down)
    def _():
        pl.semaphore_signal(barrier, inc=1, device_id=(r, c, f - 1), device_id_type=MESH)

    @pl.when(has_up)
    def _():
        pl.semaphore_signal(barrier, inc=1, device_id=(r, c, f + 1), device_id_type=MESH)

    load_tile.wait()
    load.wait()

    for i in range(rows // tile):
        for j in range(unit // tile):
            at = (pl.ds(i * tile, tile), pl.ds(j * tile, tile))
            masked = values_ref[at] * tile_ref[j, i].astype(jnp.float32)
            left[f, i * tile:(i + 1) * tile, j * tile:(j + 1) * tile] = masked.astype(jnp.bfloat16)

    neighbours = has_down.astype(jnp.int32) + has_up.astype(jnp.int32)
    pl.semaphore_wait(barrier, n_row * n_col - 1 + neighbours)

    def chunk(i):
        return pl.ds(i * step if isinstance(i, int) else pl.multiple_of(i * step, step), step)

    def along(source, i, up):
        part = left.at[source, chunk(i)]
        return pltpu.make_async_remote_copy(
            src_ref=part, dst_ref=part,
            send_sem=sent_left.at[int(up)], recv_sem=recv_left.at[source if up else source - 1, i],
            device_id=(r, c, f + 1 if up else f - 1), device_id_type=MESH,
        )

    lead, trail = helps - min(helps, TRAIL), CHUNKS - min(helps, TRAIL)

    def kept(i):
        return (i >= lead) & (i < trail)

    def lent_at(h):
        return h if h < lead else h - helps + CHUNKS

    def sends_up(i):
        return has_up & (kept(i) | (f + 1 < n_fib - 1))

    def sends_down(i):
        return has_down & (kept(i) | (f - 1 > 0))

    def gets_up(i):
        return kept(i) | has_up

    def gets_down(i):
        return kept(i) | has_down

    def right_at(ref, col, place, b):
        return ref.at[
            pl.ds(pl.multiple_of(place * rows + b * unit, unit), unit),
            pl.ds(pl.multiple_of(col * unit, unit), unit),
        ]

    def block(source, b):
        return left.at[source, pl.ds(b * unit, unit)]

    def to_right(t, b):
        return pltpu.make_async_remote_copy(
            src_ref=block(f, b), dst_ref=right_at(right, c, seat, b),
            send_sem=sent_right.at[0], recv_sem=recv_right.at[c, b],
            device_id=(t * group + seat, owner, f), device_id_type=MESH,
        )

    def came_right(col, b):
        return pltpu.make_async_remote_copy(
            src_ref=block(f, b), dst_ref=right_at(right, col, seat, b),
            send_sem=sent_right.at[0], recv_sem=recv_right.at[col, b],
            device_id=(r, c, f), device_id_type=MESH,
        )

    def to_far(col, b):
        return pltpu.make_async_remote_copy(
            src_ref=right_at(right, col, seat, b), dst_ref=right_at(right_far, col, seat, b),
            send_sem=sent_far.at[0], recv_sem=recv_far.at[col, b],
            device_id=(r, c, mate), device_id_type=MESH,
        )

    def to_side(t, b):
        return pltpu.make_async_remote_copy(
            src_ref=block(mate, b), dst_ref=right_at(right_far, c, seat, b),
            send_sem=sent_far.at[0], recv_sem=recv_far.at[c, b],
            device_id=(t * group + seat, c, f), device_id_type=MESH,
        )

    def came_far(col, b):
        return pltpu.make_async_remote_copy(
            src_ref=block(f, b), dst_ref=right_at(right_far, col, seat, b),
            send_sem=sent_far.at[0], recv_sem=recv_far.at[col, b],
            device_id=(r, c, f), device_id_type=MESH,
        )

    def pairing(ref, send, recv):
        def to_pair(col, b, other):
            return pltpu.make_async_remote_copy(
                src_ref=right_at(ref, col, seat, b), dst_ref=right_at(ref, col, seat, b),
                send_sem=send.at[0], recv_sem=recv.at[seat],
                device_id=(owner * group + other, c, f), device_id_type=MESH,
            )

        def came_pair(other, blocks):
            theirs = ref.at[pl.ds(other * rows, blocks * unit)]
            return pltpu.make_async_remote_copy(
                src_ref=theirs, dst_ref=theirs, send_sem=send.at[0], recv_sem=recv.at[other],
                device_id=(r, c, f), device_id_type=MESH,
            )

        return to_pair, came_pair

    to_pair, came_pair = pairing(right, sent_pair, recv_pair)
    to_far_pair, came_far_pair = pairing(right_far, sent_far_pair, recv_far_pair)

    def crossing(out, into, send, recv):
        def to_col(col, i):
            return pltpu.make_async_remote_copy(
                src_ref=out.at[col, chunk(i)], dst_ref=into.at[c, chunk(i)],
                send_sem=send.at[0], recv_sem=recv.at[lax.rem(c - col + n_col, n_col) - 1, i],
                device_id=(r, col, f), device_id_type=MESH,
            )

        def came_col(col, i):
            return pltpu.make_async_remote_copy(
                src_ref=out.at[col, chunk(i)], dst_ref=into.at[col, chunk(i)],
                send_sem=send.at[0], recv_sem=recv.at[lax.rem(col - c + n_col, n_col) - 1, i],
                device_id=(r, col, f), device_id_type=MESH,
            )

        return to_col, came_col

    to_col, came_col = crossing(part_out, part_in, sent_part, recv_part)
    to_help, came_help = crossing(help_out, help_in, sent_help, recv_help)

    def to_done(i):
        return pltpu.make_async_remote_copy(
            src_ref=helped.at[chunk(i)], dst_ref=helped.at[chunk(i)],
            send_sem=sent_done.at[0], recv_sem=recv_done.at[i],
            device_id=(r, c, mate), device_id_type=MESH,
        )

    def skips(place, far):
        return (far >= place * parts) & (far < (place + 1) * parts)

    def served(place, b):
        return place * parts + b != mate

    def to_serve(b):
        return seat * parts + b != f

    def send_own(i, now_down, now_up):
        @pl.when(sends_down(i) & now_down)
        def _():
            along(f, i, False).start()

        @pl.when(sends_up(i) & now_up)
        def _():
            along(f, i, True).start()

    last = max(n_fib - 3, 0) * AHEAD
    before = last + 2
    direct_down = outer | (f == 1)
    direct_up = outer | (f == n_fib - 2)

    @pl.loop(0, CHUNKS)
    def _(i):
        send_own(i, direct_down | (i < AHEAD), direct_up | (i < AHEAD))

    for b in range(parts):
        for t in range(n_row // group):
            @pl.when(jnp.logical_not(mine & (owner == t)))
            def _():
                to_right(t, b).start()

    @pl.when(mine)
    def _():
        for b in range(parts):
            spot = right_at(right, c, seat, b)
            spot[...] = left[f, b * unit:(b + 1) * unit]

    def pass_up(d, i):
        @pl.when((f - d >= 0) & gets_up(i))
        def _():
            along(f - d, i, True).wait_recv()

            @pl.when(sends_up(i))
            def _():
                along(f - d, i, True).start()

    def pass_down(d, i):
        @pl.when((f + d < n_fib) & gets_down(i))
        def _():
            along(f + d, i, False).wait_recv()

            @pl.when(sends_down(i))
            def _():
                along(f + d, i, False).start()

    def relay(s):
        @pl.when(jnp.asarray(s) < CHUNKS - AHEAD)
        def _():
            send_own(s + AHEAD, jnp.logical_not(direct_down), jnp.logical_not(direct_up))

        s = jnp.asarray(s)

        @pl.when((s < CHUNKS) & ((s < before) | (f != 1)))
        def _():
            pass_up(1, s)

        @pl.when((s < CHUNKS) & ((s < before) | (f != n_fib - 2)))
        def _():
            pass_down(1, s)

        for d in range(2, n_fib - 1):
            i = s - (d - 1) * AHEAD

            @pl.when((i >= 0) & (i < CHUNKS))
            def _():
                pass_up(d, i)
                pass_down(d, i)

    def side(b):
        @pl.when(helper & mine & served(seat, b))
        def _():
            for t in range(n_row // group):
                @pl.when(owner != t)
                def _():
                    to_side(t, b).start()

            spot = right_at(right_far, c, seat, b)
            spot[...] = left[mate, b * unit:(b + 1) * unit]

    def gather(b):
        for col in range(n_col):
            @pl.when(jnp.logical_not(mine & (c == col)))
            def _():
                came_right(col, b).wait_recv()

            if helps:
                @pl.when(outer & (c != col) & to_serve(b))
                def _():
                    to_far(col, b).start()

            for other in range(group):
                @pl.when(seat != other)
                def _():
                    to_pair(col, b, other).start()

    early = [b for b in range(parts) if (b + 1) * unit <= before * step]

    @pl.when(jnp.logical_not(outer))
    def _():
        @pl.loop(0, before - 1)
        def _(s):
            relay(s)

    for b in range(parts - 1):
        gather(b)

    @pl.when(jnp.logical_not(outer))
    def _():
        relay(before - 1)

        if helps:
            for b in early:
                side(b)

        @pl.loop(before, CHUNKS)
        def _(i):
            @pl.when(f == 1)
            def _():
                pass_up(1, i)

            @pl.when(f == n_fib - 2)
            def _():
                pass_down(1, i)

        if helps:
            for b in range(len(early), parts):
                side(b)

    gather(parts - 1)

    for other in range(group):
        @pl.when(seat != other)
        def _():
            came_pair(other, parts).wait_recv()

    def product(ref, part, col, k):
        return jnp.dot(
            left[k, part, :],
            ref[
                pl.ds(pl.multiple_of(k * unit, unit), unit),
                pl.ds(pl.multiple_of(col * unit, unit), unit),
            ],
            preferred_element_type=jnp.float32,
        )

    def all_products(part, col):
        total = product(right, part, col, 0)
        for k in range(1, n_fib):
            total += product(right, part, col, k)
        return total

    def col_at(shift):
        return lax.rem(c + shift, n_col)

    sums[r] = jnp.zeros((8, unit), jnp.float32)

    def combine(i, h=None):
        part = chunk(i)
        expanded = own[part, :]
        for shift in range(1, n_col):
            came_col(col_at(shift), i).wait_recv()
            expanded += part_in[col_at(shift), part, :].astype(jnp.float32)
        if h is not None:
            to_done(h).wait_recv()
            expanded += helped[pl.ds(h * step, step), :].astype(jnp.float32)
        squared = expanded * expanded
        own[part, :] = squared
        sums[r] += jnp.sum(squared.reshape(step // 8, 8, unit), axis=0)

    def fetch():
        for b in range(parts):
            @pl.when(served(seat, b))
            def _():
                for col in range(n_col):
                    @pl.when(jnp.logical_not(mine & (c == col)))
                    def _():
                        came_far(col, b).wait_recv()

                    for other in range(group):
                        @pl.when(seat != other)
                        def _():
                            to_far_pair(col, b, other).start()

    def answer():
        for other in range(group):
            for skipped in range(2):
                @pl.when((seat != other) & (skips(other, mate) == bool(skipped)))
                def _():
                    came_far_pair(other, parts - skipped).wait_recv()

        reckon(0, lead)

    def reckon(h, count):
        if count == 0:
            return
        part = pl.ds(lent_at(h) * step, count * step)
        there = pl.ds(h * step, count * step)
        for shift in list(range(1, n_col)) + [0]:
            col = col_at(shift)
            total = product(right_far, part, col, lax.rem(mate + 1, n_fib))
            for k in range(2, n_fib):
                total += product(right_far, part, col, lax.rem(mate + k, n_fib))
            if shift:
                help_out[col, there, :] = total.astype(jnp.bfloat16)
                for i in range(h, h + count):
                    to_help(col, i).start()
            else:
                help_own[there, :] = total

    if helps:
        @pl.when(outer)
        def _():
            for h in range(helps):
                i = lent_at(h)
                part = pl.ds(i * step, step)
                for shift in range(1, n_col):
                    col = col_at(shift)
                    part_out[col, part, :] = product(right, part, col, f).astype(jnp.bfloat16)
                    to_col(col, i).start()
                own[part, :] = product(right, part, c, f)

    @pl.loop(0, CHUNKS)
    def _(i):
        part = chunk(i)
        full = kept(i) | jnp.logical_not(outer)

        @pl.when(outer & full)
        def _():
            for d in range(1, n_fib):
                pass_up(d, i)
                pass_down(d, i)

        if helps:
            @pl.when(helper & (i == FETCH))
            def _():
                fetch()

            @pl.when(helper & (i == ANSWER))
            def _():
                answer()

            for h in range(lead, helps):
                @pl.when(helper & (i == lent_at(h)))
                def _():
                    reckon(h, 1)

        @pl.when(full)
        def _():
            for shift in range(1, n_col):
                col = col_at(shift)
                part_out[col, part, :] = all_products(part, col).astype(jnp.bfloat16)
                to_col(col, i).start()

            own[part, :] = all_products(part, c)

        @pl.when(jnp.logical_not(outer) & (i + before < CHUNKS + last))
        def _():
            relay(i + before)

        @pl.when((i >= LAG) & (kept(i - LAG) | jnp.logical_not(outer)))
        def _():
            combine(i - LAG)

    def reply(h):
        @pl.when(helper)
        def _():
            part = pl.ds(h * step, step)
            total = help_own[part, :]
            for shift in range(1, n_col):
                came_help(col_at(shift), h).wait_recv()
                total += help_in[col_at(shift), part, :].astype(jnp.float32)
            helped[part, :] = total.astype(jnp.bfloat16)
            to_done(h).start()

    for h in range(lead):
        reply(h)

    for i in range(CHUNKS - LAG, CHUNKS):
        for h in range(lead, helps):
            if lent_at(h) == i:
                reply(h)

        @pl.when(kept(jnp.asarray(i)) | jnp.logical_not(outer))
        def _():
            combine(i)

    if helps:
        @pl.when(outer)
        def _():
            for h in range(helps):
                combine(lent_at(h), h)

    def to_row(shift):
        return pltpu.make_async_remote_copy(
            src_ref=sums.at[r], dst_ref=sums.at[r],
            send_sem=sent_sum.at[0], recv_sem=recv_sum.at[0],
            device_id=(lax.rem(r + shift, n_row), c, f), device_id_type=MESH,
        )

    def came_rows():
        return pltpu.make_async_remote_copy(
            src_ref=sums.at[pl.ds(0, n_row - 1)], dst_ref=sums.at[pl.ds(0, n_row - 1)],
            send_sem=sent_sum.at[0], recv_sem=recv_sum.at[0],
            device_id=(r, c, f), device_id_type=MESH,
        )

    for shift in range(1, n_row):
        to_row(shift).start()
    came_rows().wait_recv()
    total = sums[0]
    for other in range(1, n_row):
        total += sums[other]
    scale = jnp.sum(total, axis=0, keepdims=True) / (rows * n_row) + 1e-6
    inverse_ref[...] = jnp.broadcast_to(1.0 / scale, inverse_ref.shape)

    def left_behind(sem, ref):
        pltpu.make_async_remote_copy(
            src_ref=ref, dst_ref=ref, send_sem=sem, recv_sem=recv_sum.at[0],
            device_id=(r, c, f), device_id_type=MESH,
        ).wait_send()

    few = helps * step
    for at in range(n_fib):
        @pl.when(f == at)
        def _():
            if at < n_fib - 1:
                less = few if at == n_fib - 2 else 0
                left_behind(sent_left.at[1], left.at[pl.ds(0, at + 1), pl.ds(0, rows - less)])
            if at > 0:
                less = few if at == 1 else 0
                left_behind(sent_left.at[0], left.at[pl.ds(0, n_fib - at), pl.ds(0, rows - less)])

    for less in range(2):
        if n_col > less:
            @pl.when(mine == bool(less))
            def _():
                left_behind(sent_right.at[0], part_out.at[pl.ds(0, n_col - less)])

    if group > 1:
        left_behind(sent_pair.at[0], right.at[pl.ds(0, (group - 1) * rows)])
    if n_col > 1:
        left_behind(sent_part.at[0], part_out.at[pl.ds(0, n_col - 1)])
    if n_row > 1:
        left_behind(sent_sum.at[0], sums.at[pl.ds(0, n_row - 1)])

    if helps:
        for less in range(2):
            size = (parts - less) * unit
            across = pl.ds(0, (n_col - 1) * unit)
            if size and n_col > 1:
                @pl.when(skips(seat, jnp.where(outer, f, mate)) == bool(less))
                def _():
                    @pl.when(outer | (helper & mine))
                    def _():
                        left_behind(sent_far.at[0], right.at[pl.ds(0, size), across])

            if size and group > 1:
                @pl.when(helper & (skips(seat, mate) == bool(less)))
                def _():
                    left_behind(sent_far_pair.at[0], right.at[pl.ds(0, (group - 1) * size)])

        @pl.when(helper)
        def _():
            if n_col > 1:
                left_behind(sent_help.at[0], help_out.at[pl.ds(0, n_col - 1)])
            left_behind(sent_done.at[0], helped)


def prune(keep_ref, squared_ref, inverse_ref, out_hbm, out_vmem, sem):
    tile = out_vmem.shape[1] // keep_ref.shape[0]
    copies = []
    for i in range(keep_ref.shape[1]):
        down = slice(i * tile, (i + 1) * tile)
        for j in range(keep_ref.shape[0]):
            across = slice(j * tile, (j + 1) * tile)
            factor = inverse_ref[0:1, across] * keep_ref[j, i].astype(jnp.float32)
            out_vmem[down, across] = squared_ref[down, across] * factor
        copy = pltpu.make_async_copy(out_vmem.at[down], out_hbm.at[down], sem.at[i])
        copy.start()
        copies.append(copy)
    for copy in copies:
        copy.wait()


def solution(mesh):
    n_row, n_col, n_fib = (mesh.shape[name] for name in ("row", "col", "fiber"))
    group = n_row // n_col
    helps = HELP if n_fib > 3 else 0

    def local(values, tile_mask, keep_mask):
        rows, unit = values.shape
        dma = pltpu.SemaphoreType.DMA
        parts = rows // unit
        few = rows // CHUNKS * HELP
        squared, inverse = pl.pallas_call(
            functools.partial(kernel, n_row, n_col, n_fib, helps),
            out_shape=(
                pltpu.VMEM((rows, unit), jnp.float32),
                pltpu.VMEM((8, unit), jnp.float32),
            ),
            in_specs=[
                pl.BlockSpec(memory_space=pltpu.HBM),
                pl.BlockSpec(memory_space=pltpu.HBM),
            ],
            out_specs=(
                pl.BlockSpec(memory_space=pltpu.VMEM),
                pl.BlockSpec(memory_space=pltpu.VMEM),
            ),
            scratch_shapes=[
                pltpu.SMEM(tile_mask.shape[::-1], jnp.int32),
                pltpu.VMEM((rows, unit), jnp.float32),
                pltpu.VMEM((n_fib, rows, unit), jnp.bfloat16),
                pltpu.VMEM((group * rows, n_col * unit), jnp.bfloat16),
                pltpu.VMEM((n_col, rows, unit), jnp.bfloat16),
                pltpu.VMEM((n_col, rows, unit), jnp.bfloat16),
                pltpu.VMEM((n_row, 8, unit), jnp.float32),
                pltpu.VMEM((group * rows, n_col * unit), jnp.bfloat16),
                pltpu.VMEM((few, unit), jnp.float32),
                pltpu.VMEM((n_col, few, unit), jnp.bfloat16),
                pltpu.VMEM((n_col, few, unit), jnp.bfloat16),
                pltpu.VMEM((few, unit), jnp.bfloat16),
                dma((2,)),
                dma((2,)),
                dma((1,)),
                dma((1,)),
                dma((1,)),
                dma((1,)),
                dma((1,)),
                dma((1,)),
                dma((1,)),
                dma((1,)),
                dma((n_fib - 1, CHUNKS)),
                dma((n_col, parts)),
                dma((group,)),
                dma((n_col - 1, CHUNKS)),
                dma((1,)),
                dma((n_col, parts)),
                dma((group,)),
                dma((n_col - 1, HELP)),
                dma((HELP,)),
            ],
            compiler_params=pltpu.CompilerParams(
                collective_id=0, has_side_effects=True, vmem_limit_bytes=VMEM_LIMIT
            ),
            name="expand",
        )(tile_mask.T, values)
        return pl.pallas_call(
            prune,
            out_shape=jax.ShapeDtypeStruct((rows, unit), jnp.float32),
            in_specs=[
                pl.BlockSpec(memory_space=pltpu.SMEM),
                pl.BlockSpec(memory_space=pltpu.VMEM),
                pl.BlockSpec(memory_space=pltpu.VMEM),
            ],
            out_specs=pl.BlockSpec(memory_space=pl.ANY),
            scratch_shapes=[
                pltpu.VMEM((rows, unit), jnp.float32),
                dma((keep_mask.shape[0],)),
            ],
            compiler_params=pltpu.CompilerParams(vmem_limit_bytes=8 * 1024 * 1024),
            name="prune",
        )(keep_mask.T, squared, inverse)

    spec = P("row", ("col", "fiber"))
    return jax.shard_map(
        local, mesh=mesh, in_specs=(spec, spec, spec), out_specs=spec, check_vma=False
    )
```

```python
import functools

import jax
import jax.numpy as jnp
from jax import lax
from jax.experimental import pallas as pl
from jax.experimental.pallas import tpu as pltpu
from jax.sharding import PartitionSpec as P

MESH = pl.DeviceIdType.MESH
CHUNKS = 12
HELP = 3
AHEAD = 3
FETCH = 8
ANSWER = 9
LAG = 4
VMEM_LIMIT = 62 * 1024 * 1024


def kernel(
    n_row, n_col, n_fib, helps, tile_hbm, values_hbm, own, inverse_ref,
    tile_ref, values_ref, left, right, part_out, part_in, sums,
    right_far, help_own, help_out, help_in, helped, load_sem,
    sent_left, sent_right, sent_pair, sent_part, sent_sum, sent_far, sent_far_pair, sent_help, sent_done,
    recv_left, recv_right, recv_pair, recv_part, recv_sum,
    recv_far, recv_far_pair, recv_help, recv_done,
):
    r, c, f = lax.axis_index("row"), lax.axis_index("col"), lax.axis_index("fiber")
    rows, unit = values_ref.shape
    tile = unit // tile_ref.shape[0]
    step = rows // CHUNKS
    parts = rows // unit
    group = n_row // n_col
    owner, seat = r // group, lax.rem(r, group)

    load = pltpu.make_async_copy(values_hbm, values_ref, load_sem.at[0])
    load.start()
    load_tile = pltpu.make_async_copy(tile_hbm, tile_ref, load_sem.at[1])
    load_tile.start()

    barrier = pltpu.get_barrier_semaphore()
    for dr in range(n_row):
        for dc in range(n_col):
            if dr or dc:
                pl.semaphore_signal(
                    barrier, inc=1, device_id_type=MESH,
                    device_id=(lax.rem(r + dr, n_row), lax.rem(c + dc, n_col), f),
                )

    has_down, has_up = f > 0, f < n_fib - 1
    outer = jnp.logical_not(has_down & has_up)
    helper = (f == 1) | (f == n_fib - 2)
    mate = jnp.where(outer, jnp.where(has_down, f - 1, 1), jnp.where(f == 1, 0, n_fib - 1))
    mine = owner == c

    @pl.when(has_down)
    def _():
        pl.semaphore_signal(barrier, inc=1, device_id=(r, c, f - 1), device_id_type=MESH)

    @pl.when(has_up)
    def _():
        pl.semaphore_signal(barrier, inc=1, device_id=(r, c, f + 1), device_id_type=MESH)

    load_tile.wait()
    load.wait()

    for i in range(rows // tile):
        for j in range(unit // tile):
            at = (pl.ds(i * tile, tile), pl.ds(j * tile, tile))
            masked = values_ref[at] * tile_ref[j, i].astype(jnp.float32)
            left[f, i * tile:(i + 1) * tile, j * tile:(j + 1) * tile] = masked.astype(jnp.bfloat16)

    neighbours = has_down.astype(jnp.int32) + has_up.astype(jnp.int32)
    pl.semaphore_wait(barrier, n_row * n_col - 1 + neighbours)

    def chunk(i):
        return pl.ds(i * step if isinstance(i, int) else pl.multiple_of(i * step, step), step)

    def along(source, i, up):
        part = left.at[source, chunk(i)]
        return pltpu.make_async_remote_copy(
            src_ref=part, dst_ref=part,
            send_sem=sent_left.at[int(up)], recv_sem=recv_left.at[source if up else source - 1, i],
            device_id=(r, c, f + 1 if up else f - 1), device_id_type=MESH,
        )

    def kept(i):
        return i >= helps

    def sends_up(i):
        return has_up & (kept(i) | (f + 1 < n_fib - 1))

    def sends_down(i):
        return has_down & (kept(i) | (f - 1 > 0))

    def gets_up(i):
        return kept(i) | has_up

    def gets_down(i):
        return kept(i) | has_down

    def right_at(ref, col, place, b):
        return ref.at[
            pl.ds(pl.multiple_of(place * rows + b * unit, unit), unit),
            pl.ds(pl.multiple_of(col * unit, unit), unit),
        ]

    def block(source, b):
        return left.at[source, pl.ds(b * unit, unit)]

    def to_right(t, b):
        return pltpu.make_async_remote_copy(
            src_ref=block(f, b), dst_ref=right_at(right, c, seat, b),
            send_sem=sent_right.at[0], recv_sem=recv_right.at[c, b],
            device_id=(t * group + seat, owner, f), device_id_type=MESH,
        )

    def came_right(col, b):
        return pltpu.make_async_remote_copy(
            src_ref=block(f, b), dst_ref=right_at(right, col, seat, b),
            send_sem=sent_right.at[0], recv_sem=recv_right.at[col, b],
            device_id=(r, c, f), device_id_type=MESH,
        )

    def to_far(col, b):
        return pltpu.make_async_remote_copy(
            src_ref=right_at(right, col, seat, b), dst_ref=right_at(right_far, col, seat, b),
            send_sem=sent_far.at[0], recv_sem=recv_far.at[col, b],
            device_id=(r, c, mate), device_id_type=MESH,
        )

    def to_side(t, b):
        return pltpu.make_async_remote_copy(
            src_ref=block(mate, b), dst_ref=right_at(right_far, c, seat, b),
            send_sem=sent_far.at[0], recv_sem=recv_far.at[c, b],
            device_id=(t * group + seat, c, f), device_id_type=MESH,
        )

    def came_far(col, b):
        return pltpu.make_async_remote_copy(
            src_ref=block(f, b), dst_ref=right_at(right_far, col, seat, b),
            send_sem=sent_far.at[0], recv_sem=recv_far.at[col, b],
            device_id=(r, c, f), device_id_type=MESH,
        )

    def pairing(ref, send, recv):
        def to_pair(col, b, other):
            return pltpu.make_async_remote_copy(
                src_ref=right_at(ref, col, seat, b), dst_ref=right_at(ref, col, seat, b),
                send_sem=send.at[0], recv_sem=recv.at[seat],
                device_id=(owner * group + other, c, f), device_id_type=MESH,
            )

        def came_pair(other, blocks):
            theirs = ref.at[pl.ds(other * rows, blocks * unit)]
            return pltpu.make_async_remote_copy(
                src_ref=theirs, dst_ref=theirs, send_sem=send.at[0], recv_sem=recv.at[other],
                device_id=(r, c, f), device_id_type=MESH,
            )

        return to_pair, came_pair

    to_pair, came_pair = pairing(right, sent_pair, recv_pair)
    to_far_pair, came_far_pair = pairing(right_far, sent_far_pair, recv_far_pair)

    def crossing(out, into, send, recv):
        def to_col(col, i):
            return pltpu.make_async_remote_copy(
                src_ref=out.at[col, chunk(i)], dst_ref=into.at[c, chunk(i)],
                send_sem=send.at[0], recv_sem=recv.at[lax.rem(c - col + n_col, n_col) - 1, i],
                device_id=(r, col, f), device_id_type=MESH,
            )

        def came_col(col, i):
            return pltpu.make_async_remote_copy(
                src_ref=out.at[col, chunk(i)], dst_ref=into.at[col, chunk(i)],
                send_sem=send.at[0], recv_sem=recv.at[lax.rem(col - c + n_col, n_col) - 1, i],
                device_id=(r, col, f), device_id_type=MESH,
            )

        return to_col, came_col

    to_col, came_col = crossing(part_out, part_in, sent_part, recv_part)
    to_help, came_help = crossing(help_out, help_in, sent_help, recv_help)

    def to_done(i):
        return pltpu.make_async_remote_copy(
            src_ref=helped.at[chunk(i)], dst_ref=helped.at[chunk(i)],
            send_sem=sent_done.at[0], recv_sem=recv_done.at[i],
            device_id=(r, c, mate), device_id_type=MESH,
        )

    def skips(place, far):
        return (far >= place * parts) & (far < (place + 1) * parts)

    def served(place, b):
        return place * parts + b != mate

    def to_serve(b):
        return seat * parts + b != f

    def send_own(i, now_down, now_up):
        @pl.when(sends_down(i) & now_down)
        def _():
            along(f, i, False).start()

        @pl.when(sends_up(i) & now_up)
        def _():
            along(f, i, True).start()

    low, high = f == 1, f == n_fib - 2
    inner = jnp.logical_not(outer)
    direct_down = outer | jnp.logical_not(high)
    direct_up = outer | jnp.logical_not(low)

    @pl.loop(0, CHUNKS)
    def _(i):
        send_own(i, direct_down | (i < AHEAD), direct_up | (i < AHEAD))

    for b in range(parts):
        for t in range(n_row // group):
            @pl.when(jnp.logical_not(mine & (owner == t)))
            def _():
                to_right(t, b).start()

    @pl.when(mine)
    def _():
        for b in range(parts):
            spot = right_at(right, c, seat, b)
            spot[...] = left[f, b * unit:(b + 1) * unit]

    def pass_up(d, i):
        @pl.when((f - d >= 0) & gets_up(i))
        def _():
            along(f - d, i, True).wait_recv()

            @pl.when(sends_up(i))
            def _():
                along(f - d, i, True).start()

    def pass_down(d, i):
        @pl.when((f + d < n_fib) & gets_down(i))
        def _():
            along(f + d, i, False).wait_recv()

            @pl.when(sends_down(i))
            def _():
                along(f + d, i, False).start()

    def feed(i):
        @pl.when(low)
        def _():
            pass_up(1, i)

        @pl.when(high)
        def _():
            pass_down(1, i)

        @pl.when(i + AHEAD < CHUNKS)
        def _():
            send_own(i + AHEAD, high, low)

    def near(i):
        @pl.when(jnp.logical_not(low))
        def _():
            pass_up(1, i)

        @pl.when(jnp.logical_not(high))
        def _():
            pass_down(1, i)

    def far(i):
        for d in range(2, n_fib - 1):
            pass_up(d, i)
            pass_down(d, i)

    def side(b):
        @pl.when(helper & mine & served(seat, b))
        def _():
            for t in range(n_row // group):
                @pl.when(owner != t)
                def _():
                    to_side(t, b).start()

            spot = right_at(right_far, c, seat, b)
            spot[...] = left[mate, b * unit:(b + 1) * unit]

    def gather(b):
        for col in range(n_col):
            @pl.when(jnp.logical_not(mine & (c == col)))
            def _():
                came_right(col, b).wait_recv()

            if helps:
                @pl.when(outer & (c != col) & to_serve(b))
                def _():
                    to_far(col, b).start()

            for other in range(group):
                @pl.when(seat != other)
                def _():
                    to_pair(col, b, other).start()

    half = CHUNKS // 2

    def approach(first, last):
        @pl.when(inner)
        def _():
            @pl.loop(first, last)
            def _(p):
                feed(2 * p)
                near(p)
                feed(2 * p + 1)

                @pl.when(p > 1)
                def _():
                    far(p - 2)

    for b in range(parts):
        approach(half * b // parts, half * (b + 1) // parts)
        if helps:
            side(b)
        if b < parts - 1:
            gather(b)

    @pl.when(inner)
    def _():
        near(half)

    gather(parts - 1)

    for other in range(group):
        @pl.when(seat != other)
        def _():
            came_pair(other, parts).wait_recv()

    def products(ref, part, first, count):
        return jnp.dot(
            jnp.concatenate([left[first + k, part, :] for k in range(count)], axis=1),
            ref[pl.ds(first * unit if isinstance(first, int) else pl.multiple_of(first * unit, unit), count * unit), :],
            preferred_element_type=jnp.float32,
        )

    def store(total, ours, part, out):
        kept_total = total[:, :unit]
        for col in range(n_col):
            piece = total[:, col * unit:(col + 1) * unit]
            out[col, part, :] = piece.astype(jnp.bfloat16)
            if col:
                kept_total = jnp.where(c == col, piece, kept_total)
        ours[part, :] = kept_total

    def col_at(shift):
        return lax.rem(c + shift, n_col)

    sums[r] = jnp.zeros((8, unit), jnp.float32)

    def combine(i, h=None):
        part = chunk(i)
        expanded = own[part, :]
        for shift in range(1, n_col):
            came_col(col_at(shift), i).wait_recv()
            expanded += part_in[col_at(shift), part, :].astype(jnp.float32)
        if h is not None:
            to_done(h).wait_recv()
            expanded += helped[pl.ds(h * step, step), :].astype(jnp.float32)
        squared = expanded * expanded
        own[part, :] = squared
        sums[r] += jnp.sum(squared.reshape(step // 8, 8, unit), axis=0)

    def fetch():
        for b in range(parts):
            @pl.when(served(seat, b))
            def _():
                for col in range(n_col):
                    @pl.when(jnp.logical_not(mine & (c == col)))
                    def _():
                        came_far(col, b).wait_recv()

                    for other in range(group):
                        @pl.when(seat != other)
                        def _():
                            to_far_pair(col, b, other).start()

    def answer():
        for other in range(group):
            for skipped in range(2):
                @pl.when((seat != other) & (skips(other, mate) == bool(skipped)))
                def _():
                    came_far_pair(other, parts - skipped).wait_recv()

        part = pl.ds(0, helps * step)
        total = products(right_far, part, jnp.where(mate == 0, 1, 0), n_fib - 1)
        store(total, help_own, part, help_out)
        for i in range(helps):
            for shift in range(1, n_col):
                to_help(col_at(shift), i).start()

    if helps:
        @pl.when(outer)
        def _():
            for h in range(helps):
                i = h
                part = pl.ds(i * step, step)
                store(products(right, part, f, 1), own, part, part_out)
                for shift in range(1, n_col):
                    to_col(col_at(shift), i).start()

    def advance(i):
        odd = lax.rem(i, 2) == 1

        @pl.when((i < CHUNKS - 5) & jnp.logical_not(odd))
        def _():
            far(half - 2 + i // 2)

        @pl.when((i < CHUNKS - 5) & odd)
        def _():
            near(half + 1 + i // 2)

        @pl.when((i == CHUNKS - 5) | (i == CHUNKS - 4))
        def _():
            near(i + 3)

        @pl.when((i >= CHUNKS - 5) & (i < CHUNKS - 1))
        def _():
            far(i + 1)

    @pl.loop(0, CHUNKS)
    def _(i):
        part = chunk(i)
        full = kept(i) | jnp.logical_not(outer)

        @pl.when(outer & full)
        def _():
            for d in range(1, n_fib):
                pass_up(d, i)
                pass_down(d, i)

        if helps:
            @pl.when(helper & (i == ANSWER))
            def _():
                answer()

        @pl.when(inner & (i == ANSWER))
        def _():
            advance(i)

        @pl.when(full)
        def _():
            store(products(right, part, 0, n_fib), own, part, part_out)
            for shift in range(1, n_col):
                to_col(col_at(shift), i).start()

        if helps:
            @pl.when(helper & (i == FETCH))
            def _():
                fetch()

        @pl.when(inner & (i != ANSWER))
        def _():
            advance(i)

        @pl.when((i >= LAG) & (kept(i - LAG) | jnp.logical_not(outer)))
        def _():
            combine(i - LAG)

    def reply(h):
        @pl.when(helper)
        def _():
            part = pl.ds(h * step, step)
            total = help_own[part, :]
            for shift in range(1, n_col):
                came_help(col_at(shift), h).wait_recv()
                total += help_in[col_at(shift), part, :].astype(jnp.float32)
            helped[part, :] = total.astype(jnp.bfloat16)
            to_done(h).start()

    for h in range(helps):
        reply(h)

    @pl.loop(CHUNKS - LAG, CHUNKS)
    def _(i):
        combine(i)

    if helps:
        @pl.when(outer)
        def _():
            for h in range(helps):
                combine(h, h)

    def to_row(shift):
        return pltpu.make_async_remote_copy(
            src_ref=sums.at[r], dst_ref=sums.at[r],
            send_sem=sent_sum.at[0], recv_sem=recv_sum.at[0],
            device_id=(lax.rem(r + shift, n_row), c, f), device_id_type=MESH,
        )

    def came_rows():
        return pltpu.make_async_remote_copy(
            src_ref=sums.at[pl.ds(0, n_row - 1)], dst_ref=sums.at[pl.ds(0, n_row - 1)],
            send_sem=sent_sum.at[0], recv_sem=recv_sum.at[0],
            device_id=(r, c, f), device_id_type=MESH,
        )

    for shift in range(1, n_row):
        to_row(shift).start()
    came_rows().wait_recv()
    total = sums[0]
    for other in range(1, n_row):
        total += sums[other]
    scale = jnp.sum(total, axis=0, keepdims=True) / (rows * n_row) + 1e-6
    inverse_ref[...] = jnp.broadcast_to(1.0 / scale, inverse_ref.shape)

    def left_behind(sem, ref):
        pltpu.make_async_remote_copy(
            src_ref=ref, dst_ref=ref, send_sem=sem, recv_sem=recv_sum.at[0],
            device_id=(r, c, f), device_id_type=MESH,
        ).wait_send()

    few = helps * step
    for at in range(n_fib):
        @pl.when(f == at)
        def _():
            if at < n_fib - 1:
                less = few if at == n_fib - 2 else 0
                left_behind(sent_left.at[1], left.at[pl.ds(0, at + 1), pl.ds(0, rows - less)])
            if at > 0:
                less = few if at == 1 else 0
                left_behind(sent_left.at[0], left.at[pl.ds(0, n_fib - at), pl.ds(0, rows - less)])

    for less in range(2):
        if n_col > less:
            @pl.when(mine == bool(less))
            def _():
                left_behind(sent_right.at[0], part_out.at[pl.ds(0, n_col - less)])

    if group > 1:
        left_behind(sent_pair.at[0], right.at[pl.ds(0, (group - 1) * rows)])
    if n_col > 1:
        left_behind(sent_part.at[0], part_out.at[pl.ds(0, n_col - 1)])
    if n_row > 1:
        left_behind(sent_sum.at[0], sums.at[pl.ds(0, n_row - 1)])

    if helps:
        for less in range(2):
            size = (parts - less) * unit
            across = pl.ds(0, (n_col - 1) * unit)
            if size and n_col > 1:
                @pl.when(skips(seat, jnp.where(outer, f, mate)) == bool(less))
                def _():
                    @pl.when(outer | (helper & mine))
                    def _():
                        left_behind(sent_far.at[0], right.at[pl.ds(0, size), across])

            if size and group > 1:
                @pl.when(helper & (skips(seat, mate) == bool(less)))
                def _():
                    left_behind(sent_far_pair.at[0], right.at[pl.ds(0, (group - 1) * size)])

        @pl.when(helper)
        def _():
            if n_col > 1:
                left_behind(sent_help.at[0], help_out.at[pl.ds(0, n_col - 1)])
            left_behind(sent_done.at[0], helped)


def prune(keep_ref, squared_ref, inverse_ref, out_hbm, out_vmem, sem):
    tile = out_vmem.shape[1] // keep_ref.shape[0]
    copies = []
    for i in range(keep_ref.shape[1]):
        down = slice(i * tile, (i + 1) * tile)
        for j in range(keep_ref.shape[0]):
            across = slice(j * tile, (j + 1) * tile)
            factor = inverse_ref[0:1, across] * keep_ref[j, i].astype(jnp.float32)
            out_vmem[down, across] = squared_ref[down, across] * factor
        copy = pltpu.make_async_copy(out_vmem.at[down], out_hbm.at[down], sem.at[i])
        copy.start()
        copies.append(copy)
    for copy in copies:
        copy.wait()


def solution(mesh):
    n_row, n_col, n_fib = (mesh.shape[name] for name in ("row", "col", "fiber"))
    group = n_row // n_col
    helps = HELP if n_fib > 3 else 0

    def local(values, tile_mask, keep_mask):
        rows, unit = values.shape
        dma = pltpu.SemaphoreType.DMA
        parts = rows // unit
        few = rows // CHUNKS * HELP
        squared, inverse = pl.pallas_call(
            functools.partial(kernel, n_row, n_col, n_fib, helps),
            out_shape=(
                pltpu.VMEM((rows, unit), jnp.float32),
                pltpu.VMEM((8, unit), jnp.float32),
            ),
            in_specs=[
                pl.BlockSpec(memory_space=pltpu.HBM),
                pl.BlockSpec(memory_space=pltpu.HBM),
            ],
            out_specs=(
                pl.BlockSpec(memory_space=pltpu.VMEM),
                pl.BlockSpec(memory_space=pltpu.VMEM),
            ),
            scratch_shapes=[
                pltpu.SMEM(tile_mask.shape[::-1], jnp.int32),
                pltpu.VMEM((rows, unit), jnp.float32),
                pltpu.VMEM((n_fib, rows, unit), jnp.bfloat16),
                pltpu.VMEM((group * rows, n_col * unit), jnp.bfloat16),
                pltpu.VMEM((n_col, rows, unit), jnp.bfloat16),
                pltpu.VMEM((n_col, rows, unit), jnp.bfloat16),
                pltpu.VMEM((n_row, 8, unit), jnp.float32),
                pltpu.VMEM((group * rows, n_col * unit), jnp.bfloat16),
                pltpu.VMEM((few, unit), jnp.float32),
                pltpu.VMEM((n_col, few, unit), jnp.bfloat16),
                pltpu.VMEM((n_col, few, unit), jnp.bfloat16),
                pltpu.VMEM((few, unit), jnp.bfloat16),
                dma((2,)),
                dma((2,)),
                dma((1,)),
                dma((1,)),
                dma((1,)),
                dma((1,)),
                dma((1,)),
                dma((1,)),
                dma((1,)),
                dma((1,)),
                dma((n_fib - 1, CHUNKS)),
                dma((n_col, parts)),
                dma((group,)),
                dma((n_col - 1, CHUNKS)),
                dma((1,)),
                dma((n_col, parts)),
                dma((group,)),
                dma((n_col - 1, HELP)),
                dma((HELP,)),
            ],
            compiler_params=pltpu.CompilerParams(
                collective_id=0, has_side_effects=True, vmem_limit_bytes=VMEM_LIMIT
            ),
            name="expand",
        )(tile_mask.T, values)
        return pl.pallas_call(
            prune,
            out_shape=jax.ShapeDtypeStruct((rows, unit), jnp.float32),
            in_specs=[
                pl.BlockSpec(memory_space=pltpu.SMEM),
                pl.BlockSpec(memory_space=pltpu.VMEM),
                pl.BlockSpec(memory_space=pltpu.VMEM),
            ],
            out_specs=pl.BlockSpec(memory_space=pl.ANY),
            scratch_shapes=[
                pltpu.VMEM((rows, unit), jnp.float32),
                dma((keep_mask.shape[0],)),
            ],
            compiler_params=pltpu.CompilerParams(vmem_limit_bytes=8 * 1024 * 1024),
            name="prune",
        )(keep_mask.T, squared, inverse)

    spec = P("row", ("col", "fiber"))
    return jax.shard_map(
        local, mesh=mesh, in_specs=(spec, spec, spec), out_specs=spec, check_vma=False
    )
```

```python
import functools

import jax
import jax.numpy as jnp
from jax import lax
from jax.experimental import pallas as pl
from jax.experimental.pallas import tpu as pltpu
from jax.sharding import PartitionSpec as P

MESH = pl.DeviceIdType.MESH
CHUNKS = 12
HELP = 3
TRAIL = 1
AHEAD = 3
FETCH = 8
ANSWER = 9
LAG = 4
VMEM_LIMIT = 62 * 1024 * 1024


def kernel(
    n_row, n_col, n_fib, helps, tile_hbm, values_hbm, own, inverse_ref,
    tile_ref, values_ref, left, right, part_out, part_in, sums,
    right_far, help_own, help_out, help_in, helped, load_sem,
    sent_left, sent_right, sent_pair, sent_part, sent_sum, sent_far, sent_far_pair, sent_help, sent_done, sent_owner,
    recv_left, recv_right, recv_pair, recv_part, recv_sum,
    recv_far, recv_far_pair, recv_help, recv_done,
):
    r, c, f = lax.axis_index("row"), lax.axis_index("col"), lax.axis_index("fiber")
    rows, unit = values_ref.shape
    tile = unit // tile_ref.shape[0]
    step = rows // CHUNKS
    parts = rows // unit
    group = n_row // n_col
    owner, seat = r // group, lax.rem(r, group)

    load = pltpu.make_async_copy(values_hbm, values_ref, load_sem.at[0])
    load.start()
    load_tile = pltpu.make_async_copy(tile_hbm, tile_ref, load_sem.at[1])
    load_tile.start()

    barrier = pltpu.get_barrier_semaphore()
    for dr in range(n_row):
        for dc in range(n_col):
            if dr or dc:
                pl.semaphore_signal(
                    barrier, inc=1, device_id_type=MESH,
                    device_id=(lax.rem(r + dr, n_row), lax.rem(c + dc, n_col), f),
                )

    has_down, has_up = f > 0, f < n_fib - 1
    outer = jnp.logical_not(has_down & has_up)
    helper = (f == 1) | (f == n_fib - 2)
    mate = jnp.where(outer, jnp.where(has_down, f - 1, 1), jnp.where(f == 1, 0, n_fib - 1))
    mine = owner == c

    @pl.when(has_down)
    def _():
        pl.semaphore_signal(barrier, inc=1, device_id=(r, c, f - 1), device_id_type=MESH)

    @pl.when(has_up)
    def _():
        pl.semaphore_signal(barrier, inc=1, device_id=(r, c, f + 1), device_id_type=MESH)

    load_tile.wait()
    load.wait()

    for i in range(rows // tile):
        for j in range(unit // tile):
            at = (pl.ds(i * tile, tile), pl.ds(j * tile, tile))
            masked = values_ref[at] * tile_ref[j, i].astype(jnp.float32)
            left[f, i * tile:(i + 1) * tile, j * tile:(j + 1) * tile] = masked.astype(jnp.bfloat16)

    neighbours = has_down.astype(jnp.int32) + has_up.astype(jnp.int32)
    pl.semaphore_wait(barrier, n_row * n_col - 1 + neighbours)

    def chunk(i):
        return pl.ds(i * step if isinstance(i, int) else pl.multiple_of(i * step, step), step)

    def along(source, i, up):
        part = left.at[source, chunk(i)]
        return pltpu.make_async_remote_copy(
            src_ref=part, dst_ref=part,
            send_sem=sent_left.at[int(up)], recv_sem=recv_left.at[source if up else source - 1, i],
            device_id=(r, c, f + 1 if up else f - 1), device_id_type=MESH,
        )

    late = min(helps, TRAIL)
    lead = helps - late

    def kept(i):
        return (i >= lead) & (i < CHUNKS - late)

    def lent_at(h):
        return h if h < lead else h - helps + CHUNKS

    def sends_up(i):
        return has_up & (kept(i) | (f + 1 < n_fib - 1))

    def sends_down(i):
        return has_down & (kept(i) | (f - 1 > 0))

    def gets_up(i):
        return kept(i) | has_up

    def gets_down(i):
        return kept(i) | has_down

    def right_at(ref, col, place, b):
        return ref.at[
            pl.ds(pl.multiple_of(place * rows + b * unit, unit), unit),
            pl.ds(pl.multiple_of(col * unit, unit), unit),
        ]

    def block(source, b):
        return left.at[source, pl.ds(b * unit, unit)]

    def to_right(t, b):
        return pltpu.make_async_remote_copy(
            src_ref=block(f, b), dst_ref=right_at(right, c, seat, b),
            send_sem=sent_right.at[0], recv_sem=recv_right.at[c, b],
            device_id=(t * group + seat, owner, f), device_id_type=MESH,
        )

    def came_right(col, b):
        return pltpu.make_async_remote_copy(
            src_ref=block(f, b), dst_ref=right_at(right, col, seat, b),
            send_sem=sent_right.at[0], recv_sem=recv_right.at[col, b],
            device_id=(r, c, f), device_id_type=MESH,
        )

    def to_far(col, b):
        return pltpu.make_async_remote_copy(
            src_ref=right_at(right, col, seat, b), dst_ref=right_at(right_far, col, seat, b),
            send_sem=sent_far.at[0], recv_sem=recv_far.at[col, b],
            device_id=(r, c, mate), device_id_type=MESH,
        )

    def to_side(t, b):
        return pltpu.make_async_remote_copy(
            src_ref=block(mate, b), dst_ref=right_at(right_far, c, seat, b),
            send_sem=sent_far.at[0], recv_sem=recv_far.at[c, b],
            device_id=(t * group + seat, c, f), device_id_type=MESH,
        )

    def came_far(col, b):
        return pltpu.make_async_remote_copy(
            src_ref=block(f, b), dst_ref=right_at(right_far, col, seat, b),
            send_sem=sent_far.at[0], recv_sem=recv_far.at[col, b],
            device_id=(r, c, f), device_id_type=MESH,
        )

    def pairing(ref, send, recv):
        def to_pair(col, b, other):
            return pltpu.make_async_remote_copy(
                src_ref=right_at(ref, col, seat, b), dst_ref=right_at(ref, col, seat, b),
                send_sem=send.at[0], recv_sem=recv.at[seat],
                device_id=(owner * group + other, c, f), device_id_type=MESH,
            )

        def came_pair(other, blocks):
            theirs = ref.at[pl.ds(other * rows, blocks * unit)]
            return pltpu.make_async_remote_copy(
                src_ref=theirs, dst_ref=theirs, send_sem=send.at[0], recv_sem=recv.at[other],
                device_id=(r, c, f), device_id_type=MESH,
            )

        return to_pair, came_pair

    to_pair, came_pair = pairing(right, sent_pair, recv_pair)
    to_far_pair, came_far_pair = pairing(right_far, sent_far_pair, recv_far_pair)

    def crossing(out, into, send, recv):
        def to_col(col, i):
            return pltpu.make_async_remote_copy(
                src_ref=out.at[col, chunk(i)], dst_ref=into.at[c, chunk(i)],
                send_sem=send.at[0], recv_sem=recv.at[lax.rem(c - col + n_col, n_col) - 1, i],
                device_id=(r, col, f), device_id_type=MESH,
            )

        def came_col(col, i):
            return pltpu.make_async_remote_copy(
                src_ref=out.at[col, chunk(i)], dst_ref=into.at[col, chunk(i)],
                send_sem=send.at[0], recv_sem=recv.at[lax.rem(col - c + n_col, n_col) - 1, i],
                device_id=(r, col, f), device_id_type=MESH,
            )

        return to_col, came_col

    to_col, came_col = crossing(part_out, part_in, sent_part, recv_part)
    to_help, came_help = crossing(help_out, help_in, sent_help, recv_help)

    def to_done(i):
        return pltpu.make_async_remote_copy(
            src_ref=helped.at[chunk(i)], dst_ref=helped.at[chunk(i)],
            send_sem=sent_done.at[0], recv_sem=recv_done.at[i],
            device_id=(r, c, mate), device_id_type=MESH,
        )

    def skips(place, far):
        return (far >= place * parts) & (far < (place + 1) * parts)

    def to_owner(col, i):
        return pltpu.make_async_remote_copy(
            src_ref=help_out.at[col, chunk(i)], dst_ref=help_in.at[c, chunk(i)],
            send_sem=sent_owner.at[0], recv_sem=recv_done.at[i],
            device_id=(r, col, mate), device_id_type=MESH,
        )

    def came_owner(i):
        all_cols = help_in.at[pl.ds(0, n_col), chunk(i)]
        return pltpu.make_async_remote_copy(
            src_ref=all_cols, dst_ref=all_cols, send_sem=sent_owner.at[0], recv_sem=recv_done.at[i],
            device_id=(r, c, f), device_id_type=MESH,
        )

    def served(place, b):
        return place * parts + b != mate

    def to_serve(b):
        return seat * parts + b != f

    def send_own(i, now_down, now_up):
        @pl.when(sends_down(i) & now_down)
        def _():
            along(f, i, False).start()

        @pl.when(sends_up(i) & now_up)
        def _():
            along(f, i, True).start()

    low, high = f == 1, f == n_fib - 2
    inner = jnp.logical_not(outer)
    direct_down = outer | jnp.logical_not(high)
    direct_up = outer | jnp.logical_not(low)

    @pl.loop(0, CHUNKS)
    def _(i):
        send_own(i, direct_down | (i < AHEAD), direct_up | (i < AHEAD))

    for b in range(parts):
        for t in range(n_row // group):
            @pl.when(jnp.logical_not(mine & (owner == t)))
            def _():
                to_right(t, b).start()

    @pl.when(mine)
    def _():
        for b in range(parts):
            spot = right_at(right, c, seat, b)
            spot[...] = left[f, b * unit:(b + 1) * unit]

    def pass_up(d, i):
        @pl.when((f - d >= 0) & gets_up(i))
        def _():
            along(f - d, i, True).wait_recv()

            @pl.when(sends_up(i))
            def _():
                along(f - d, i, True).start()

    def pass_down(d, i):
        @pl.when((f + d < n_fib) & gets_down(i))
        def _():
            along(f + d, i, False).wait_recv()

            @pl.when(sends_down(i))
            def _():
                along(f + d, i, False).start()

    def feed(i):
        @pl.when(low)
        def _():
            pass_up(1, i)

        @pl.when(high)
        def _():
            pass_down(1, i)

        @pl.when(i + AHEAD < CHUNKS)
        def _():
            send_own(i + AHEAD, high, low)

    def near(i):
        @pl.when(jnp.logical_not(low))
        def _():
            pass_up(1, i)

        @pl.when(jnp.logical_not(high))
        def _():
            pass_down(1, i)

    def far(i):
        for d in range(2, n_fib - 1):
            pass_up(d, i)
            pass_down(d, i)

    def side(b):
        @pl.when(helper & mine & served(seat, b))
        def _():
            for t in range(n_row // group):
                @pl.when(owner != t)
                def _():
                    to_side(t, b).start()

            spot = right_at(right_far, c, seat, b)
            spot[...] = left[mate, b * unit:(b + 1) * unit]

    def gather(b):
        for col in range(n_col):
            @pl.when(jnp.logical_not(mine & (c == col)))
            def _():
                came_right(col, b).wait_recv()

            if helps:
                @pl.when(outer & (c != col) & to_serve(b))
                def _():
                    to_far(col, b).start()

            for other in range(group):
                @pl.when(seat != other)
                def _():
                    to_pair(col, b, other).start()

    half = CHUNKS // 2

    def approach(first, last):
        @pl.when(inner)
        def _():
            @pl.loop(first, last)
            def _(p):
                feed(2 * p)
                near(p)
                feed(2 * p + 1)

                @pl.when(p > 1)
                def _():
                    far(p - 2)

    for b in range(parts):
        approach(half * b // parts, half * (b + 1) // parts)
        if helps:
            side(b)
        if b < parts - 1:
            gather(b)

    @pl.when(inner)
    def _():
        near(half)

    gather(parts - 1)

    for other in range(group):
        @pl.when(seat != other)
        def _():
            came_pair(other, parts).wait_recv()

    def products(ref, part, first, count):
        return jnp.dot(
            jnp.concatenate([left[first + k, part, :] for k in range(count)], axis=1),
            ref[pl.ds(first * unit if isinstance(first, int) else pl.multiple_of(first * unit, unit), count * unit), :],
            preferred_element_type=jnp.float32,
        )

    def store(total, ours, part, out):
        kept_total = total[:, :unit]
        for col in range(n_col):
            piece = total[:, col * unit:(col + 1) * unit]
            out[col, part, :] = piece.astype(jnp.bfloat16)
            if col:
                kept_total = jnp.where(c == col, piece, kept_total)
        ours[part, :] = kept_total

    def col_at(shift):
        return lax.rem(c + shift, n_col)

    sums[r] = jnp.zeros((8, unit), jnp.float32)

    def combine(i, h=None):
        part = chunk(i)
        expanded = own[part, :]
        for shift in range(1, n_col):
            came_col(col_at(shift), i).wait_recv()
            expanded += part_in[col_at(shift), part, :].astype(jnp.float32)
        if h is not None and h >= lead:
            came_owner(h).wait_recv()
            for col in range(n_col):
                expanded += help_in[col, pl.ds(h * step, step), :].astype(jnp.float32)
        elif h is not None:
            to_done(h).wait_recv()
            expanded += helped[pl.ds(h * step, step), :].astype(jnp.float32)
        squared = expanded * expanded
        own[part, :] = squared
        sums[r] += jnp.sum(squared.reshape(step // 8, 8, unit), axis=0)

    def fetch():
        for b in range(parts):
            @pl.when(served(seat, b))
            def _():
                for col in range(n_col):
                    @pl.when(jnp.logical_not(mine & (c == col)))
                    def _():
                        came_far(col, b).wait_recv()

                    for other in range(group):
                        @pl.when(seat != other)
                        def _():
                            to_far_pair(col, b, other).start()

    def answer():
        for other in range(group):
            for skipped in range(2):
                @pl.when((seat != other) & (skips(other, mate) == bool(skipped)))
                def _():
                    came_far_pair(other, parts - skipped).wait_recv()

        reckon(0, lead)

    def reckon(h, count):
        part = pl.ds(lent_at(h) * step, count * step)
        total = products(right_far, part, jnp.where(mate == 0, 1, 0), n_fib - 1)
        store(total, help_own, pl.ds(h * step, count * step), help_out)
        for i in range(h, h + count):
            for shift in range(n_col):
                if h >= lead:
                    to_owner(col_at(shift), i).start()
                elif shift:
                    to_help(col_at(shift), i).start()

    if helps:
        @pl.when(outer)
        def _():
            for h in range(helps):
                i = lent_at(h)
                part = pl.ds(i * step, step)
                store(products(right, part, f, 1), own, part, part_out)
                for shift in range(1, n_col):
                    to_col(col_at(shift), i).start()

    def advance(i):
        odd = lax.rem(i, 2) == 1

        @pl.when((i < CHUNKS - 5) & jnp.logical_not(odd))
        def _():
            far(half - 2 + i // 2)

        @pl.when((i < CHUNKS - 5) & odd)
        def _():
            near(half + 1 + i // 2)

        @pl.when((i == CHUNKS - 5) | (i == CHUNKS - 4))
        def _():
            near(i + 3)

        @pl.when((i >= CHUNKS - 5) & (i < CHUNKS - 1))
        def _():
            far(i + 1)

    @pl.loop(0, CHUNKS)
    def _(i):
        part = chunk(i)
        full = kept(i) | jnp.logical_not(outer)

        @pl.when(outer & full)
        def _():
            for d in range(1, n_fib):
                pass_up(d, i)
                pass_down(d, i)

        if helps:
            @pl.when(helper & (i == ANSWER))
            def _():
                answer()

        @pl.when(inner & ((i == ANSWER) | (i == CHUNKS - 2)))
        def _():
            advance(i)

        if late:
            @pl.when(helper & (i == CHUNKS - 2))
            def _():
                reckon(lead, late)

        @pl.when(full)
        def _():
            store(products(right, part, 0, n_fib), own, part, part_out)
            for shift in range(1, n_col):
                to_col(col_at(shift), i).start()

        if helps:
            @pl.when(helper & (i == FETCH))
            def _():
                fetch()

        @pl.when(inner & (i != ANSWER) & (i != CHUNKS - 2))
        def _():
            advance(i)

        @pl.when((i >= LAG) & (kept(i - LAG) | jnp.logical_not(outer)))
        def _():
            combine(i - LAG)

    def reply(h):
        @pl.when(helper)
        def _():
            part = pl.ds(h * step, step)
            total = help_own[part, :]
            for shift in range(1, n_col):
                came_help(col_at(shift), h).wait_recv()
                total += help_in[col_at(shift), part, :].astype(jnp.float32)
            helped[part, :] = total.astype(jnp.bfloat16)
            to_done(h).start()

    for h in range(lead):
        reply(h)

    @pl.loop(CHUNKS - LAG, CHUNKS)
    def _(i):
        @pl.when(kept(i) | inner)
        def _():
            combine(i)

    if helps:
        @pl.when(outer)
        def _():
            for h in range(helps):
                combine(lent_at(h), h)

    def to_row(shift):
        return pltpu.make_async_remote_copy(
            src_ref=sums.at[r], dst_ref=sums.at[r],
            send_sem=sent_sum.at[0], recv_sem=recv_sum.at[0],
            device_id=(lax.rem(r + shift, n_row), c, f), device_id_type=MESH,
        )

    def came_rows():
        return pltpu.make_async_remote_copy(
            src_ref=sums.at[pl.ds(0, n_row - 1)], dst_ref=sums.at[pl.ds(0, n_row - 1)],
            send_sem=sent_sum.at[0], recv_sem=recv_sum.at[0],
            device_id=(r, c, f), device_id_type=MESH,
        )

    for shift in range(1, n_row):
        to_row(shift).start()
    came_rows().wait_recv()
    total = sums[0]
    for other in range(1, n_row):
        total += sums[other]
    scale = jnp.sum(total, axis=0, keepdims=True) / (rows * n_row) + 1e-6
    inverse_ref[...] = jnp.broadcast_to(1.0 / scale, inverse_ref.shape)

    def left_behind(sem, ref):
        pltpu.make_async_remote_copy(
            src_ref=ref, dst_ref=ref, send_sem=sem, recv_sem=recv_sum.at[0],
            device_id=(r, c, f), device_id_type=MESH,
        ).wait_send()

    few = helps * step
    for at in range(n_fib):
        @pl.when(f == at)
        def _():
            if at < n_fib - 1:
                less = few if at == n_fib - 2 else 0
                left_behind(sent_left.at[1], left.at[pl.ds(0, at + 1), pl.ds(0, rows - less)])
            if at > 0:
                less = few if at == 1 else 0
                left_behind(sent_left.at[0], left.at[pl.ds(0, n_fib - at), pl.ds(0, rows - less)])

    for less in range(2):
        if n_col > less:
            @pl.when(mine == bool(less))
            def _():
                left_behind(sent_right.at[0], part_out.at[pl.ds(0, n_col - less)])

    if group > 1:
        left_behind(sent_pair.at[0], right.at[pl.ds(0, (group - 1) * rows)])
    if n_col > 1:
        left_behind(sent_part.at[0], part_out.at[pl.ds(0, n_col - 1)])
    if n_row > 1:
        left_behind(sent_sum.at[0], sums.at[pl.ds(0, n_row - 1)])

    if helps:
        for less in range(2):
            size = (parts - less) * unit
            across = pl.ds(0, (n_col - 1) * unit)
            if size and n_col > 1:
                @pl.when(skips(seat, jnp.where(outer, f, mate)) == bool(less))
                def _():
                    @pl.when(outer | (helper & mine))
                    def _():
                        left_behind(sent_far.at[0], right.at[pl.ds(0, size), across])

            if size and group > 1:
                @pl.when(helper & (skips(seat, mate) == bool(less)))
                def _():
                    left_behind(sent_far_pair.at[0], right.at[pl.ds(0, (group - 1) * size)])

        @pl.when(helper)
        def _():
            if lead:
                if n_col > 1:
                    left_behind(sent_help.at[0], help_out.at[pl.ds(0, n_col - 1), pl.ds(0, lead * step)])
                left_behind(sent_done.at[0], helped.at[pl.ds(0, lead * step)])
            if late:
                left_behind(sent_owner.at[0], help_out.at[pl.ds(0, n_col), pl.ds(lead * step, late * step)])


def prune(keep_ref, squared_ref, inverse_ref, out_hbm, out_vmem, sem):
    tile = out_vmem.shape[1] // keep_ref.shape[0]
    copies = []
    for i in range(keep_ref.shape[1]):
        down = slice(i * tile, (i + 1) * tile)
        for j in range(keep_ref.shape[0]):
            across = slice(j * tile, (j + 1) * tile)
            factor = inverse_ref[0:1, across] * keep_ref[j, i].astype(jnp.float32)
            out_vmem[down, across] = squared_ref[down, across] * factor
        copy = pltpu.make_async_copy(out_vmem.at[down], out_hbm.at[down], sem.at[i])
        copy.start()
        copies.append(copy)
    for copy in copies:
        copy.wait()


def solution(mesh):
    n_row, n_col, n_fib = (mesh.shape[name] for name in ("row", "col", "fiber"))
    group = n_row // n_col
    helps = HELP if n_fib > 3 else 0

    def local(values, tile_mask, keep_mask):
        rows, unit = values.shape
        dma = pltpu.SemaphoreType.DMA
        parts = rows // unit
        few = rows // CHUNKS * HELP
        squared, inverse = pl.pallas_call(
            functools.partial(kernel, n_row, n_col, n_fib, helps),
            out_shape=(
                pltpu.VMEM((rows, unit), jnp.float32),
                pltpu.VMEM((8, unit), jnp.float32),
            ),
            in_specs=[
                pl.BlockSpec(memory_space=pltpu.HBM),
                pl.BlockSpec(memory_space=pltpu.HBM),
            ],
            out_specs=(
                pl.BlockSpec(memory_space=pltpu.VMEM),
                pl.BlockSpec(memory_space=pltpu.VMEM),
            ),
            scratch_shapes=[
                pltpu.SMEM(tile_mask.shape[::-1], jnp.int32),
                pltpu.VMEM((rows, unit), jnp.float32),
                pltpu.VMEM((n_fib, rows, unit), jnp.bfloat16),
                pltpu.VMEM((group * rows, n_col * unit), jnp.bfloat16),
                pltpu.VMEM((n_col, rows, unit), jnp.bfloat16),
                pltpu.VMEM((n_col, rows, unit), jnp.bfloat16),
                pltpu.VMEM((n_row, 8, unit), jnp.float32),
                pltpu.VMEM((group * rows, n_col * unit), jnp.bfloat16),
                pltpu.VMEM((few, unit), jnp.float32),
                pltpu.VMEM((n_col, few, unit), jnp.bfloat16),
                pltpu.VMEM((n_col, few, unit), jnp.bfloat16),
                pltpu.VMEM((few, unit), jnp.bfloat16),
                dma((2,)),
                dma((2,)),
                dma((1,)),
                dma((1,)),
                dma((1,)),
                dma((1,)),
                dma((1,)),
                dma((1,)),
                dma((1,)),
                dma((1,)),
                dma((1,)),
                dma((n_fib - 1, CHUNKS)),
                dma((n_col, parts)),
                dma((group,)),
                dma((n_col - 1, CHUNKS)),
                dma((1,)),
                dma((n_col, parts)),
                dma((group,)),
                dma((n_col - 1, HELP)),
                dma((HELP,)),
            ],
            compiler_params=pltpu.CompilerParams(
                collective_id=0, has_side_effects=True, vmem_limit_bytes=VMEM_LIMIT
            ),
            name="expand",
        )(tile_mask.T, values)
        return pl.pallas_call(
            prune,
            out_shape=jax.ShapeDtypeStruct((rows, unit), jnp.float32),
            in_specs=[
                pl.BlockSpec(memory_space=pltpu.SMEM),
                pl.BlockSpec(memory_space=pltpu.VMEM),
                pl.BlockSpec(memory_space=pltpu.VMEM),
            ],
            out_specs=pl.BlockSpec(memory_space=pl.ANY),
            scratch_shapes=[
                pltpu.VMEM((rows, unit), jnp.float32),
                dma((keep_mask.shape[0],)),
            ],
            compiler_params=pltpu.CompilerParams(vmem_limit_bytes=8 * 1024 * 1024),
            name="prune",
        )(keep_mask.T, squared, inverse)

    spec = P("row", ("col", "fiber"))
    return jax.shard_map(
        local, mesh=mesh, in_specs=(spec, spec, spec), out_specs=spec, check_vma=False
    )
```

```python
import functools

import jax
import jax.numpy as jnp
from jax import lax
from jax.experimental import pallas as pl
from jax.experimental.pallas import tpu as pltpu
from jax.sharding import PartitionSpec as P

MESH = pl.DeviceIdType.MESH
CHUNKS = 12
HELP = 3
TRAIL = 1
AHEAD = 4
FETCH = 7
ANSWER = 9
LAG = 4
VMEM_LIMIT = 62 * 1024 * 1024


def kernel(
    n_row, n_col, n_fib, helps, tile_hbm, values_hbm, own, inverse_ref,
    tile_ref, values_ref, left, right, part_out, part_in, folded, sums,
    right_far, help_own, help_out, help_in, helped, load_sem,
    sent_left, sent_right, sent_pair, sent_part, sent_sum, sent_far, sent_far_pair, sent_help, sent_done, sent_owner,
    recv_left, recv_right, recv_pair, recv_part, recv_sum,
    recv_far, recv_far_pair, recv_help, recv_done,
):
    r, c, f = lax.axis_index("row"), lax.axis_index("col"), lax.axis_index("fiber")
    rows, unit = values_ref.shape
    tile = unit // tile_ref.shape[0]
    step = rows // CHUNKS
    parts = rows // unit
    group = n_row // n_col
    owner, seat = r // group, lax.rem(r, group)

    load = pltpu.make_async_copy(values_hbm, values_ref, load_sem.at[0])
    load.start()
    load_tile = pltpu.make_async_copy(tile_hbm, tile_ref, load_sem.at[1])
    load_tile.start()

    barrier = pltpu.get_barrier_semaphore()
    for dr in range(n_row):
        for dc in range(n_col):
            if dr or dc:
                pl.semaphore_signal(
                    barrier, inc=1, device_id_type=MESH,
                    device_id=(lax.rem(r + dr, n_row), lax.rem(c + dc, n_col), f),
                )

    has_down, has_up = f > 0, f < n_fib - 1
    outer = jnp.logical_not(has_down & has_up)
    helper = (f == 1) | (f == n_fib - 2)
    mate = jnp.where(outer, jnp.where(has_down, f - 1, 1), jnp.where(f == 1, 0, n_fib - 1))
    mine = owner == c

    @pl.when(has_down)
    def _():
        pl.semaphore_signal(barrier, inc=1, device_id=(r, c, f - 1), device_id_type=MESH)

    @pl.when(has_up)
    def _():
        pl.semaphore_signal(barrier, inc=1, device_id=(r, c, f + 1), device_id_type=MESH)

    load_tile.wait()
    load.wait()

    for i in range(rows // tile):
        for j in range(unit // tile):
            at = (pl.ds(i * tile, tile), pl.ds(j * tile, tile))
            masked = values_ref[at] * tile_ref[j, i].astype(jnp.float32)
            left[f, i * tile:(i + 1) * tile, j * tile:(j + 1) * tile] = masked.astype(jnp.bfloat16)

    neighbours = has_down.astype(jnp.int32) + has_up.astype(jnp.int32)
    pl.semaphore_wait(barrier, n_row * n_col - 1 + neighbours)

    def chunk(i):
        return pl.ds(i * step if isinstance(i, int) else pl.multiple_of(i * step, step), step)

    def along(source, i, up):
        part = left.at[source, chunk(i)]
        return pltpu.make_async_remote_copy(
            src_ref=part, dst_ref=part,
            send_sem=sent_left.at[int(up)], recv_sem=recv_left.at[source if up else source - 1, i],
            device_id=(r, c, f + 1 if up else f - 1), device_id_type=MESH,
        )

    late = min(helps, TRAIL)
    lead = helps - late

    def kept(i):
        return (i >= lead) & (i < CHUNKS - late)

    def lent_at(h):
        return h if h < lead else h - helps + CHUNKS

    def sends_up(i):
        return has_up & (kept(i) | (f + 1 < n_fib - 1))

    def sends_down(i):
        return has_down & (kept(i) | (f - 1 > 0))

    def gets_up(i):
        return kept(i) | has_up

    def gets_down(i):
        return kept(i) | has_down

    def right_at(ref, col, place, b):
        return ref.at[
            pl.ds(pl.multiple_of(place * rows + b * unit, unit), unit),
            pl.ds(pl.multiple_of(col * unit, unit), unit),
        ]

    def block(source, b):
        return left.at[source, pl.ds(b * unit, unit)]

    def to_right(t, b):
        return pltpu.make_async_remote_copy(
            src_ref=block(f, b), dst_ref=right_at(right, c, seat, b),
            send_sem=sent_right.at[0], recv_sem=recv_right.at[c, b],
            device_id=(t * group + seat, owner, f), device_id_type=MESH,
        )

    def came_right(col, b):
        return pltpu.make_async_remote_copy(
            src_ref=block(f, b), dst_ref=right_at(right, col, seat, b),
            send_sem=sent_right.at[0], recv_sem=recv_right.at[col, b],
            device_id=(r, c, f), device_id_type=MESH,
        )

    def to_far(col, b):
        return pltpu.make_async_remote_copy(
            src_ref=right_at(right, col, seat, b), dst_ref=right_at(right_far, col, seat, b),
            send_sem=sent_far.at[0], recv_sem=recv_far.at[col, b],
            device_id=(r, c, mate), device_id_type=MESH,
        )

    def to_side(t, b):
        return pltpu.make_async_remote_copy(
            src_ref=block(mate, b), dst_ref=right_at(right_far, c, seat, b),
            send_sem=sent_far.at[0], recv_sem=recv_far.at[c, b],
            device_id=(t * group + seat, c, f), device_id_type=MESH,
        )

    def came_far(col, b):
        return pltpu.make_async_remote_copy(
            src_ref=block(f, b), dst_ref=right_at(right_far, col, seat, b),
            send_sem=sent_far.at[0], recv_sem=recv_far.at[col, b],
            device_id=(r, c, f), device_id_type=MESH,
        )

    def pairing(ref, send, recv):
        def to_pair(col, b, other):
            return pltpu.make_async_remote_copy(
                src_ref=right_at(ref, col, seat, b), dst_ref=right_at(ref, col, seat, b),
                send_sem=send.at[0], recv_sem=recv.at[seat],
                device_id=(owner * group + other, c, f), device_id_type=MESH,
            )

        def came_pair(other, blocks):
            theirs = ref.at[pl.ds(other * rows, blocks * unit)]
            return pltpu.make_async_remote_copy(
                src_ref=theirs, dst_ref=theirs, send_sem=send.at[0], recv_sem=recv.at[other],
                device_id=(r, c, f), device_id_type=MESH,
            )

        return to_pair, came_pair

    to_pair, came_pair = pairing(right, sent_pair, recv_pair)
    to_far_pair, came_far_pair = pairing(right_far, sent_far_pair, recv_far_pair)

    def crossing(out, into, send, recv):
        def to_col(col, i):
            return pltpu.make_async_remote_copy(
                src_ref=out.at[col, chunk(i)], dst_ref=into.at[c, chunk(i)],
                send_sem=send.at[0], recv_sem=recv.at[lax.rem(c - col + n_col, n_col) - 1, i],
                device_id=(r, col, f), device_id_type=MESH,
            )

        def came_col(col, i):
            return pltpu.make_async_remote_copy(
                src_ref=out.at[col, chunk(i)], dst_ref=into.at[col, chunk(i)],
                send_sem=send.at[0], recv_sem=recv.at[lax.rem(col - c + n_col, n_col) - 1, i],
                device_id=(r, col, f), device_id_type=MESH,
            )

        return to_col, came_col

    to_col, came_col = crossing(part_out, part_in, sent_part, recv_part)
    to_help, came_help = crossing(help_out, help_in, sent_help, recv_help)

    def to_done(i):
        return pltpu.make_async_remote_copy(
            src_ref=helped.at[chunk(i)], dst_ref=helped.at[chunk(i)],
            send_sem=sent_done.at[0], recv_sem=recv_done.at[i],
            device_id=(r, c, mate), device_id_type=MESH,
        )

    def skips(place, far):
        return (far >= place * parts) & (far < (place + 1) * parts)

    def to_owner(col, i):
        return pltpu.make_async_remote_copy(
            src_ref=help_out.at[col, chunk(i)], dst_ref=help_in.at[c, chunk(i)],
            send_sem=sent_owner.at[0], recv_sem=recv_done.at[i],
            device_id=(r, col, mate), device_id_type=MESH,
        )

    def came_owner(i):
        all_cols = help_in.at[pl.ds(0, n_col), chunk(i)]
        return pltpu.make_async_remote_copy(
            src_ref=all_cols, dst_ref=all_cols, send_sem=sent_owner.at[0], recv_sem=recv_done.at[i],
            device_id=(r, c, f), device_id_type=MESH,
        )

    def served(place, b):
        return place * parts + b != mate

    def to_serve(b):
        return seat * parts + b != f

    def send_own(i, now_down, now_up):
        @pl.when(sends_down(i) & now_down)
        def _():
            along(f, i, False).start()

        @pl.when(sends_up(i) & now_up)
        def _():
            along(f, i, True).start()

    low, high = f == 1, f == n_fib - 2
    inner = jnp.logical_not(outer)
    direct_down = outer | jnp.logical_not(high)
    direct_up = outer | jnp.logical_not(low)

    @pl.loop(0, CHUNKS)
    def _(i):
        send_own(i, direct_down | (i < AHEAD), direct_up | (i < AHEAD))

    for b in range(parts):
        for t in range(n_row // group):
            @pl.when(jnp.logical_not(mine & (owner == t)))
            def _():
                to_right(t, b).start()

    @pl.when(mine)
    def _():
        for b in range(parts):
            spot = right_at(right, c, seat, b)
            spot[...] = left[f, b * unit:(b + 1) * unit]

    def pass_up(d, i):
        @pl.when((f - d >= 0) & gets_up(i))
        def _():
            along(f - d, i, True).wait_recv()

            @pl.when(sends_up(i))
            def _():
                along(f - d, i, True).start()

    def pass_down(d, i):
        @pl.when((f + d < n_fib) & gets_down(i))
        def _():
            along(f + d, i, False).wait_recv()

            @pl.when(sends_down(i))
            def _():
                along(f + d, i, False).start()

    def feed(i):
        @pl.when(low)
        def _():
            pass_up(1, i)

        @pl.when(high)
        def _():
            pass_down(1, i)

        @pl.when(i + AHEAD < CHUNKS)
        def _():
            send_own(i + AHEAD, high, low)

    def near(i):
        @pl.when(jnp.logical_not(low))
        def _():
            pass_up(1, i)

        @pl.when(jnp.logical_not(high))
        def _():
            pass_down(1, i)

    def far(i):
        for d in range(2, n_fib - 1):
            pass_up(d, i)
            pass_down(d, i)

    def side(b):
        @pl.when(helper & mine & served(seat, b))
        def _():
            for t in range(n_row // group):
                @pl.when(owner != t)
                def _():
                    to_side(t, b).start()

            spot = right_at(right_far, c, seat, b)
            spot[...] = left[mate, b * unit:(b + 1) * unit]

    def gather(b):
        for col in range(n_col):
            @pl.when(jnp.logical_not(mine & (c == col)))
            def _():
                came_right(col, b).wait_recv()

            if helps:
                @pl.when(outer & (c != col) & to_serve(b))
                def _():
                    to_far(col, b).start()

            for other in range(group):
                @pl.when(seat != other)
                def _():
                    to_pair(col, b, other).start()

    half = CHUNKS // 2

    def approach(first, last):
        @pl.when(inner)
        def _():
            @pl.loop(first, last)
            def _(p):
                feed(2 * p)
                near(p)
                feed(2 * p + 1)

                @pl.when(p > 1)
                def _():
                    far(p - 2)

    for b in range(parts):
        approach(half * b // parts, half * (b + 1) // parts)
        if helps:
            side(b)
        if b < parts - 1:
            gather(b)

    @pl.when(inner)
    def _():
        near(half)

    gather(parts - 1)

    for other in range(group):
        @pl.when(seat != other)
        def _():
            came_pair(other, parts).wait_recv()

    def products(ref, part, first, count):
        return jnp.dot(
            jnp.concatenate([left[first + k, part, :] for k in range(count)], axis=1),
            ref[pl.ds(first * unit if isinstance(first, int) else pl.multiple_of(first * unit, unit), count * unit), :],
            preferred_element_type=jnp.float32,
        )

    def store(total, ours, part, out):
        kept_total = total[:, :unit]
        for col in range(n_col):
            piece = total[:, col * unit:(col + 1) * unit]
            out[col, part, :] = piece.astype(jnp.bfloat16)
            if col:
                kept_total = jnp.where(c == col, piece, kept_total)
        ours[part, :] = kept_total

    def col_at(shift):
        return lax.rem(c + shift, n_col)

    folded[...] = jnp.zeros((8, unit), jnp.float32)

    def combine(i, h=None):
        part = chunk(i)
        expanded = own[part, :]
        for shift in range(1, n_col):
            came_col(col_at(shift), i).wait_recv()
            expanded += part_in[col_at(shift), part, :].astype(jnp.float32)
        if h is not None and h >= lead:
            came_owner(h).wait_recv()
            for col in range(n_col):
                expanded += help_in[col, pl.ds(h * step, step), :].astype(jnp.float32)
        elif h is not None:
            to_done(h).wait_recv()
            expanded += helped[pl.ds(h * step, step), :].astype(jnp.float32)
        squared = expanded * expanded
        own[part, :] = squared
        folded[...] += jnp.sum(squared.reshape(step // 8, 8, unit), axis=0)

    def fetch():
        for b in range(parts):
            @pl.when(served(seat, b))
            def _():
                for col in range(n_col):
                    @pl.when(jnp.logical_not(mine & (c == col)))
                    def _():
                        came_far(col, b).wait_recv()

                    for other in range(group):
                        @pl.when(seat != other)
                        def _():
                            to_far_pair(col, b, other).start()

    def answer():
        for other in range(group):
            for skipped in range(2):
                @pl.when((seat != other) & (skips(other, mate) == bool(skipped)))
                def _():
                    came_far_pair(other, parts - skipped).wait_recv()

        reckon(0, lead)

    def reckon(h, count):
        part = pl.ds(lent_at(h) * step, count * step)
        total = products(right_far, part, jnp.where(mate == 0, 1, 0), n_fib - 1)
        store(total, help_own, pl.ds(h * step, count * step), help_out)
        for i in range(h, h + count):
            for shift in range(n_col):
                if h >= lead:
                    to_owner(col_at(shift), i).start()
                elif shift:
                    to_help(col_at(shift), i).start()

    if helps:
        @pl.when(outer)
        def _():
            for h in range(helps):
                i = lent_at(h)
                part = pl.ds(i * step, step)
                store(products(right, part, f, 1), own, part, part_out)
                for shift in range(1, n_col):
                    to_col(col_at(shift), i).start()

    def advance(i):
        odd = lax.rem(i, 2) == 1

        @pl.when(i == 0)
        def _():
            near(half + 1)

        @pl.when((i < CHUNKS - 5) & jnp.logical_not(odd))
        def _():
            far(half - 2 + i // 2)

        @pl.when((i <= CHUNKS - 5) & odd)
        def _():
            near(half + 2 + i // 2)

        @pl.when((i >= CHUNKS - 5) & (i < CHUNKS - 1))
        def _():
            far(i + 1)

    @pl.loop(0, CHUNKS)
    def _(i):
        part = chunk(i)
        full = kept(i) | jnp.logical_not(outer)

        @pl.when(outer & full)
        def _():
            for d in range(1, n_fib):
                pass_up(d, i)
                pass_down(d, i)

        if helps:
            @pl.when(helper & (i == ANSWER))
            def _():
                answer()

        @pl.when(inner & ((i == ANSWER) | (i == CHUNKS - 2)))
        def _():
            advance(i)

        if late:
            @pl.when(helper & (i == CHUNKS - 2))
            def _():
                reckon(lead, late)

        @pl.when(full)
        def _():
            store(products(right, part, 0, n_fib), own, part, part_out)
            for shift in range(1, n_col):
                to_col(col_at(shift), i).start()

        if helps:
            @pl.when(helper & (i == FETCH))
            def _():
                fetch()

        @pl.when(inner & (i != ANSWER) & (i != CHUNKS - 2))
        def _():
            advance(i)

        @pl.when((i >= LAG) & (kept(i - LAG) | jnp.logical_not(outer)))
        def _():
            combine(i - LAG)

    def reply(h):
        @pl.when(helper)
        def _():
            part = pl.ds(h * step, step)
            total = help_own[part, :]
            for shift in range(1, n_col):
                came_help(col_at(shift), h).wait_recv()
                total += help_in[col_at(shift), part, :].astype(jnp.float32)
            helped[part, :] = total.astype(jnp.bfloat16)
            to_done(h).start()

    for h in range(lead):
        reply(h)

    @pl.loop(CHUNKS - LAG, CHUNKS)
    def _(i):
        @pl.when(kept(i) | inner)
        def _():
            combine(i)

    if helps:
        @pl.when(outer)
        def _():
            for h in range(helps):
                combine(lent_at(h), h)

    def to_row(shift):
        return pltpu.make_async_remote_copy(
            src_ref=sums.at[r], dst_ref=sums.at[r],
            send_sem=sent_sum.at[0], recv_sem=recv_sum.at[0],
            device_id=(lax.rem(r + shift, n_row), c, f), device_id_type=MESH,
        )

    def came_rows():
        return pltpu.make_async_remote_copy(
            src_ref=sums.at[pl.ds(0, n_row - 1)], dst_ref=sums.at[pl.ds(0, n_row - 1)],
            send_sem=sent_sum.at[0], recv_sem=recv_sum.at[0],
            device_id=(r, c, f), device_id_type=MESH,
        )

    sums[r] = jnp.sum(folded[...], axis=0, keepdims=True)
    for shift in range(1, n_row):
        to_row(shift).start()
    came_rows().wait_recv()
    total = sums[0]
    for other in range(1, n_row):
        total += sums[other]
    scale = total / (rows * n_row) + 1e-6
    inverse_ref[...] = jnp.broadcast_to(1.0 / scale, inverse_ref.shape)

    def left_behind(sem, ref):
        pltpu.make_async_remote_copy(
            src_ref=ref, dst_ref=ref, send_sem=sem, recv_sem=recv_sum.at[0],
            device_id=(r, c, f), device_id_type=MESH,
        ).wait_send()

    few = helps * step
    for at in range(n_fib):
        @pl.when(f == at)
        def _():
            if at < n_fib - 1:
                less = few if at == n_fib - 2 else 0
                left_behind(sent_left.at[1], left.at[pl.ds(0, at + 1), pl.ds(0, rows - less)])
            if at > 0:
                less = few if at == 1 else 0
                left_behind(sent_left.at[0], left.at[pl.ds(0, n_fib - at), pl.ds(0, rows - less)])

    for less in range(2):
        if n_col > less:
            @pl.when(mine == bool(less))
            def _():
                left_behind(sent_right.at[0], part_out.at[pl.ds(0, n_col - less)])

    if group > 1:
        left_behind(sent_pair.at[0], right.at[pl.ds(0, (group - 1) * rows)])
    if n_col > 1:
        left_behind(sent_part.at[0], part_out.at[pl.ds(0, n_col - 1)])
    if n_row > 1:
        left_behind(sent_sum.at[0], sums.at[pl.ds(0, n_row - 1)])

    if helps:
        for less in range(2):
            size = (parts - less) * unit
            across = pl.ds(0, (n_col - 1) * unit)
            if size and n_col > 1:
                @pl.when(skips(seat, jnp.where(outer, f, mate)) == bool(less))
                def _():
                    @pl.when(outer | (helper & mine))
                    def _():
                        left_behind(sent_far.at[0], right.at[pl.ds(0, size), across])

            if size and group > 1:
                @pl.when(helper & (skips(seat, mate) == bool(less)))
                def _():
                    left_behind(sent_far_pair.at[0], right.at[pl.ds(0, (group - 1) * size)])

        @pl.when(helper)
        def _():
            if lead:
                if n_col > 1:
                    left_behind(sent_help.at[0], help_out.at[pl.ds(0, n_col - 1), pl.ds(0, lead * step)])
                left_behind(sent_done.at[0], helped.at[pl.ds(0, lead * step)])
            if late:
                left_behind(sent_owner.at[0], help_out.at[pl.ds(0, n_col), pl.ds(lead * step, late * step)])


def prune(keep_ref, squared_ref, inverse_ref, out_hbm, out_vmem, sem):
    tile = out_vmem.shape[1] // keep_ref.shape[0]
    copies = []
    for i in range(keep_ref.shape[1]):
        down = slice(i * tile, (i + 1) * tile)
        for j in range(keep_ref.shape[0]):
            across = slice(j * tile, (j + 1) * tile)
            factor = inverse_ref[0:1, across] * keep_ref[j, i].astype(jnp.float32)
            out_vmem[down, across] = squared_ref[down, across] * factor
        copy = pltpu.make_async_copy(out_vmem.at[down], out_hbm.at[down], sem.at[i])
        copy.start()
        copies.append(copy)
    for copy in copies:
        copy.wait()


def solution(mesh):
    n_row, n_col, n_fib = (mesh.shape[name] for name in ("row", "col", "fiber"))
    group = n_row // n_col
    helps = HELP if n_fib > 3 else 0

    def local(values, tile_mask, keep_mask):
        rows, unit = values.shape
        dma = pltpu.SemaphoreType.DMA
        parts = rows // unit
        few = rows // CHUNKS * HELP
        squared, inverse = pl.pallas_call(
            functools.partial(kernel, n_row, n_col, n_fib, helps),
            out_shape=(
                pltpu.VMEM((rows, unit), jnp.float32),
                pltpu.VMEM((8, unit), jnp.float32),
            ),
            in_specs=[
                pl.BlockSpec(memory_space=pltpu.HBM),
                pl.BlockSpec(memory_space=pltpu.HBM),
            ],
            out_specs=(
                pl.BlockSpec(memory_space=pltpu.VMEM),
                pl.BlockSpec(memory_space=pltpu.VMEM),
            ),
            scratch_shapes=[
                pltpu.SMEM(tile_mask.shape[::-1], jnp.int32),
                pltpu.VMEM((rows, unit), jnp.float32),
                pltpu.VMEM((n_fib, rows, unit), jnp.bfloat16),
                pltpu.VMEM((group * rows, n_col * unit), jnp.bfloat16),
                pltpu.VMEM((n_col, rows, unit), jnp.bfloat16),
                pltpu.VMEM((n_col, rows, unit), jnp.bfloat16),
                pltpu.VMEM((8, unit), jnp.float32),
                pltpu.VMEM((n_row, 1, unit), jnp.float32),
                pltpu.VMEM((group * rows, n_col * unit), jnp.bfloat16),
                pltpu.VMEM((few, unit), jnp.float32),
                pltpu.VMEM((n_col, few, unit), jnp.bfloat16),
                pltpu.VMEM((n_col, few, unit), jnp.bfloat16),
                pltpu.VMEM((few, unit), jnp.bfloat16),
                dma((2,)),
                dma((2,)),
                dma((1,)),
                dma((1,)),
                dma((1,)),
                dma((1,)),
                dma((1,)),
                dma((1,)),
                dma((1,)),
                dma((1,)),
                dma((1,)),
                dma((n_fib - 1, CHUNKS)),
                dma((n_col, parts)),
                dma((group,)),
                dma((n_col - 1, CHUNKS)),
                dma((1,)),
                dma((n_col, parts)),
                dma((group,)),
                dma((n_col - 1, HELP)),
                dma((HELP,)),
            ],
            compiler_params=pltpu.CompilerParams(
                collective_id=0, has_side_effects=True, vmem_limit_bytes=VMEM_LIMIT
            ),
            name="expand",
        )(tile_mask.T, values)
        return pl.pallas_call(
            prune,
            out_shape=jax.ShapeDtypeStruct((rows, unit), jnp.float32),
            in_specs=[
                pl.BlockSpec(memory_space=pltpu.SMEM),
                pl.BlockSpec(memory_space=pltpu.VMEM),
                pl.BlockSpec(memory_space=pltpu.VMEM),
            ],
            out_specs=pl.BlockSpec(memory_space=pl.ANY),
            scratch_shapes=[
                pltpu.VMEM((rows, unit), jnp.float32),
                dma((keep_mask.shape[0],)),
            ],
            compiler_params=pltpu.CompilerParams(vmem_limit_bytes=8 * 1024 * 1024),
            name="prune",
        )(keep_mask.T, squared, inverse)

    spec = P("row", ("col", "fiber"))
    return jax.shard_map(
        local, mesh=mesh, in_specs=(spec, spec, spec), out_specs=spec, check_vma=False
    )
```

```python
import functools

import jax
import jax.numpy as jnp
from jax import lax
from jax.experimental import pallas as pl
from jax.experimental.pallas import tpu as pltpu
from jax.sharding import PartitionSpec as P

MESH = pl.DeviceIdType.MESH
CHUNKS = 12
HELP = 3
TRAIL = 1
AHEAD = 4
FETCH = 7
ANSWER = 9
LAG = 4
VMEM_LIMIT = 62 * 1024 * 1024


def kernel(
    n_row, n_col, n_fib, helps, tile_hbm, keep_hbm, values_hbm, own, factor_ref,
    tile_ref, keep_ref, values_ref, left, right, part_out, part_in, folded, sums,
    right_far, help_own, help_out, help_in, helped, load_sem,
    sent_left, sent_right, sent_pair, sent_part, sent_sum, sent_far, sent_far_pair, sent_help, sent_done, sent_owner,
    recv_left, recv_right, recv_pair, recv_part, recv_sum,
    recv_far, recv_far_pair, recv_help, recv_done,
):
    r, c, f = lax.axis_index("row"), lax.axis_index("col"), lax.axis_index("fiber")
    rows, unit = values_ref.shape
    tile = unit // tile_ref.shape[0]
    step = rows // CHUNKS
    parts = rows // unit
    group = n_row // n_col
    owner, seat = r // group, lax.rem(r, group)

    load = pltpu.make_async_copy(values_hbm, values_ref, load_sem.at[0])
    load.start()
    load_tile = pltpu.make_async_copy(tile_hbm, tile_ref, load_sem.at[1])
    load_tile.start()
    load_keep = pltpu.make_async_copy(keep_hbm, keep_ref, load_sem.at[2])
    load_keep.start()

    barrier = pltpu.get_barrier_semaphore()
    for dr in range(n_row):
        for dc in range(n_col):
            if dr or dc:
                pl.semaphore_signal(
                    barrier, inc=1, device_id_type=MESH,
                    device_id=(lax.rem(r + dr, n_row), lax.rem(c + dc, n_col), f),
                )

    has_down, has_up = f > 0, f < n_fib - 1
    outer = jnp.logical_not(has_down & has_up)
    helper = (f == 1) | (f == n_fib - 2)
    mate = jnp.where(outer, jnp.where(has_down, f - 1, 1), jnp.where(f == 1, 0, n_fib - 1))
    mine = owner == c

    @pl.when(has_down)
    def _():
        pl.semaphore_signal(barrier, inc=1, device_id=(r, c, f - 1), device_id_type=MESH)

    @pl.when(has_up)
    def _():
        pl.semaphore_signal(barrier, inc=1, device_id=(r, c, f + 1), device_id_type=MESH)

    load_tile.wait()
    load_keep.wait()
    load.wait()

    for i in range(rows // tile):
        for j in range(unit // tile):
            at = (pl.ds(i * tile, tile), pl.ds(j * tile, tile))
            masked = values_ref[at] * tile_ref[j, i].astype(jnp.float32)
            left[f, i * tile:(i + 1) * tile, j * tile:(j + 1) * tile] = masked.astype(jnp.bfloat16)

    neighbours = has_down.astype(jnp.int32) + has_up.astype(jnp.int32)
    pl.semaphore_wait(barrier, n_row * n_col - 1 + neighbours)

    def chunk(i):
        return pl.ds(i * step if isinstance(i, int) else pl.multiple_of(i * step, step), step)

    def along(source, i, up):
        part = left.at[source, chunk(i)]
        return pltpu.make_async_remote_copy(
            src_ref=part, dst_ref=part,
            send_sem=sent_left.at[int(up)], recv_sem=recv_left.at[source if up else source - 1, i],
            device_id=(r, c, f + 1 if up else f - 1), device_id_type=MESH,
        )

    late = min(helps, TRAIL)
    lead = helps - late

    def kept(i):
        return (i >= lead) & (i < CHUNKS - late)

    def lent_at(h):
        return h if h < lead else h - helps + CHUNKS

    def sends_up(i):
        return has_up & (kept(i) | (f + 1 < n_fib - 1))

    def sends_down(i):
        return has_down & (kept(i) | (f - 1 > 0))

    def gets_up(i):
        return kept(i) | has_up

    def gets_down(i):
        return kept(i) | has_down

    def right_at(ref, col, place, b):
        return ref.at[
            pl.ds(pl.multiple_of(place * rows + b * unit, unit), unit),
            pl.ds(pl.multiple_of(col * unit, unit), unit),
        ]

    def block(source, b):
        return left.at[source, pl.ds(b * unit, unit)]

    def to_right(t, b):
        return pltpu.make_async_remote_copy(
            src_ref=block(f, b), dst_ref=right_at(right, c, seat, b),
            send_sem=sent_right.at[0], recv_sem=recv_right.at[c, b],
            device_id=(t * group + seat, owner, f), device_id_type=MESH,
        )

    def came_right(col, b):
        return pltpu.make_async_remote_copy(
            src_ref=block(f, b), dst_ref=right_at(right, col, seat, b),
            send_sem=sent_right.at[0], recv_sem=recv_right.at[col, b],
            device_id=(r, c, f), device_id_type=MESH,
        )

    def to_far(col, b):
        return pltpu.make_async_remote_copy(
            src_ref=right_at(right, col, seat, b), dst_ref=right_at(right_far, col, seat, b),
            send_sem=sent_far.at[0], recv_sem=recv_far.at[col, b],
            device_id=(r, c, mate), device_id_type=MESH,
        )

    def to_side(t, b):
        return pltpu.make_async_remote_copy(
            src_ref=block(mate, b), dst_ref=right_at(right_far, c, seat, b),
            send_sem=sent_far.at[0], recv_sem=recv_far.at[c, b],
            device_id=(t * group + seat, c, f), device_id_type=MESH,
        )

    def came_far(col, b):
        return pltpu.make_async_remote_copy(
            src_ref=block(f, b), dst_ref=right_at(right_far, col, seat, b),
            send_sem=sent_far.at[0], recv_sem=recv_far.at[col, b],
            device_id=(r, c, f), device_id_type=MESH,
        )

    def pairing(ref, send, recv):
        def to_pair(col, b, other):
            return pltpu.make_async_remote_copy(
                src_ref=right_at(ref, col, seat, b), dst_ref=right_at(ref, col, seat, b),
                send_sem=send.at[0], recv_sem=recv.at[seat],
                device_id=(owner * group + other, c, f), device_id_type=MESH,
            )

        def came_pair(other, blocks):
            theirs = ref.at[pl.ds(other * rows, blocks * unit)]
            return pltpu.make_async_remote_copy(
                src_ref=theirs, dst_ref=theirs, send_sem=send.at[0], recv_sem=recv.at[other],
                device_id=(r, c, f), device_id_type=MESH,
            )

        return to_pair, came_pair

    to_pair, came_pair = pairing(right, sent_pair, recv_pair)
    to_far_pair, came_far_pair = pairing(right_far, sent_far_pair, recv_far_pair)

    def crossing(out, into, send, recv):
        def to_col(col, i):
            return pltpu.make_async_remote_copy(
                src_ref=out.at[col, chunk(i)], dst_ref=into.at[c, chunk(i)],
                send_sem=send.at[0], recv_sem=recv.at[lax.rem(c - col + n_col, n_col) - 1, i],
                device_id=(r, col, f), device_id_type=MESH,
            )

        def came_col(col, i):
            return pltpu.make_async_remote_copy(
                src_ref=out.at[col, chunk(i)], dst_ref=into.at[col, chunk(i)],
                send_sem=send.at[0], recv_sem=recv.at[lax.rem(col - c + n_col, n_col) - 1, i],
                device_id=(r, col, f), device_id_type=MESH,
            )

        return to_col, came_col

    to_col, came_col = crossing(part_out, part_in, sent_part, recv_part)
    to_help, came_help = crossing(help_out, help_in, sent_help, recv_help)

    def to_done(i):
        return pltpu.make_async_remote_copy(
            src_ref=helped.at[chunk(i)], dst_ref=helped.at[chunk(i)],
            send_sem=sent_done.at[0], recv_sem=recv_done.at[i],
            device_id=(r, c, mate), device_id_type=MESH,
        )

    def skips(place, far):
        return (far >= place * parts) & (far < (place + 1) * parts)

    def to_owner(col, i):
        return pltpu.make_async_remote_copy(
            src_ref=help_out.at[col, chunk(i)], dst_ref=help_in.at[c, chunk(i)],
            send_sem=sent_owner.at[0], recv_sem=recv_done.at[i],
            device_id=(r, col, mate), device_id_type=MESH,
        )

    def came_owner(i):
        all_cols = help_in.at[pl.ds(0, n_col), chunk(i)]
        return pltpu.make_async_remote_copy(
            src_ref=all_cols, dst_ref=all_cols, send_sem=sent_owner.at[0], recv_sem=recv_done.at[i],
            device_id=(r, c, f), device_id_type=MESH,
        )

    def served(place, b):
        return place * parts + b != mate

    def to_serve(b):
        return seat * parts + b != f

    def send_own(i, now_down, now_up):
        @pl.when(sends_down(i) & now_down)
        def _():
            along(f, i, False).start()

        @pl.when(sends_up(i) & now_up)
        def _():
            along(f, i, True).start()

    low, high = f == 1, f == n_fib - 2
    inner = jnp.logical_not(outer)
    direct_down = outer | jnp.logical_not(high)
    direct_up = outer | jnp.logical_not(low)

    @pl.loop(0, CHUNKS)
    def _(i):
        send_own(i, direct_down | (i < AHEAD), direct_up | (i < AHEAD))

    for b in range(parts):
        for t in range(n_row // group):
            @pl.when(jnp.logical_not(mine & (owner == t)))
            def _():
                to_right(t, b).start()

    @pl.when(mine)
    def _():
        for b in range(parts):
            spot = right_at(right, c, seat, b)
            spot[...] = left[f, b * unit:(b + 1) * unit]

    def pass_up(d, i):
        @pl.when((f - d >= 0) & gets_up(i))
        def _():
            along(f - d, i, True).wait_recv()

            @pl.when(sends_up(i))
            def _():
                along(f - d, i, True).start()

    def pass_down(d, i):
        @pl.when((f + d < n_fib) & gets_down(i))
        def _():
            along(f + d, i, False).wait_recv()

            @pl.when(sends_down(i))
            def _():
                along(f + d, i, False).start()

    def feed(i):
        @pl.when(low)
        def _():
            pass_up(1, i)

        @pl.when(high)
        def _():
            pass_down(1, i)

        @pl.when(i + AHEAD < CHUNKS)
        def _():
            send_own(i + AHEAD, high, low)

    def near(i):
        @pl.when(jnp.logical_not(low))
        def _():
            pass_up(1, i)

        @pl.when(jnp.logical_not(high))
        def _():
            pass_down(1, i)

    def far(i):
        for d in range(2, n_fib - 1):
            pass_up(d, i)
            pass_down(d, i)

    def side(b):
        @pl.when(helper & mine & served(seat, b))
        def _():
            for t in range(n_row // group):
                @pl.when(owner != t)
                def _():
                    to_side(t, b).start()

            spot = right_at(right_far, c, seat, b)
            spot[...] = left[mate, b * unit:(b + 1) * unit]

    def gather(b):
        for col in range(n_col):
            @pl.when(jnp.logical_not(mine & (c == col)))
            def _():
                came_right(col, b).wait_recv()

            if helps:
                @pl.when(outer & (c != col) & to_serve(b))
                def _():
                    to_far(col, b).start()

            for other in range(group):
                @pl.when(seat != other)
                def _():
                    to_pair(col, b, other).start()

    half = CHUNKS // 2

    def approach(first, last):
        @pl.when(inner)
        def _():
            @pl.loop(first, last)
            def _(p):
                feed(2 * p)
                near(p)
                feed(2 * p + 1)

                @pl.when(p > 1)
                def _():
                    far(p - 2)

    for b in range(parts):
        approach(half * b // parts, half * (b + 1) // parts)
        if helps:
            side(b)
        if b < parts - 1:
            gather(b)

    @pl.when(inner)
    def _():
        near(half)

    gather(parts - 1)

    for other in range(group):
        @pl.when(seat != other)
        def _():
            came_pair(other, parts).wait_recv()

    def products(ref, part, first, count):
        return jnp.dot(
            jnp.concatenate([left[first + k, part, :] for k in range(count)], axis=1),
            ref[pl.ds(first * unit if isinstance(first, int) else pl.multiple_of(first * unit, unit), count * unit), :],
            preferred_element_type=jnp.float32,
        )

    def store(total, ours, part, out):
        kept_total = total[:, :unit]
        for col in range(n_col):
            piece = total[:, col * unit:(col + 1) * unit]
            out[col, part, :] = piece.astype(jnp.bfloat16)
            if col:
                kept_total = jnp.where(c == col, piece, kept_total)
        ours[part, :] = kept_total

    def col_at(shift):
        return lax.rem(c + shift, n_col)

    folded[...] = jnp.zeros((8, unit), jnp.float32)

    def combine(i, h=None):
        part = chunk(i)
        expanded = own[part, :]
        for shift in range(1, n_col):
            came_col(col_at(shift), i).wait_recv()
            expanded += part_in[col_at(shift), part, :].astype(jnp.float32)
        if h is not None and h >= lead:
            came_owner(h).wait_recv()
            for col in range(n_col):
                expanded += help_in[col, pl.ds(h * step, step), :].astype(jnp.float32)
        elif h is not None:
            to_done(h).wait_recv()
            expanded += helped[pl.ds(h * step, step), :].astype(jnp.float32)
        squared = expanded * expanded
        own[part, :] = squared
        folded[...] += jnp.sum(squared.reshape(step // 8, 8, unit), axis=0)

    def fetch():
        for b in range(parts):
            @pl.when(served(seat, b))
            def _():
                for col in range(n_col):
                    @pl.when(jnp.logical_not(mine & (c == col)))
                    def _():
                        came_far(col, b).wait_recv()

                    for other in range(group):
                        @pl.when(seat != other)
                        def _():
                            to_far_pair(col, b, other).start()

    def answer():
        for other in range(group):
            for skipped in range(2):
                @pl.when((seat != other) & (skips(other, mate) == bool(skipped)))
                def _():
                    came_far_pair(other, parts - skipped).wait_recv()

        if lead:
            reckon(0, lead)

    def reckon(h, count):
        part = pl.ds(lent_at(h) * step, count * step)
        total = products(right_far, part, jnp.where(mate == 0, 1, 0), n_fib - 1)
        store(total, help_own, pl.ds(h * step, count * step), help_out)
        for i in range(h, h + count):
            for shift in range(n_col):
                if h >= lead:
                    to_owner(col_at(shift), i).start()
                elif shift:
                    to_help(col_at(shift), i).start()

    if helps:
        @pl.when(outer)
        def _():
            for h in range(helps):
                i = lent_at(h)
                part = pl.ds(i * step, step)
                store(products(right, part, f, 1), own, part, part_out)
                for shift in range(1, n_col):
                    to_col(col_at(shift), i).start()

    def advance(i):
        odd = lax.rem(i, 2) == 1

        @pl.when(i == 0)
        def _():
            near(half + 1)

        @pl.when((i < CHUNKS - 5) & jnp.logical_not(odd))
        def _():
            far(half - 2 + i // 2)

        @pl.when((i <= CHUNKS - 5) & odd)
        def _():
            near(half + 2 + i // 2)

        @pl.when((i >= CHUNKS - 5) & (i < CHUNKS - 1))
        def _():
            far(i + 1)

    @pl.loop(0, CHUNKS)
    def _(i):
        part = chunk(i)
        full = kept(i) | jnp.logical_not(outer)

        @pl.when(outer & full)
        def _():
            for d in range(1, n_fib):
                pass_up(d, i)
                pass_down(d, i)

        if helps:
            @pl.when(helper & (i == ANSWER))
            def _():
                answer()

        @pl.when(inner & (i >= ANSWER))
        def _():
            advance(i)

        for h in range(lead, helps):
            @pl.when(helper & (i == max(lent_at(h) - 1, ANSWER)))
            def _():
                reckon(h, 1)

        @pl.when(full)
        def _():
            store(products(right, part, 0, n_fib), own, part, part_out)
            for shift in range(1, n_col):
                to_col(col_at(shift), i).start()

        if helps:
            @pl.when(helper & (i == FETCH))
            def _():
                fetch()

        @pl.when(inner & (i < ANSWER))
        def _():
            advance(i)

        @pl.when((i >= LAG) & (kept(i - LAG) | jnp.logical_not(outer)))
        def _():
            combine(i - LAG)

    def reply(h):
        @pl.when(helper)
        def _():
            part = pl.ds(h * step, step)
            total = help_own[part, :]
            for shift in range(1, n_col):
                came_help(col_at(shift), h).wait_recv()
                total += help_in[col_at(shift), part, :].astype(jnp.float32)
            helped[part, :] = total.astype(jnp.bfloat16)
            to_done(h).start()

    for h in range(lead):
        reply(h)

    @pl.loop(CHUNKS - LAG, CHUNKS)
    def _(i):
        @pl.when(kept(i) | inner)
        def _():
            combine(i)

    if helps:
        @pl.when(outer)
        def _():
            for h in range(helps):
                combine(lent_at(h), h)

    def to_row(shift):
        return pltpu.make_async_remote_copy(
            src_ref=sums.at[r], dst_ref=sums.at[r],
            send_sem=sent_sum.at[0], recv_sem=recv_sum.at[0],
            device_id=(lax.rem(r + shift, n_row), c, f), device_id_type=MESH,
        )

    def came_rows():
        return pltpu.make_async_remote_copy(
            src_ref=sums.at[pl.ds(0, n_row - 1)], dst_ref=sums.at[pl.ds(0, n_row - 1)],
            send_sem=sent_sum.at[0], recv_sem=recv_sum.at[0],
            device_id=(r, c, f), device_id_type=MESH,
        )

    sums[r] = jnp.sum(folded[...], axis=0, keepdims=True)
    for shift in range(1, n_row):
        to_row(shift).start()
    came_rows().wait_recv()
    total = sums[0]
    for other in range(1, n_row):
        total += sums[other]
    scale = total / (rows * n_row) + 1e-6
    inverse = 1.0 / scale
    for i in range(rows // tile):
        for j in range(unit // tile):
            across = slice(j * tile, (j + 1) * tile)
            factor_ref[i:i + 1, across] = inverse[:, across] * keep_ref[j, i].astype(jnp.float32)

    def left_behind(sem, ref):
        pltpu.make_async_remote_copy(
            src_ref=ref, dst_ref=ref, send_sem=sem, recv_sem=recv_sum.at[0],
            device_id=(r, c, f), device_id_type=MESH,
        ).wait_send()

    few = helps * step
    for at in range(n_fib):
        @pl.when(f == at)
        def _():
            if at < n_fib - 1:
                less = few if at == n_fib - 2 else 0
                left_behind(sent_left.at[1], left.at[pl.ds(0, at + 1), pl.ds(0, rows - less)])
            if at > 0:
                less = few if at == 1 else 0
                left_behind(sent_left.at[0], left.at[pl.ds(0, n_fib - at), pl.ds(0, rows - less)])

    for less in range(2):
        if n_col > less:
            @pl.when(mine == bool(less))
            def _():
                left_behind(sent_right.at[0], part_out.at[pl.ds(0, n_col - less)])

    if group > 1:
        left_behind(sent_pair.at[0], right.at[pl.ds(0, (group - 1) * rows)])
    if n_col > 1:
        left_behind(sent_part.at[0], part_out.at[pl.ds(0, n_col - 1)])
    if n_row > 1:
        left_behind(sent_sum.at[0], sums.at[pl.ds(0, n_row - 1)])

    if helps:
        for less in range(2):
            size = (parts - less) * unit
            across = pl.ds(0, (n_col - 1) * unit)
            if size and n_col > 1:
                @pl.when(skips(seat, jnp.where(outer, f, mate)) == bool(less))
                def _():
                    @pl.when(outer | (helper & mine))
                    def _():
                        left_behind(sent_far.at[0], right.at[pl.ds(0, size), across])

            if size and group > 1:
                @pl.when(helper & (skips(seat, mate) == bool(less)))
                def _():
                    left_behind(sent_far_pair.at[0], right.at[pl.ds(0, (group - 1) * size)])

        @pl.when(helper)
        def _():
            if lead:
                if n_col > 1:
                    left_behind(sent_help.at[0], help_out.at[pl.ds(0, n_col - 1), pl.ds(0, lead * step)])
                left_behind(sent_done.at[0], helped.at[pl.ds(0, lead * step)])
            if late:
                left_behind(sent_owner.at[0], help_out.at[pl.ds(0, n_col), pl.ds(lead * step, late * step)])


def prune(squared_ref, factor_ref, out_hbm, out_vmem, sem):
    tile = out_vmem.shape[0] // factor_ref.shape[0]
    copies = []
    for i in range(factor_ref.shape[0]):
        down = slice(i * tile, (i + 1) * tile)
        out_vmem[down] = squared_ref[down] * factor_ref[i:i + 1]
        copy = pltpu.make_async_copy(out_vmem.at[down], out_hbm.at[down], sem.at[i])
        copy.start()
        copies.append(copy)
    for copy in copies:
        copy.wait()


def solution(mesh):
    n_row, n_col, n_fib = (mesh.shape[name] for name in ("row", "col", "fiber"))
    group = n_row // n_col
    helps = HELP if n_fib > 3 else 0

    def local(values, tile_mask, keep_mask):
        rows, unit = values.shape
        dma = pltpu.SemaphoreType.DMA
        parts = rows // unit
        few = rows // CHUNKS * HELP
        squared, factor = pl.pallas_call(
            functools.partial(kernel, n_row, n_col, n_fib, helps),
            out_shape=(
                pltpu.VMEM((rows, unit), jnp.float32),
                pltpu.VMEM((tile_mask.shape[0], unit), jnp.float32),
            ),
            in_specs=[
                pl.BlockSpec(memory_space=pltpu.HBM),
                pl.BlockSpec(memory_space=pltpu.HBM),
                pl.BlockSpec(memory_space=pltpu.HBM),
            ],
            out_specs=(
                pl.BlockSpec(memory_space=pltpu.VMEM),
                pl.BlockSpec(memory_space=pltpu.VMEM),
            ),
            scratch_shapes=[
                pltpu.SMEM(tile_mask.shape[::-1], jnp.int32),
                pltpu.SMEM(keep_mask.shape[::-1], jnp.int32),
                pltpu.VMEM((rows, unit), jnp.float32),
                pltpu.VMEM((n_fib, rows, unit), jnp.bfloat16),
                pltpu.VMEM((group * rows, n_col * unit), jnp.bfloat16),
                pltpu.VMEM((n_col, rows, unit), jnp.bfloat16),
                pltpu.VMEM((n_col, rows, unit), jnp.bfloat16),
                pltpu.VMEM((8, unit), jnp.float32),
                pltpu.VMEM((n_row, 1, unit), jnp.float32),
                pltpu.VMEM((group * rows, n_col * unit), jnp.bfloat16),
                pltpu.VMEM((few, unit), jnp.float32),
                pltpu.VMEM((n_col, few, unit), jnp.bfloat16),
                pltpu.VMEM((n_col, few, unit), jnp.bfloat16),
                pltpu.VMEM((few, unit), jnp.bfloat16),
                dma((3,)),
                dma((2,)),
                dma((1,)),
                dma((1,)),
                dma((1,)),
                dma((1,)),
                dma((1,)),
                dma((1,)),
                dma((1,)),
                dma((1,)),
                dma((1,)),
                dma((n_fib - 1, CHUNKS)),
                dma((n_col, parts)),
                dma((group,)),
                dma((n_col - 1, CHUNKS)),
                dma((1,)),
                dma((n_col, parts)),
                dma((group,)),
                dma((n_col - 1, HELP)),
                dma((HELP,)),
            ],
            compiler_params=pltpu.CompilerParams(
                collective_id=0, has_side_effects=True, vmem_limit_bytes=VMEM_LIMIT
            ),
            name="expand",
        )(tile_mask.T, keep_mask.T, values)
        return pl.pallas_call(
            prune,
            out_shape=jax.ShapeDtypeStruct((rows, unit), jnp.float32),
            in_specs=[
                pl.BlockSpec(memory_space=pltpu.VMEM),
                pl.BlockSpec(memory_space=pltpu.VMEM),
            ],
            out_specs=pl.BlockSpec(memory_space=pl.ANY),
            scratch_shapes=[
                pltpu.VMEM((rows, unit), jnp.float32),
                dma((keep_mask.shape[0],)),
            ],
            compiler_params=pltpu.CompilerParams(vmem_limit_bytes=8 * 1024 * 1024),
            name="prune",
        )(squared, factor)

    spec = P("row", ("col", "fiber"))
    return jax.shard_map(
        local, mesh=mesh, in_specs=(spec, spec, spec), out_specs=spec, check_vma=False
    )
```

```python
import functools

import jax
import jax.numpy as jnp
from jax import lax
from jax.experimental import pallas as pl
from jax.experimental.pallas import tpu as pltpu
from jax.sharding import PartitionSpec as P

MESH = pl.DeviceIdType.MESH
CHUNKS = 12
HELP = 3
TRAIL = 1
AHEAD = 4
FIRST_FETCH = 4
FETCH = 7
ANSWER = 9
LAG = 5
VMEM_LIMIT = 62 * 1024 * 1024


def kernel(
    n_row, n_col, n_fib, helps, tile_hbm, keep_hbm, values_hbm, own, factor_ref,
    tile_ref, keep_ref, values_ref, left, right, part_out, part_in, folded, sums, partial,
    right_far, help_own, help_out, help_in, helped, load_sem,
    sent_left, sent_right, sent_pair, sent_part, sent_sum, sent_far, sent_helper,
    recv_left, recv_right, recv_pair, recv_part, recv_sum,
    recv_far, recv_far_pair, recv_help, recv_done,
):
    r, c, f = lax.axis_index("row"), lax.axis_index("col"), lax.axis_index("fiber")
    rows, unit = values_ref.shape
    tile = unit // tile_ref.shape[0]
    step = rows // CHUNKS
    parts = rows // unit
    group = n_row // n_col
    owner, seat = r // group, lax.rem(r, group)

    load = pltpu.make_async_copy(values_hbm, values_ref, load_sem.at[0])
    load.start()
    load_tile = pltpu.make_async_copy(tile_hbm, tile_ref, load_sem.at[1])
    load_tile.start()
    load_keep = pltpu.make_async_copy(keep_hbm, keep_ref, load_sem.at[2])
    load_keep.start()

    barrier = pltpu.get_barrier_semaphore()
    for dr in range(n_row):
        for dc in range(n_col):
            if dr or dc:
                pl.semaphore_signal(
                    barrier, inc=1, device_id_type=MESH,
                    device_id=(lax.rem(r + dr, n_row), lax.rem(c + dc, n_col), f),
                )

    has_down, has_up = f > 0, f < n_fib - 1
    outer = jnp.logical_not(has_down & has_up)
    helper = (f == 1) | (f == n_fib - 2)
    mate = jnp.where(outer, jnp.where(has_down, f - 1, 1), jnp.where(f == 1, 0, n_fib - 1))
    mine = owner == c

    @pl.when(has_down)
    def _():
        pl.semaphore_signal(barrier, inc=1, device_id=(r, c, f - 1), device_id_type=MESH)

    @pl.when(has_up)
    def _():
        pl.semaphore_signal(barrier, inc=1, device_id=(r, c, f + 1), device_id_type=MESH)

    load_tile.wait()
    load_keep.wait()
    load.wait()

    for i in range(rows // tile):
        for j in range(unit // tile):
            at = (pl.ds(i * tile, tile), pl.ds(j * tile, tile))
            masked = values_ref[at] * tile_ref[j, i].astype(jnp.float32)
            left[f, i * tile:(i + 1) * tile, j * tile:(j + 1) * tile] = masked.astype(jnp.bfloat16)

    neighbours = has_down.astype(jnp.int32) + has_up.astype(jnp.int32)
    pl.semaphore_wait(barrier, n_row * n_col - 1 + neighbours)

    def chunk(i):
        return pl.ds(i * step if isinstance(i, int) else pl.multiple_of(i * step, step), step)

    def along(source, i, up):
        part = left.at[source, chunk(i)]
        return pltpu.make_async_remote_copy(
            src_ref=part, dst_ref=part,
            send_sem=sent_left.at[int(up)], recv_sem=recv_left.at[source if up else source - 1, i],
            device_id=(r, c, f + 1 if up else f - 1), device_id_type=MESH,
        )

    late = min(helps, TRAIL)
    lead = helps - late

    def kept(i):
        return (i >= lead) & (i < CHUNKS - late)

    def lent_at(h):
        return h if h < lead else h - helps + CHUNKS

    def sends_up(i):
        return has_up & (kept(i) | (f + 1 < n_fib - 1))

    def sends_down(i):
        return has_down & (kept(i) | (f - 1 > 0))

    def gets_up(i):
        return kept(i) | has_up

    def gets_down(i):
        return kept(i) | has_down

    def right_at(ref, col, place, b):
        return ref.at[
            pl.ds(pl.multiple_of(place * rows + b * unit, unit), unit),
            pl.ds(pl.multiple_of(col * unit, unit), unit),
        ]

    def block(source, b):
        return left.at[source, pl.ds(b * unit, unit)]

    def to_right(t, b):
        return pltpu.make_async_remote_copy(
            src_ref=block(f, b), dst_ref=right_at(right, c, seat, b),
            send_sem=sent_right.at[0], recv_sem=recv_right.at[b],
            device_id=(t * group + seat, owner, f), device_id_type=MESH,
        )

    def arrived(ref, recv, b):
        for less in range(2):
            if n_col > less:
                @pl.when(mine == bool(less))
                def _():
                    theirs = ref.at[pl.ds(0, unit), pl.ds(0, (n_col - less) * unit)]
                    pltpu.make_async_remote_copy(
                        src_ref=theirs, dst_ref=theirs, send_sem=sent_right.at[0],
                        recv_sem=recv.at[b], device_id=(r, c, f), device_id_type=MESH,
                    ).wait_recv()

    def to_far(col, b):
        return pltpu.make_async_remote_copy(
            src_ref=right_at(right, col, seat, b), dst_ref=right_at(right_far, col, seat, b),
            send_sem=sent_far.at[0], recv_sem=recv_far.at[b],
            device_id=(r, c, mate), device_id_type=MESH,
        )

    def to_side(t, b):
        return pltpu.make_async_remote_copy(
            src_ref=block(mate, b), dst_ref=right_at(right_far, c, seat, b),
            send_sem=sent_far.at[0], recv_sem=recv_far.at[b],
            device_id=(t * group + seat, c, f), device_id_type=MESH,
        )

    def pairing(ref, send, recv):
        def to_pair(col, b, other):
            return pltpu.make_async_remote_copy(
                src_ref=right_at(ref, col, seat, b), dst_ref=right_at(ref, col, seat, b),
                send_sem=send.at[0], recv_sem=recv.at[seat],
                device_id=(owner * group + other, c, f), device_id_type=MESH,
            )

        def came_pair(other, blocks):
            theirs = ref.at[pl.ds(other * rows, blocks * unit)]
            return pltpu.make_async_remote_copy(
                src_ref=theirs, dst_ref=theirs, send_sem=send.at[0], recv_sem=recv.at[other],
                device_id=(r, c, f), device_id_type=MESH,
            )

        return to_pair, came_pair

    to_pair, came_pair = pairing(right, sent_pair, recv_pair)
    to_far_pair, came_far_pair = pairing(right_far, sent_helper, recv_far_pair)

    def crossing(out, into, send, recv, share):
        def to_col(col, i):
            return pltpu.make_async_remote_copy(
                src_ref=out.at[col, chunk(i)], dst_ref=into.at[c, chunk(i)],
                send_sem=send.at[0],
                recv_sem=recv.at[lax.rem(c - col + n_col, n_col) - 1, i // share],
                device_id=(r, col, f), device_id_type=MESH,
            )

        def came_col(col, i):
            both = into.at[col, pl.ds(i * step, share * step)]
            return pltpu.make_async_remote_copy(
                src_ref=both, dst_ref=both, send_sem=send.at[0],
                recv_sem=recv.at[lax.rem(col - c + n_col, n_col) - 1, i // share],
                device_id=(r, col, f), device_id_type=MESH,
            )

        return to_col, came_col

    to_col, came_col = crossing(part_out, part_in, sent_part, recv_part, 2)
    to_help, came_help = crossing(help_out, help_in, sent_helper, recv_help, 1)

    def to_done(i):
        return pltpu.make_async_remote_copy(
            src_ref=helped.at[chunk(i)], dst_ref=helped.at[chunk(i)],
            send_sem=sent_helper.at[0], recv_sem=recv_done.at[i],
            device_id=(r, c, mate), device_id_type=MESH,
        )

    def skips(place, far):
        return (far >= place * parts) & (far < (place + 1) * parts)

    def to_owner(col, i):
        return pltpu.make_async_remote_copy(
            src_ref=help_out.at[col, chunk(i)], dst_ref=help_in.at[c, chunk(i)],
            send_sem=sent_helper.at[0], recv_sem=recv_done.at[i],
            device_id=(r, col, mate), device_id_type=MESH,
        )

    def came_owner(i):
        all_cols = help_in.at[pl.ds(0, n_col), chunk(i)]
        return pltpu.make_async_remote_copy(
            src_ref=all_cols, dst_ref=all_cols, send_sem=sent_helper.at[0], recv_sem=recv_done.at[i],
            device_id=(r, c, f), device_id_type=MESH,
        )

    def served(place, b):
        return place * parts + b != mate

    def to_serve(b):
        return seat * parts + b != f

    def send_own(i, now_down, now_up):
        @pl.when(sends_down(i) & now_down)
        def _():
            along(f, i, False).start()

        @pl.when(sends_up(i) & now_up)
        def _():
            along(f, i, True).start()

    low, high = f == 1, f == n_fib - 2
    inner = jnp.logical_not(outer)
    direct_down = outer | jnp.logical_not(high)
    direct_up = outer | jnp.logical_not(low)

    @pl.loop(0, CHUNKS)
    def _(i):
        send_own(i, direct_down | (i < AHEAD), direct_up | (i < AHEAD))

    for b in range(parts):
        for t in range(n_row // group):
            @pl.when(jnp.logical_not(mine & (owner == t)))
            def _():
                to_right(t, b).start()

    @pl.when(mine)
    def _():
        for b in range(parts):
            spot = right_at(right, c, seat, b)
            spot[...] = left[f, b * unit:(b + 1) * unit]

    def pass_up(d, i):
        @pl.when((f - d >= 0) & gets_up(i))
        def _():
            along(f - d, i, True).wait_recv()

            @pl.when(sends_up(i))
            def _():
                along(f - d, i, True).start()

    def pass_down(d, i):
        @pl.when((f + d < n_fib) & gets_down(i))
        def _():
            along(f + d, i, False).wait_recv()

            @pl.when(sends_down(i))
            def _():
                along(f + d, i, False).start()

    def feed(i):
        @pl.when(low)
        def _():
            pass_up(1, i)

        @pl.when(high)
        def _():
            pass_down(1, i)

        @pl.when(i + AHEAD < CHUNKS)
        def _():
            send_own(i + AHEAD, high, low)

    def near(i):
        @pl.when(jnp.logical_not(low))
        def _():
            pass_up(1, i)

        @pl.when(jnp.logical_not(high))
        def _():
            pass_down(1, i)

    def far(i):
        for d in range(2, n_fib - 1):
            pass_up(d, i)
            pass_down(d, i)

    def side(b):
        @pl.when(helper & mine & served(seat, b))
        def _():
            for t in range(n_row // group):
                @pl.when(owner != t)
                def _():
                    to_side(t, b).start()

            spot = right_at(right_far, c, seat, b)
            spot[...] = left[mate, b * unit:(b + 1) * unit]

    def gather(b):
        arrived(right, recv_right, b)
        for col in range(n_col):
            if helps:
                @pl.when(outer & (c != col) & to_serve(b))
                def _():
                    to_far(col, b).start()

            for other in range(group):
                @pl.when(seat != other)
                def _():
                    to_pair(col, b, other).start()

    half = CHUNKS // 2

    def approach(first, last):
        @pl.when(inner)
        def _():
            @pl.loop(first, last)
            def _(p):
                feed(2 * p)
                near(p)
                feed(2 * p + 1)

                @pl.when(p > 1)
                def _():
                    far(p - 2)

    for b in range(parts):
        approach(half * b // parts, half * (b + 1) // parts)
        if helps:
            side(b)
        if b < parts - 1:
            gather(b)

    @pl.when(inner)
    def _():
        near(half)

    gather(parts - 1)

    for other in range(group):
        @pl.when(seat != other)
        def _():
            came_pair(other, parts).wait_recv()

    def products(ref, part, first, count):
        return jnp.dot(
            jnp.concatenate([left[first + k, part, :] for k in range(count)], axis=1),
            ref[pl.ds(first * unit if isinstance(first, int) else pl.multiple_of(first * unit, unit), count * unit), :],
            preferred_element_type=jnp.float32,
        )

    def store(total, ours, part, out):
        kept_total = total[:, :unit]
        for col in range(n_col):
            piece = total[:, col * unit:(col + 1) * unit]
            out[col, part, :] = piece.astype(jnp.bfloat16)
            if col:
                kept_total = jnp.where(c == col, piece, kept_total)
        ours[part, :] = kept_total

    def col_at(shift):
        return lax.rem(c + shift, n_col)

    folded[...] = jnp.zeros((8, unit), jnp.float32)

    def combine(i, h=None):
        part = chunk(i)
        expanded = own[part, :]
        def await_two():
            for shift in range(1, n_col):
                came_col(col_at(shift), i).wait_recv()

        if not isinstance(i, int):
            pl.when(lax.rem(i, 2) == 0)(await_two)
        elif i % 2 == 0:
            await_two()

        for shift in range(1, n_col):
            expanded += part_in[col_at(shift), part, :].astype(jnp.float32)
        if h is not None and h >= lead:
            came_owner(h).wait_recv()
            for col in range(n_col):
                expanded += help_in[col, pl.ds(h * step, step), :].astype(jnp.float32)
        elif h is not None:
            to_done(h).wait_recv()
            expanded += helped[pl.ds(h * step, step), :].astype(jnp.float32)
        squared = expanded * expanded
        own[part, :] = squared
        folded[...] += jnp.sum(squared.reshape(step // 8, 8, unit), axis=0)

    def fetch(b):
        @pl.when(served(seat, b))
        def _():
            arrived(right_far, recv_far, b)
            for col in range(n_col):
                for other in range(group):
                    @pl.when(seat != other)
                    def _():
                        to_far_pair(col, b, other).start()

    def answer():
        for other in range(group):
            for skipped in range(2):
                @pl.when((seat != other) & (skips(other, mate) == bool(skipped)))
                def _():
                    came_far_pair(other, parts - skipped).wait_recv()

        if lead:
            reckon(0, lead)

    def reckon(h, count):
        part = pl.ds(lent_at(h) * step, count * step)
        total = products(right_far, part, jnp.where(mate == 0, 1, 0), n_fib - 1)
        store(total, help_own, pl.ds(h * step, count * step), help_out)
        for i in range(h, h + count):
            for shift in range(n_col):
                if h >= lead:
                    to_owner(col_at(shift), i).start()
                elif shift:
                    to_help(col_at(shift), i).start()

    if helps:
        @pl.when(outer)
        def _():
            for h in range(helps):
                i = lent_at(h)
                part = pl.ds(i * step, step)
                store(products(right, part, f, 1), own, part, part_out)
                for shift in range(1, n_col):
                    to_col(col_at(shift), i).start()

    def advance(i):
        odd = lax.rem(i, 2) == 1

        @pl.when(i == 0)
        def _():
            near(half + 1)

        @pl.when((i < CHUNKS - 5) & jnp.logical_not(odd))
        def _():
            far(half - 2 + i // 2)

        @pl.when((i <= CHUNKS - 5) & odd)
        def _():
            near(half + 2 + i // 2)

        @pl.when((i >= CHUNKS - 5) & (i < CHUNKS - 1))
        def _():
            far(i + 1)

    @pl.loop(0, CHUNKS)
    def _(i):
        part = chunk(i)
        full = kept(i) | jnp.logical_not(outer)

        @pl.when(outer & full)
        def _():
            for d in range(1, n_fib - 1):
                pass_up(d, i)
                pass_down(d, i)
            partial[...] = products(right, part, jnp.where(has_down, 1, 0), n_fib - 1)
            pass_up(n_fib - 1, i)
            pass_down(n_fib - 1, i)
            total = partial[...] + products(right, part, jnp.where(has_down, 0, n_fib - 1), 1)
            store(total, own, part, part_out)

        if helps:
            @pl.when(helper & (i == ANSWER))
            def _():
                answer()

        @pl.when(inner & (i >= ANSWER))
        def _():
            advance(i)

        for h in range(lead, helps):
            @pl.when(helper & (i == max(lent_at(h) - 1, ANSWER)))
            def _():
                reckon(h, 1)

        @pl.when(inner)
        def _():
            store(products(right, part, 0, n_fib), own, part, part_out)

        @pl.when(full)
        def _():
            for shift in range(1, n_col):
                to_col(col_at(shift), i).start()

        if helps:
            for b in range(parts):
                @pl.when(helper & (i == (FIRST_FETCH if b < parts - 1 else FETCH)))
                def _():
                    fetch(b)

        @pl.when(inner & (i < ANSWER))
        def _():
            advance(i)

        @pl.when((i >= LAG) & (kept(i - LAG) | jnp.logical_not(outer)))
        def _():
            combine(i - LAG)

    def reply(h):
        @pl.when(helper)
        def _():
            part = pl.ds(h * step, step)
            total = help_own[part, :]
            for shift in range(1, n_col):
                came_help(col_at(shift), h).wait_recv()
                total += help_in[col_at(shift), part, :].astype(jnp.float32)
            helped[part, :] = total.astype(jnp.bfloat16)
            to_done(h).start()

    for h in range(lead):
        reply(h)

    @pl.loop(CHUNKS - LAG, CHUNKS)
    def _(i):
        @pl.when(kept(i) | inner)
        def _():
            combine(i)

    if helps:
        @pl.when(outer)
        def _():
            for h in range(helps):
                combine(lent_at(h), h)

    def to_row(shift):
        return pltpu.make_async_remote_copy(
            src_ref=sums.at[r], dst_ref=sums.at[r],
            send_sem=sent_sum.at[0], recv_sem=recv_sum.at[0],
            device_id=(lax.rem(r + shift, n_row), c, f), device_id_type=MESH,
        )

    def came_rows():
        return pltpu.make_async_remote_copy(
            src_ref=sums.at[pl.ds(0, n_row - 1)], dst_ref=sums.at[pl.ds(0, n_row - 1)],
            send_sem=sent_sum.at[0], recv_sem=recv_sum.at[0],
            device_id=(r, c, f), device_id_type=MESH,
        )

    sums[r] = jnp.sum(folded[...], axis=0, keepdims=True)
    for shift in range(1, n_row):
        to_row(shift).start()
    came_rows().wait_recv()
    total = sums[0]
    for other in range(1, n_row):
        total += sums[other]
    scale = total / (rows * n_row) + 1e-6
    inverse = 1.0 / scale
    for i in range(rows // tile):
        for j in range(unit // tile):
            across = slice(j * tile, (j + 1) * tile)
            factor_ref[i:i + 1, across] = inverse[:, across] * keep_ref[j, i].astype(jnp.float32)

    def left_behind(sem, ref):
        pltpu.make_async_remote_copy(
            src_ref=ref, dst_ref=ref, send_sem=sem, recv_sem=recv_sum.at[0],
            device_id=(r, c, f), device_id_type=MESH,
        ).wait_send()

    few = helps * step
    for at in range(n_fib):
        @pl.when(f == at)
        def _():
            if at < n_fib - 1:
                less = few if at == n_fib - 2 else 0
                left_behind(sent_left.at[1], left.at[pl.ds(0, at + 1), pl.ds(0, rows - less)])
            if at > 0:
                less = few if at == 1 else 0
                left_behind(sent_left.at[0], left.at[pl.ds(0, n_fib - at), pl.ds(0, rows - less)])

    for less in range(2):
        if n_col > less:
            @pl.when(mine == bool(less))
            def _():
                left_behind(sent_right.at[0], part_out.at[pl.ds(0, n_col - less)])

    if group > 1:
        left_behind(sent_pair.at[0], right.at[pl.ds(0, (group - 1) * rows)])
    if n_col > 1:
        left_behind(sent_part.at[0], part_out.at[pl.ds(0, n_col - 1)])
    if n_row > 1:
        left_behind(sent_sum.at[0], sums.at[pl.ds(0, n_row - 1)])

    if helps:
        for less in range(2):
            size = (parts - less) * unit
            across = pl.ds(0, (n_col - 1) * unit)
            if size and n_col > 1:
                @pl.when(skips(seat, jnp.where(outer, f, mate)) == bool(less))
                def _():
                    @pl.when(outer | (helper & mine))
                    def _():
                        left_behind(sent_far.at[0], right.at[pl.ds(0, size), across])

            @pl.when(helper & (skips(seat, mate) == bool(less)))
            def _():
                left_behind(sent_helper.at[0], right_far.at[pl.ds(0, (group - 1) * size + few)])


def prune(squared_ref, factor_ref, out_hbm, out_vmem, sem):
    tile = out_vmem.shape[0] // factor_ref.shape[0]
    copies = []
    for i in range(factor_ref.shape[0]):
        down = slice(i * tile, (i + 1) * tile)
        out_vmem[down] = squared_ref[down] * factor_ref[i:i + 1]
        copy = pltpu.make_async_copy(out_vmem.at[down], out_hbm.at[down], sem.at[i])
        copy.start()
        copies.append(copy)
    for copy in copies:
        copy.wait()


def solution(mesh):
    n_row, n_col, n_fib = (mesh.shape[name] for name in ("row", "col", "fiber"))
    group = n_row // n_col
    helps = HELP if n_fib > 3 else 0

    def local(values, tile_mask, keep_mask):
        rows, unit = values.shape
        dma = pltpu.SemaphoreType.DMA
        parts = rows // unit
        few = rows // CHUNKS * HELP
        squared, factor = pl.pallas_call(
            functools.partial(kernel, n_row, n_col, n_fib, helps),
            out_shape=(
                pltpu.VMEM((rows, unit), jnp.float32),
                pltpu.VMEM((tile_mask.shape[0], unit), jnp.float32),
            ),
            in_specs=[
                pl.BlockSpec(memory_space=pltpu.HBM),
                pl.BlockSpec(memory_space=pltpu.HBM),
                pl.BlockSpec(memory_space=pltpu.HBM),
            ],
            out_specs=(
                pl.BlockSpec(memory_space=pltpu.VMEM),
                pl.BlockSpec(memory_space=pltpu.VMEM),
            ),
            scratch_shapes=[
                pltpu.SMEM(tile_mask.shape[::-1], jnp.int32),
                pltpu.SMEM(keep_mask.shape[::-1], jnp.int32),
                pltpu.VMEM((rows, unit), jnp.float32),
                pltpu.VMEM((n_fib, rows, unit), jnp.bfloat16),
                pltpu.VMEM((group * rows, n_col * unit), jnp.bfloat16),
                pltpu.VMEM((n_col, rows, unit), jnp.bfloat16),
                pltpu.VMEM((n_col, rows, unit), jnp.bfloat16),
                pltpu.VMEM((8, unit), jnp.float32),
                pltpu.VMEM((n_row, 1, unit), jnp.float32),
                pltpu.VMEM((rows // CHUNKS, n_col * unit), jnp.float32),
                pltpu.VMEM((group * rows, n_col * unit), jnp.bfloat16),
                pltpu.VMEM((few, unit), jnp.float32),
                pltpu.VMEM((n_col, few, unit), jnp.bfloat16),
                pltpu.VMEM((n_col, few, unit), jnp.bfloat16),
                pltpu.VMEM((few, unit), jnp.bfloat16),
                dma((3,)),
                dma((2,)),
                dma((1,)),
                dma((1,)),
                dma((1,)),
                dma((1,)),
                dma((1,)),
                dma((1,)),
                dma((n_fib - 1, CHUNKS)),
                dma((parts,)),
                dma((group,)),
                dma((n_col - 1, CHUNKS // 2)),
                dma((1,)),
                dma((parts,)),
                dma((group,)),
                dma((n_col - 1, max(HELP - TRAIL, 1))),
                dma((HELP,)),
            ],
            compiler_params=pltpu.CompilerParams(
                collective_id=0, has_side_effects=True, vmem_limit_bytes=VMEM_LIMIT
            ),
            name="expand",
        )(tile_mask.T, keep_mask.T, values)
        return pl.pallas_call(
            prune,
            out_shape=jax.ShapeDtypeStruct((rows, unit), jnp.float32),
            in_specs=[
                pl.BlockSpec(memory_space=pltpu.VMEM),
                pl.BlockSpec(memory_space=pltpu.VMEM),
            ],
            out_specs=pl.BlockSpec(memory_space=pl.ANY),
            scratch_shapes=[
                pltpu.VMEM((rows, unit), jnp.float32),
                dma((keep_mask.shape[0],)),
            ],
            compiler_params=pltpu.CompilerParams(vmem_limit_bytes=8 * 1024 * 1024),
            name="prune",
        )(squared, factor)

    spec = P("row", ("col", "fiber"))
    return jax.shard_map(
        local, mesh=mesh, in_specs=(spec, spec, spec), out_specs=spec, check_vma=False
    )
```

```python
import functools

import jax
import jax.numpy as jnp
from jax import lax
from jax.experimental import pallas as pl
from jax.experimental.pallas import tpu as pltpu
from jax.sharding import PartitionSpec as P

MESH = pl.DeviceIdType.MESH
CHUNKS = 12
HELP = 3
TRAIL = 1
AHEAD = 4
FIRST_FETCH = 4
FETCH = 7
ANSWER = 9
LAG = 5
SLICES = 4
VMEM_LIMIT = 62 * 1024 * 1024


def kernel(
    n_row, n_col, n_fib, helps, tile_hbm, keep_hbm, values_hbm, own, factor_ref,
    tile_ref, keep_ref, values_ref, left, right, part_out, part_in, folded, sums, partial,
    right_far, help_own, help_out, help_in, helped, load_sem,
    sent_left, sent_right, sent_pair, sent_part, sent_sum, sent_far, sent_helper,
    recv_left, recv_right, recv_pair, recv_part, recv_sum,
    recv_far, recv_far_pair, recv_help, recv_done,
):
    r, c, f = lax.axis_index("row"), lax.axis_index("col"), lax.axis_index("fiber")
    rows, unit = values_ref.shape
    tile = unit // tile_ref.shape[0]
    step = rows // CHUNKS
    parts = rows // unit
    group = n_row // n_col
    owner, seat = r // group, lax.rem(r, group)

    load = pltpu.make_async_copy(values_hbm, values_ref, load_sem.at[0])
    load.start()
    load_tile = pltpu.make_async_copy(tile_hbm, tile_ref, load_sem.at[1])
    load_tile.start()
    load_keep = pltpu.make_async_copy(keep_hbm, keep_ref, load_sem.at[2])
    load_keep.start()

    barrier = pltpu.get_barrier_semaphore()
    for dr in range(n_row):
        for dc in range(n_col):
            if dr or dc:
                pl.semaphore_signal(
                    barrier, inc=1, device_id_type=MESH,
                    device_id=(lax.rem(r + dr, n_row), lax.rem(c + dc, n_col), f),
                )

    has_down, has_up = f > 0, f < n_fib - 1
    outer = jnp.logical_not(has_down & has_up)
    helper = (f == 1) | (f == n_fib - 2)
    mate = jnp.where(outer, jnp.where(has_down, f - 1, 1), jnp.where(f == 1, 0, n_fib - 1))
    mine = owner == c

    @pl.when(has_down)
    def _():
        pl.semaphore_signal(barrier, inc=1, device_id=(r, c, f - 1), device_id_type=MESH)

    @pl.when(has_up)
    def _():
        pl.semaphore_signal(barrier, inc=1, device_id=(r, c, f + 1), device_id_type=MESH)

    load_tile.wait()
    load_keep.wait()
    load.wait()

    for i in range(rows // tile):
        for j in range(unit // tile):
            at = (pl.ds(i * tile, tile), pl.ds(j * tile, tile))
            masked = values_ref[at] * tile_ref[j, i].astype(jnp.float32)
            left[f, i * tile:(i + 1) * tile, j * tile:(j + 1) * tile] = masked.astype(jnp.bfloat16)

    neighbours = has_down.astype(jnp.int32) + has_up.astype(jnp.int32)
    pl.semaphore_wait(barrier, n_row * n_col - 1 + neighbours)

    def chunk(i):
        return pl.ds(i * step if isinstance(i, int) else pl.multiple_of(i * step, step), step)

    def along(source, i, up):
        part = left.at[source, chunk(i)]
        return pltpu.make_async_remote_copy(
            src_ref=part, dst_ref=part,
            send_sem=sent_left.at[int(up)], recv_sem=recv_left.at[source if up else source - 1, i],
            device_id=(r, c, f + 1 if up else f - 1), device_id_type=MESH,
        )

    late = min(helps, TRAIL)
    lead = helps - late

    def kept(i):
        return (i >= lead) & (i < CHUNKS - late)

    def lent_at(h):
        return h if h < lead else h - helps + CHUNKS

    def sends_up(i):
        return has_up & (kept(i) | (f + 1 < n_fib - 1))

    def sends_down(i):
        return has_down & (kept(i) | (f - 1 > 0))

    def gets_up(i):
        return kept(i) | has_up

    def gets_down(i):
        return kept(i) | has_down

    def right_at(ref, col, place, b):
        return ref.at[
            pl.ds(pl.multiple_of(place * rows + b * unit, unit), unit),
            pl.ds(pl.multiple_of(col * unit, unit), unit),
        ]

    def block(source, b):
        return left.at[source, pl.ds(b * unit, unit)]

    def to_right(t, b):
        return pltpu.make_async_remote_copy(
            src_ref=block(f, b), dst_ref=right_at(right, c, seat, b),
            send_sem=sent_right.at[0], recv_sem=recv_right.at[b],
            device_id=(t * group + seat, owner, f), device_id_type=MESH,
        )

    def arrived(ref, recv, b):
        for less in range(2):
            if n_col > less:
                @pl.when(mine == bool(less))
                def _():
                    theirs = ref.at[pl.ds(0, unit), pl.ds(0, (n_col - less) * unit)]
                    pltpu.make_async_remote_copy(
                        src_ref=theirs, dst_ref=theirs, send_sem=sent_right.at[0],
                        recv_sem=recv.at[b], device_id=(r, c, f), device_id_type=MESH,
                    ).wait_recv()

    def to_far(col, b):
        return pltpu.make_async_remote_copy(
            src_ref=right_at(right, col, seat, b), dst_ref=right_at(right_far, col, seat, b),
            send_sem=sent_far.at[0], recv_sem=recv_far.at[b],
            device_id=(r, c, mate), device_id_type=MESH,
        )

    def to_side(t, b):
        return pltpu.make_async_remote_copy(
            src_ref=block(mate, b), dst_ref=right_at(right_far, c, seat, b),
            send_sem=sent_far.at[0], recv_sem=recv_far.at[b],
            device_id=(t * group + seat, c, f), device_id_type=MESH,
        )

    def pairing(ref, send, recv):
        def to_pair(col, b, other):
            return pltpu.make_async_remote_copy(
                src_ref=right_at(ref, col, seat, b), dst_ref=right_at(ref, col, seat, b),
                send_sem=send.at[0], recv_sem=recv.at[seat],
                device_id=(owner * group + other, c, f), device_id_type=MESH,
            )

        def came_pair(other, blocks):
            theirs = ref.at[pl.ds(other * rows, blocks * unit)]
            return pltpu.make_async_remote_copy(
                src_ref=theirs, dst_ref=theirs, send_sem=send.at[0], recv_sem=recv.at[other],
                device_id=(r, c, f), device_id_type=MESH,
            )

        return to_pair, came_pair

    to_pair, came_pair = pairing(right, sent_pair, recv_pair)
    to_far_pair, came_far_pair = pairing(right_far, sent_helper, recv_far_pair)

    def crossing(out, into, send, recv, share):
        def to_col(col, i):
            return pltpu.make_async_remote_copy(
                src_ref=out.at[col, chunk(i)], dst_ref=into.at[c, chunk(i)],
                send_sem=send.at[0],
                recv_sem=recv.at[lax.rem(c - col + n_col, n_col) - 1, i // share],
                device_id=(r, col, f), device_id_type=MESH,
            )

        def came_col(col, i):
            both = into.at[col, pl.ds(i * step, share * step)]
            return pltpu.make_async_remote_copy(
                src_ref=both, dst_ref=both, send_sem=send.at[0],
                recv_sem=recv.at[lax.rem(col - c + n_col, n_col) - 1, i // share],
                device_id=(r, col, f), device_id_type=MESH,
            )

        return to_col, came_col

    to_col, came_col = crossing(part_out, part_in, sent_part, recv_part, 2)
    to_help, came_help = crossing(help_out, help_in, sent_helper, recv_help, 1)

    def to_done(i):
        return pltpu.make_async_remote_copy(
            src_ref=helped.at[chunk(i)], dst_ref=helped.at[chunk(i)],
            send_sem=sent_helper.at[0], recv_sem=recv_done.at[i],
            device_id=(r, c, mate), device_id_type=MESH,
        )

    def skips(place, far):
        return (far >= place * parts) & (far < (place + 1) * parts)

    def to_owner(col, i):
        return pltpu.make_async_remote_copy(
            src_ref=help_out.at[col, chunk(i)], dst_ref=help_in.at[c, chunk(i)],
            send_sem=sent_helper.at[0], recv_sem=recv_done.at[i],
            device_id=(r, col, mate), device_id_type=MESH,
        )

    def came_owner(i):
        all_cols = help_in.at[pl.ds(0, n_col), chunk(i)]
        return pltpu.make_async_remote_copy(
            src_ref=all_cols, dst_ref=all_cols, send_sem=sent_helper.at[0], recv_sem=recv_done.at[i],
            device_id=(r, c, f), device_id_type=MESH,
        )

    def served(place, b):
        return place * parts + b != mate

    def to_serve(b):
        return seat * parts + b != f

    def send_own(i, now_down, now_up):
        @pl.when(sends_down(i) & now_down)
        def _():
            along(f, i, False).start()

        @pl.when(sends_up(i) & now_up)
        def _():
            along(f, i, True).start()

    low, high = f == 1, f == n_fib - 2
    inner = jnp.logical_not(outer)
    direct_down = outer | jnp.logical_not(high)
    direct_up = outer | jnp.logical_not(low)

    @pl.loop(0, CHUNKS)
    def _(i):
        send_own(i, direct_down | (i < AHEAD), direct_up | (i < AHEAD))

    for b in range(parts):
        for t in range(n_row // group):
            @pl.when(jnp.logical_not(mine & (owner == t)))
            def _():
                to_right(t, b).start()

    @pl.when(mine)
    def _():
        for b in range(parts):
            spot = right_at(right, c, seat, b)
            spot[...] = left[f, b * unit:(b + 1) * unit]

    def pass_up(d, i):
        @pl.when((f - d >= 0) & gets_up(i))
        def _():
            along(f - d, i, True).wait_recv()

            @pl.when(sends_up(i))
            def _():
                along(f - d, i, True).start()

    def pass_down(d, i):
        @pl.when((f + d < n_fib) & gets_down(i))
        def _():
            along(f + d, i, False).wait_recv()

            @pl.when(sends_down(i))
            def _():
                along(f + d, i, False).start()

    def feed(i):
        @pl.when(low)
        def _():
            pass_up(1, i)

        @pl.when(high)
        def _():
            pass_down(1, i)

        @pl.when(i + AHEAD < CHUNKS)
        def _():
            send_own(i + AHEAD, high, low)

    def near(i):
        @pl.when(jnp.logical_not(low))
        def _():
            pass_up(1, i)

        @pl.when(jnp.logical_not(high))
        def _():
            pass_down(1, i)

    def far(i):
        for d in range(2, n_fib - 1):
            pass_up(d, i)
            pass_down(d, i)

    def side(b):
        @pl.when(helper & mine & served(seat, b))
        def _():
            for t in range(n_row // group):
                @pl.when(owner != t)
                def _():
                    to_side(t, b).start()

            spot = right_at(right_far, c, seat, b)
            spot[...] = left[mate, b * unit:(b + 1) * unit]

    def gather(b):
        arrived(right, recv_right, b)
        for col in range(n_col):
            if helps:
                @pl.when(outer & (c != col) & to_serve(b))
                def _():
                    to_far(col, b).start()

            for other in range(group):
                @pl.when(seat != other)
                def _():
                    to_pair(col, b, other).start()

    half = CHUNKS // 2

    def approach(first, last):
        @pl.when(inner)
        def _():
            @pl.loop(first, last)
            def _(p):
                feed(2 * p)
                near(p)
                feed(2 * p + 1)

                @pl.when(p > 1)
                def _():
                    far(p - 2)

    for b in range(parts):
        approach(half * b // parts, half * (b + 1) // parts)
        if helps:
            side(b)
        if b < parts - 1:
            gather(b)

    @pl.when(inner)
    def _():
        near(half)

    gather(parts - 1)

    for other in range(group):
        @pl.when(seat != other)
        def _():
            came_pair(other, parts).wait_recv()

    def products(ref, part, first, count):
        return jnp.dot(
            jnp.concatenate([left[first + k, part, :] for k in range(count)], axis=1),
            ref[pl.ds(first * unit if isinstance(first, int) else pl.multiple_of(first * unit, unit), count * unit), :],
            preferred_element_type=jnp.float32,
        )

    def store(total, ours, part, out):
        kept_total = total[:, :unit]
        for col in range(n_col):
            piece = total[:, col * unit:(col + 1) * unit]
            out[col, part, :] = piece.astype(jnp.bfloat16)
            if col:
                kept_total = jnp.where(c == col, piece, kept_total)
        ours[part, :] = kept_total

    def col_at(shift):
        return lax.rem(c + shift, n_col)

    folded[...] = jnp.zeros((8, unit), jnp.float32)

    def combine(i, h=None):
        part = chunk(i)
        expanded = own[part, :]
        def await_two():
            for shift in range(1, n_col):
                came_col(col_at(shift), i).wait_recv()

        if not isinstance(i, int):
            pl.when(lax.rem(i, 2) == 0)(await_two)
        elif i % 2 == 0:
            await_two()

        for shift in range(1, n_col):
            expanded += part_in[col_at(shift), part, :].astype(jnp.float32)
        if h is not None and h >= lead:
            came_owner(h).wait_recv()
            for col in range(n_col):
                expanded += help_in[col, pl.ds(h * step, step), :].astype(jnp.float32)
        elif h is not None:
            to_done(h).wait_recv()
            expanded += helped[pl.ds(h * step, step), :].astype(jnp.float32)
        squared = expanded * expanded
        own[part, :] = squared
        folded[...] += jnp.sum(squared.reshape(step // 8, 8, unit), axis=0)

    def fetch(b):
        @pl.when(served(seat, b))
        def _():
            arrived(right_far, recv_far, b)
            for col in range(n_col):
                for other in range(group):
                    @pl.when(seat != other)
                    def _():
                        to_far_pair(col, b, other).start()

    def answer():
        for other in range(group):
            for skipped in range(2):
                @pl.when((seat != other) & (skips(other, mate) == bool(skipped)))
                def _():
                    came_far_pair(other, parts - skipped).wait_recv()

        if lead:
            reckon(0, lead)

    def reckon(h, count):
        part = pl.ds(lent_at(h) * step, count * step)
        total = products(right_far, part, jnp.where(mate == 0, 1, 0), n_fib - 1)
        store(total, help_own, pl.ds(h * step, count * step), help_out)
        for i in range(h, h + count):
            for shift in range(n_col):
                if h >= lead:
                    to_owner(col_at(shift), i).start()
                elif shift:
                    to_help(col_at(shift), i).start()

    if helps:
        @pl.when(outer)
        def _():
            for h in range(helps):
                i = lent_at(h)
                part = pl.ds(i * step, step)
                store(products(right, part, f, 1), own, part, part_out)
                for shift in range(1, n_col):
                    to_col(col_at(shift), i).start()

    def advance(i):
        odd = lax.rem(i, 2) == 1

        @pl.when(i == 0)
        def _():
            near(half + 1)

        @pl.when((i < CHUNKS - 5) & jnp.logical_not(odd))
        def _():
            far(half - 2 + i // 2)

        @pl.when((i <= CHUNKS - 5) & odd)
        def _():
            near(half + 2 + i // 2)

        @pl.when((i >= CHUNKS - 5) & (i < CHUNKS - 1))
        def _():
            far(i + 1)

    @pl.loop(0, CHUNKS)
    def _(i):
        part = chunk(i)
        full = kept(i) | jnp.logical_not(outer)

        @pl.when(outer & full)
        def _():
            for d in range(1, n_fib - 1):
                pass_up(d, i)
                pass_down(d, i)
            partial[...] = products(right, part, jnp.where(has_down, 1, 0), n_fib - 1)
            pass_up(n_fib - 1, i)
            pass_down(n_fib - 1, i)
            total = partial[...] + products(right, part, jnp.where(has_down, 0, n_fib - 1), 1)
            store(total, own, part, part_out)

        if helps:
            @pl.when(helper & (i == ANSWER))
            def _():
                answer()

        @pl.when(inner & (i >= ANSWER))
        def _():
            advance(i)

        for h in range(lead, helps):
            @pl.when(helper & (i == max(lent_at(h) - 1, ANSWER)))
            def _():
                reckon(h, 1)

        @pl.when(inner)
        def _():
            store(products(right, part, 0, n_fib), own, part, part_out)

        @pl.when(full)
        def _():
            for shift in range(1, n_col):
                to_col(col_at(shift), i).start()

        if helps:
            for b in range(parts):
                @pl.when(helper & (i == (FIRST_FETCH if b < parts - 1 else FETCH)))
                def _():
                    fetch(b)

        @pl.when(inner & (i < ANSWER))
        def _():
            advance(i)

        @pl.when((i >= LAG) & (kept(i - LAG) | jnp.logical_not(outer)))
        def _():
            combine(i - LAG)

    def reply(h):
        @pl.when(helper)
        def _():
            part = pl.ds(h * step, step)
            total = help_own[part, :]
            for shift in range(1, n_col):
                came_help(col_at(shift), h).wait_recv()
                total += help_in[col_at(shift), part, :].astype(jnp.float32)
            helped[part, :] = total.astype(jnp.bfloat16)
            to_done(h).start()

    for h in range(lead):
        reply(h)

    @pl.loop(CHUNKS - LAG, CHUNKS)
    def _(i):
        @pl.when(kept(i) | inner)
        def _():
            combine(i)

    if helps:
        @pl.when(outer)
        def _():
            for h in range(helps):
                combine(lent_at(h), h)

    def to_row(shift):
        return pltpu.make_async_remote_copy(
            src_ref=sums.at[r], dst_ref=sums.at[r],
            send_sem=sent_sum.at[0], recv_sem=recv_sum.at[0],
            device_id=(lax.rem(r + shift, n_row), c, f), device_id_type=MESH,
        )

    def came_rows():
        return pltpu.make_async_remote_copy(
            src_ref=sums.at[pl.ds(0, n_row - 1)], dst_ref=sums.at[pl.ds(0, n_row - 1)],
            send_sem=sent_sum.at[0], recv_sem=recv_sum.at[0],
            device_id=(r, c, f), device_id_type=MESH,
        )

    sums[r] = jnp.sum(folded[...], axis=0, keepdims=True)
    for shift in range(1, n_row):
        to_row(shift).start()
    came_rows().wait_recv()
    total = sums[0]
    for other in range(1, n_row):
        total += sums[other]
    scale = total / (rows * n_row) + 1e-6
    inverse = 1.0 / scale
    for i in range(rows // tile):
        for j in range(unit // tile):
            across = slice(j * tile, (j + 1) * tile)
            factor_ref[i:i + 1, across] = inverse[:, across] * keep_ref[j, i].astype(jnp.float32)

    def left_behind(sem, ref):
        pltpu.make_async_remote_copy(
            src_ref=ref, dst_ref=ref, send_sem=sem, recv_sem=recv_sum.at[0],
            device_id=(r, c, f), device_id_type=MESH,
        ).wait_send()

    few = helps * step
    for at in range(n_fib):
        @pl.when(f == at)
        def _():
            if at < n_fib - 1:
                less = few if at == n_fib - 2 else 0
                left_behind(sent_left.at[1], left.at[pl.ds(0, at + 1), pl.ds(0, rows - less)])
            if at > 0:
                less = few if at == 1 else 0
                left_behind(sent_left.at[0], left.at[pl.ds(0, n_fib - at), pl.ds(0, rows - less)])

    for less in range(2):
        if n_col > less:
            @pl.when(mine == bool(less))
            def _():
                left_behind(sent_right.at[0], part_out.at[pl.ds(0, n_col - less)])

    if group > 1:
        left_behind(sent_pair.at[0], right.at[pl.ds(0, (group - 1) * rows)])
    if n_col > 1:
        left_behind(sent_part.at[0], part_out.at[pl.ds(0, n_col - 1)])
    if n_row > 1:
        left_behind(sent_sum.at[0], sums.at[pl.ds(0, n_row - 1)])

    if helps:
        for less in range(2):
            size = (parts - less) * unit
            across = pl.ds(0, (n_col - 1) * unit)
            if size and n_col > 1:
                @pl.when(skips(seat, jnp.where(outer, f, mate)) == bool(less))
                def _():
                    @pl.when(outer | (helper & mine))
                    def _():
                        left_behind(sent_far.at[0], right.at[pl.ds(0, size), across])

            @pl.when(helper & (skips(seat, mate) == bool(less)))
            def _():
                left_behind(sent_helper.at[0], right_far.at[pl.ds(0, (group - 1) * size + few)])


def prune(squared_ref, factor_ref, out_hbm, out_vmem, sem):
    tile = out_vmem.shape[0] // factor_ref.shape[0]
    size = tile // SLICES
    for i in range(factor_ref.shape[0] * SLICES):
        down = slice(i * size, (i + 1) * size)
        at = i // SLICES
        out_vmem[down] = squared_ref[down] * factor_ref[at:at + 1]
        pltpu.make_async_copy(out_vmem.at[down], out_hbm.at[down], sem.at[0]).start()
    pltpu.make_async_copy(out_vmem, out_hbm, sem.at[0]).wait()


def solution(mesh):
    n_row, n_col, n_fib = (mesh.shape[name] for name in ("row", "col", "fiber"))
    group = n_row // n_col
    helps = HELP if n_fib > 3 else 0

    def local(values, tile_mask, keep_mask):
        rows, unit = values.shape
        dma = pltpu.SemaphoreType.DMA
        parts = rows // unit
        few = rows // CHUNKS * HELP
        squared, factor = pl.pallas_call(
            functools.partial(kernel, n_row, n_col, n_fib, helps),
            out_shape=(
                pltpu.VMEM((rows, unit), jnp.float32),
                pltpu.VMEM((tile_mask.shape[0], unit), jnp.float32),
            ),
            in_specs=[
                pl.BlockSpec(memory_space=pltpu.HBM),
                pl.BlockSpec(memory_space=pltpu.HBM),
                pl.BlockSpec(memory_space=pltpu.HBM),
            ],
            out_specs=(
                pl.BlockSpec(memory_space=pltpu.VMEM),
                pl.BlockSpec(memory_space=pltpu.VMEM),
            ),
            scratch_shapes=[
                pltpu.SMEM(tile_mask.shape[::-1], jnp.int32),
                pltpu.SMEM(keep_mask.shape[::-1], jnp.int32),
                pltpu.VMEM((rows, unit), jnp.float32),
                pltpu.VMEM((n_fib, rows, unit), jnp.bfloat16),
                pltpu.VMEM((group * rows, n_col * unit), jnp.bfloat16),
                pltpu.VMEM((n_col, rows, unit), jnp.bfloat16),
                pltpu.VMEM((n_col, rows, unit), jnp.bfloat16),
                pltpu.VMEM((8, unit), jnp.float32),
                pltpu.VMEM((n_row, 1, unit), jnp.float32),
                pltpu.VMEM((rows // CHUNKS, n_col * unit), jnp.float32),
                pltpu.VMEM((group * rows, n_col * unit), jnp.bfloat16),
                pltpu.VMEM((few, unit), jnp.float32),
                pltpu.VMEM((n_col, few, unit), jnp.bfloat16),
                pltpu.VMEM((n_col, few, unit), jnp.bfloat16),
                pltpu.VMEM((few, unit), jnp.bfloat16),
                dma((3,)),
                dma((2,)),
                dma((1,)),
                dma((1,)),
                dma((1,)),
                dma((1,)),
                dma((1,)),
                dma((1,)),
                dma((n_fib - 1, CHUNKS)),
                dma((parts,)),
                dma((group,)),
                dma((n_col - 1, CHUNKS // 2)),
                dma((1,)),
                dma((parts,)),
                dma((group,)),
                dma((n_col - 1, max(HELP - TRAIL, 1))),
                dma((HELP,)),
            ],
            compiler_params=pltpu.CompilerParams(
                collective_id=0, has_side_effects=True, vmem_limit_bytes=VMEM_LIMIT
            ),
            name="expand",
        )(tile_mask.T, keep_mask.T, values)
        return pl.pallas_call(
            prune,
            out_shape=jax.ShapeDtypeStruct((rows, unit), jnp.float32),
            in_specs=[
                pl.BlockSpec(memory_space=pltpu.VMEM),
                pl.BlockSpec(memory_space=pltpu.VMEM),
            ],
            out_specs=pl.BlockSpec(memory_space=pl.ANY),
            scratch_shapes=[
                pltpu.VMEM((rows, unit), jnp.float32),
                dma((1,)),
            ],
            compiler_params=pltpu.CompilerParams(vmem_limit_bytes=8 * 1024 * 1024),
            name="prune",
        )(squared, factor)

    spec = P("row", ("col", "fiber"))
    return jax.shard_map(
        local, mesh=mesh, in_specs=(spec, spec, spec), out_specs=spec, check_vma=False
    )
```

```python
import functools

import jax
import jax.numpy as jnp
from jax import lax
from jax.experimental import pallas as pl
from jax.experimental.pallas import tpu as pltpu
from jax.sharding import PartitionSpec as P

MESH = pl.DeviceIdType.MESH
CHUNKS = 12
HELP = 3
TRAIL = 1
AHEAD = 4
FIRST_FETCH = 4
FETCH = 7
ANSWER = 9
LAG = 5
SLICES = 4
VMEM_LIMIT = 62 * 1024 * 1024


def kernel(
    n_row, n_col, n_fib, helps, tile_hbm, keep_hbm, values_hbm, own, factor_ref,
    tile_ref, keep_ref, values_ref, left, right, part_out, part_in, folded, sums, partial,
    right_far, help_own, help_out, help_in, helped, load_sem,
    sent_left, sent_right, sent_pair, sent_part, sent_sum, sent_far, sent_helper,
    recv_left, recv_right, recv_pair, recv_part, recv_sum,
    recv_far, recv_far_pair, recv_help, recv_done,
):
    r, c, f = lax.axis_index("row"), lax.axis_index("col"), lax.axis_index("fiber")
    rows, unit = values_ref.shape
    tile = unit // tile_ref.shape[0]
    step = rows // CHUNKS
    parts = rows // unit
    group = n_row // n_col
    owner, seat = r // group, lax.rem(r, group)

    load = pltpu.make_async_copy(values_hbm, values_ref, load_sem.at[0])
    load.start()
    load_tile = pltpu.make_async_copy(tile_hbm, tile_ref, load_sem.at[1])
    load_tile.start()
    load_keep = pltpu.make_async_copy(keep_hbm, keep_ref, load_sem.at[2])
    load_keep.start()

    barrier = pltpu.get_barrier_semaphore()

    def greet(row, col):
        pl.semaphore_signal(barrier, inc=1, device_id=(row, col, f), device_id_type=MESH)

    for t in range(n_row // group):
        @pl.when((owner != c) & (owner != t))
        def _():
            greet(t * group + seat, owner)

    for dc in range(1, n_col):
        col = lax.rem(c + dc, n_col)

        @pl.when((owner != c) & (owner != col))
        def _():
            greet(c * group + seat, col)

        greet(r, col)

    for dr in range(1, n_row):
        greet(lax.rem(r + dr, n_row), c)

    peers = n_row + n_col - 2 + jnp.where(owner == c, 0, 2 * n_col - 3)

    has_down, has_up = f > 0, f < n_fib - 1
    outer = jnp.logical_not(has_down & has_up)
    helper = (f == 1) | (f == n_fib - 2)
    mate = jnp.where(outer, jnp.where(has_down, f - 1, 1), jnp.where(f == 1, 0, n_fib - 1))
    mine = owner == c

    @pl.when(has_down)
    def _():
        pl.semaphore_signal(barrier, inc=1, device_id=(r, c, f - 1), device_id_type=MESH)

    @pl.when(has_up)
    def _():
        pl.semaphore_signal(barrier, inc=1, device_id=(r, c, f + 1), device_id_type=MESH)

    load_tile.wait()
    load_keep.wait()
    load.wait()

    for i in range(rows // tile):
        for j in range(unit // tile):
            at = (pl.ds(i * tile, tile), pl.ds(j * tile, tile))
            masked = values_ref[at] * tile_ref[j, i].astype(jnp.float32)
            left[f, i * tile:(i + 1) * tile, j * tile:(j + 1) * tile] = masked.astype(jnp.bfloat16)

    neighbours = has_down.astype(jnp.int32) + has_up.astype(jnp.int32)
    pl.semaphore_wait(barrier, peers + neighbours)

    def chunk(i):
        return pl.ds(i * step if isinstance(i, int) else pl.multiple_of(i * step, step), step)

    def along(source, i, up):
        part = left.at[source, chunk(i)]
        return pltpu.make_async_remote_copy(
            src_ref=part, dst_ref=part,
            send_sem=sent_left.at[int(up)], recv_sem=recv_left.at[source if up else source - 1, i],
            device_id=(r, c, f + 1 if up else f - 1), device_id_type=MESH,
        )

    late = min(helps, TRAIL)
    lead = helps - late

    def kept(i):
        return (i >= lead) & (i < CHUNKS - late)

    def lent_at(h):
        return h if h < lead else h - helps + CHUNKS

    def sends_up(i):
        return has_up & (kept(i) | (f + 1 < n_fib - 1))

    def sends_down(i):
        return has_down & (kept(i) | (f - 1 > 0))

    def gets_up(i):
        return kept(i) | has_up

    def gets_down(i):
        return kept(i) | has_down

    def right_at(ref, col, place, b):
        return ref.at[
            pl.ds(pl.multiple_of(place * rows + b * unit, unit), unit),
            pl.ds(pl.multiple_of(col * unit, unit), unit),
        ]

    def block(source, b):
        return left.at[source, pl.ds(b * unit, unit)]

    def to_right(t, b):
        return pltpu.make_async_remote_copy(
            src_ref=block(f, b), dst_ref=right_at(right, c, seat, b),
            send_sem=sent_right.at[0], recv_sem=recv_right.at[b],
            device_id=(t * group + seat, owner, f), device_id_type=MESH,
        )

    def arrived(ref, recv, b):
        for less in range(2):
            if n_col > less:
                @pl.when(mine == bool(less))
                def _():
                    theirs = ref.at[pl.ds(0, unit), pl.ds(0, (n_col - less) * unit)]
                    pltpu.make_async_remote_copy(
                        src_ref=theirs, dst_ref=theirs, send_sem=sent_right.at[0],
                        recv_sem=recv.at[b], device_id=(r, c, f), device_id_type=MESH,
                    ).wait_recv()

    def to_far(col, b):
        return pltpu.make_async_remote_copy(
            src_ref=right_at(right, col, seat, b), dst_ref=right_at(right_far, col, seat, b),
            send_sem=sent_far.at[0], recv_sem=recv_far.at[b],
            device_id=(r, c, mate), device_id_type=MESH,
        )

    def to_side(t, b):
        return pltpu.make_async_remote_copy(
            src_ref=block(mate, b), dst_ref=right_at(right_far, c, seat, b),
            send_sem=sent_far.at[0], recv_sem=recv_far.at[b],
            device_id=(t * group + seat, c, f), device_id_type=MESH,
        )

    def pairing(ref, send, recv):
        def to_pair(col, b, other):
            return pltpu.make_async_remote_copy(
                src_ref=right_at(ref, col, seat, b), dst_ref=right_at(ref, col, seat, b),
                send_sem=send.at[0], recv_sem=recv.at[seat],
                device_id=(owner * group + other, c, f), device_id_type=MESH,
            )

        def came_pair(other, blocks):
            theirs = ref.at[pl.ds(other * rows, blocks * unit)]
            return pltpu.make_async_remote_copy(
                src_ref=theirs, dst_ref=theirs, send_sem=send.at[0], recv_sem=recv.at[other],
                device_id=(r, c, f), device_id_type=MESH,
            )

        return to_pair, came_pair

    to_pair, came_pair = pairing(right, sent_pair, recv_pair)
    to_far_pair, came_far_pair = pairing(right_far, sent_helper, recv_far_pair)

    def crossing(out, into, send, recv, share):
        def to_col(col, i):
            return pltpu.make_async_remote_copy(
                src_ref=out.at[col, chunk(i)], dst_ref=into.at[c, chunk(i)],
                send_sem=send.at[0],
                recv_sem=recv.at[lax.rem(c - col + n_col, n_col) - 1, i // share],
                device_id=(r, col, f), device_id_type=MESH,
            )

        def came_col(col, i):
            both = into.at[col, pl.ds(i * step, share * step)]
            return pltpu.make_async_remote_copy(
                src_ref=both, dst_ref=both, send_sem=send.at[0],
                recv_sem=recv.at[lax.rem(col - c + n_col, n_col) - 1, i // share],
                device_id=(r, col, f), device_id_type=MESH,
            )

        return to_col, came_col

    to_col, came_col = crossing(part_out, part_in, sent_part, recv_part, 2)
    to_help, came_help = crossing(help_out, help_in, sent_helper, recv_help, 1)

    def to_done(i):
        return pltpu.make_async_remote_copy(
            src_ref=helped.at[chunk(i)], dst_ref=helped.at[chunk(i)],
            send_sem=sent_helper.at[0], recv_sem=recv_done.at[i],
            device_id=(r, c, mate), device_id_type=MESH,
        )

    def skips(place, far):
        return (far >= place * parts) & (far < (place + 1) * parts)

    def to_owner(col, i):
        return pltpu.make_async_remote_copy(
            src_ref=help_out.at[col, chunk(i)], dst_ref=help_in.at[c, chunk(i)],
            send_sem=sent_helper.at[0], recv_sem=recv_done.at[i],
            device_id=(r, col, mate), device_id_type=MESH,
        )

    def came_owner(i):
        all_cols = help_in.at[pl.ds(0, n_col), chunk(i)]
        return pltpu.make_async_remote_copy(
            src_ref=all_cols, dst_ref=all_cols, send_sem=sent_helper.at[0], recv_sem=recv_done.at[i],
            device_id=(r, c, f), device_id_type=MESH,
        )

    def served(place, b):
        return place * parts + b != mate

    def to_serve(b):
        return seat * parts + b != f

    def send_own(i, now_down, now_up):
        @pl.when(sends_down(i) & now_down)
        def _():
            along(f, i, False).start()

        @pl.when(sends_up(i) & now_up)
        def _():
            along(f, i, True).start()

    low, high = f == 1, f == n_fib - 2
    inner = jnp.logical_not(outer)
    direct_down = outer | jnp.logical_not(high)
    direct_up = outer | jnp.logical_not(low)

    @pl.loop(0, CHUNKS)
    def _(i):
        send_own(i, direct_down | (i < AHEAD), direct_up | (i < AHEAD))

    for b in range(parts):
        for t in range(n_row // group):
            @pl.when(jnp.logical_not(mine & (owner == t)))
            def _():
                to_right(t, b).start()

    @pl.when(mine)
    def _():
        for b in range(parts):
            spot = right_at(right, c, seat, b)
            spot[...] = left[f, b * unit:(b + 1) * unit]

    def pass_up(d, i):
        @pl.when((f - d >= 0) & gets_up(i))
        def _():
            along(f - d, i, True).wait_recv()

            @pl.when(sends_up(i))
            def _():
                along(f - d, i, True).start()

    def pass_down(d, i):
        @pl.when((f + d < n_fib) & gets_down(i))
        def _():
            along(f + d, i, False).wait_recv()

            @pl.when(sends_down(i))
            def _():
                along(f + d, i, False).start()

    def feed(i):
        @pl.when(low)
        def _():
            pass_up(1, i)

        @pl.when(high)
        def _():
            pass_down(1, i)

        @pl.when(i + AHEAD < CHUNKS)
        def _():
            send_own(i + AHEAD, high, low)

    def near(i):
        @pl.when(jnp.logical_not(low))
        def _():
            pass_up(1, i)

        @pl.when(jnp.logical_not(high))
        def _():
            pass_down(1, i)

    def far(i):
        for d in range(2, n_fib - 1):
            pass_up(d, i)
            pass_down(d, i)

    def side(b):
        @pl.when(helper & mine & served(seat, b))
        def _():
            for t in range(n_row // group):
                @pl.when(owner != t)
                def _():
                    to_side(t, b).start()

            spot = right_at(right_far, c, seat, b)
            spot[...] = left[mate, b * unit:(b + 1) * unit]

    def gather(b):
        arrived(right, recv_right, b)
        for col in range(n_col):
            if helps:
                @pl.when(outer & (c != col) & to_serve(b))
                def _():
                    to_far(col, b).start()

            for other in range(group):
                @pl.when(seat != other)
                def _():
                    to_pair(col, b, other).start()

    half = CHUNKS // 2

    def approach(first, last):
        @pl.when(inner)
        def _():
            @pl.loop(first, last)
            def _(p):
                feed(2 * p)
                near(p)
                feed(2 * p + 1)

                @pl.when(p > 1)
                def _():
                    far(p - 2)

    for b in range(parts):
        approach(half * b // parts, half * (b + 1) // parts)
        if helps:
            side(b)
        if b < parts - 1:
            gather(b)

    @pl.when(inner)
    def _():
        near(half)

    gather(parts - 1)

    for other in range(group):
        @pl.when(seat != other)
        def _():
            came_pair(other, parts).wait_recv()

    def products(ref, part, first, count):
        return jnp.dot(
            jnp.concatenate([left[first + k, part, :] for k in range(count)], axis=1),
            ref[pl.ds(first * unit if isinstance(first, int) else pl.multiple_of(first * unit, unit), count * unit), :],
            preferred_element_type=jnp.float32,
        )

    def store(total, ours, part, out):
        kept_total = total[:, :unit]
        for col in range(n_col):
            piece = total[:, col * unit:(col + 1) * unit]
            out[col, part, :] = piece.astype(jnp.bfloat16)
            if col:
                kept_total = jnp.where(c == col, piece, kept_total)
        ours[part, :] = kept_total

    def col_at(shift):
        return lax.rem(c + shift, n_col)

    folded[...] = jnp.zeros((8, unit), jnp.float32)

    def combine(i, h=None):
        part = chunk(i)
        expanded = own[part, :]
        def await_two():
            for shift in range(1, n_col):
                came_col(col_at(shift), i).wait_recv()

        if not isinstance(i, int):
            pl.when(lax.rem(i, 2) == 0)(await_two)
        elif i % 2 == 0:
            await_two()

        for shift in range(1, n_col):
            expanded += part_in[col_at(shift), part, :].astype(jnp.float32)
        if h is not None and h >= lead:
            came_owner(h).wait_recv()
            for col in range(n_col):
                expanded += help_in[col, pl.ds(h * step, step), :].astype(jnp.float32)
        elif h is not None:
            to_done(h).wait_recv()
            expanded += helped[pl.ds(h * step, step), :].astype(jnp.float32)
        squared = expanded * expanded
        own[part, :] = squared
        folded[...] += jnp.sum(squared.reshape(step // 8, 8, unit), axis=0)

    def fetch(b):
        @pl.when(served(seat, b))
        def _():
            arrived(right_far, recv_far, b)
            for col in range(n_col):
                for other in range(group):
                    @pl.when(seat != other)
                    def _():
                        to_far_pair(col, b, other).start()

    def answer():
        for other in range(group):
            for skipped in range(2):
                @pl.when((seat != other) & (skips(other, mate) == bool(skipped)))
                def _():
                    came_far_pair(other, parts - skipped).wait_recv()

        if lead:
            reckon(0, lead)

    def reckon(h, count):
        part = pl.ds(lent_at(h) * step, count * step)
        total = products(right_far, part, jnp.where(mate == 0, 1, 0), n_fib - 1)
        store(total, help_own, pl.ds(h * step, count * step), help_out)
        for i in range(h, h + count):
            for shift in range(n_col):
                if h >= lead:
                    to_owner(col_at(shift), i).start()
                elif shift:
                    to_help(col_at(shift), i).start()

    if helps:
        @pl.when(outer)
        def _():
            for h in range(helps):
                i = lent_at(h)
                part = pl.ds(i * step, step)
                store(products(right, part, f, 1), own, part, part_out)
                for shift in range(1, n_col):
                    to_col(col_at(shift), i).start()

    def advance(i):
        odd = lax.rem(i, 2) == 1

        @pl.when(i == 0)
        def _():
            near(half + 1)

        @pl.when((i < CHUNKS - 5) & jnp.logical_not(odd))
        def _():
            far(half - 2 + i // 2)

        @pl.when((i <= CHUNKS - 5) & odd)
        def _():
            near(half + 2 + i // 2)

        @pl.when((i >= CHUNKS - 5) & (i < CHUNKS - 1))
        def _():
            far(i + 1)

    @pl.loop(0, CHUNKS)
    def _(i):
        part = chunk(i)
        full = kept(i) | jnp.logical_not(outer)

        @pl.when(outer & full)
        def _():
            for d in range(1, n_fib - 1):
                pass_up(d, i)
                pass_down(d, i)
            partial[...] = products(right, part, jnp.where(has_down, 1, 0), n_fib - 1)
            pass_up(n_fib - 1, i)
            pass_down(n_fib - 1, i)
            total = partial[...] + products(right, part, jnp.where(has_down, 0, n_fib - 1), 1)
            store(total, own, part, part_out)

        if helps:
            @pl.when(helper & (i == ANSWER))
            def _():
                answer()

        @pl.when(inner & (i >= ANSWER))
        def _():
            advance(i)

        for h in range(lead, helps):
            @pl.when(helper & (i == max(lent_at(h) - 1, ANSWER)))
            def _():
                reckon(h, 1)

        @pl.when(inner)
        def _():
            store(products(right, part, 0, n_fib), own, part, part_out)

        @pl.when(full)
        def _():
            for shift in range(1, n_col):
                to_col(col_at(shift), i).start()

        if helps:
            for b in range(parts):
                @pl.when(helper & (i == (FIRST_FETCH if b < parts - 1 else FETCH)))
                def _():
                    fetch(b)

        @pl.when(inner & (i < ANSWER))
        def _():
            advance(i)

        @pl.when((i >= LAG) & (kept(i - LAG) | jnp.logical_not(outer)))
        def _():
            combine(i - LAG)

    def reply(h):
        @pl.when(helper)
        def _():
            part = pl.ds(h * step, step)
            total = help_own[part, :]
            for shift in range(1, n_col):
                came_help(col_at(shift), h).wait_recv()
                total += help_in[col_at(shift), part, :].astype(jnp.float32)
            helped[part, :] = total.astype(jnp.bfloat16)
            to_done(h).start()

    for h in range(lead):
        reply(h)

    @pl.loop(CHUNKS - LAG, CHUNKS)
    def _(i):
        @pl.when(kept(i) | inner)
        def _():
            combine(i)

    if helps:
        @pl.when(outer)
        def _():
            for h in range(helps):
                combine(lent_at(h), h)

    def to_row(shift):
        return pltpu.make_async_remote_copy(
            src_ref=sums.at[r], dst_ref=sums.at[r],
            send_sem=sent_sum.at[0], recv_sem=recv_sum.at[0],
            device_id=(lax.rem(r + shift, n_row), c, f), device_id_type=MESH,
        )

    def came_rows():
        return pltpu.make_async_remote_copy(
            src_ref=sums.at[pl.ds(0, n_row - 1)], dst_ref=sums.at[pl.ds(0, n_row - 1)],
            send_sem=sent_sum.at[0], recv_sem=recv_sum.at[0],
            device_id=(r, c, f), device_id_type=MESH,
        )

    sums[r] = jnp.sum(folded[...], axis=0, keepdims=True)
    for shift in range(1, n_row):
        to_row(shift).start()
    came_rows().wait_recv()
    total = sums[0]
    for other in range(1, n_row):
        total += sums[other]
    scale = total / (rows * n_row) + 1e-6
    inverse = 1.0 / scale
    for i in range(rows // tile):
        for j in range(unit // tile):
            across = slice(j * tile, (j + 1) * tile)
            factor_ref[i:i + 1, across] = inverse[:, across] * keep_ref[j, i].astype(jnp.float32)

    def left_behind(sem, ref):
        pltpu.make_async_remote_copy(
            src_ref=ref, dst_ref=ref, send_sem=sem, recv_sem=recv_sum.at[0],
            device_id=(r, c, f), device_id_type=MESH,
        ).wait_send()

    few = helps * step
    for at in range(n_fib):
        @pl.when(f == at)
        def _():
            if at < n_fib - 1:
                less = few if at == n_fib - 2 else 0
                left_behind(sent_left.at[1], left.at[pl.ds(0, at + 1), pl.ds(0, rows - less)])
            if at > 0:
                less = few if at == 1 else 0
                left_behind(sent_left.at[0], left.at[pl.ds(0, n_fib - at), pl.ds(0, rows - less)])

    for less in range(2):
        if n_col > less:
            @pl.when(mine == bool(less))
            def _():
                left_behind(sent_right.at[0], part_out.at[pl.ds(0, n_col - less)])

    if group > 1:
        left_behind(sent_pair.at[0], right.at[pl.ds(0, (group - 1) * rows)])
    if n_col > 1:
        left_behind(sent_part.at[0], part_out.at[pl.ds(0, n_col - 1)])
    if n_row > 1:
        left_behind(sent_sum.at[0], sums.at[pl.ds(0, n_row - 1)])

    if helps:
        for less in range(2):
            size = (parts - less) * unit
            across = pl.ds(0, (n_col - 1) * unit)
            if size and n_col > 1:
                @pl.when(skips(seat, jnp.where(outer, f, mate)) == bool(less))
                def _():
                    @pl.when(outer | (helper & mine))
                    def _():
                        left_behind(sent_far.at[0], right.at[pl.ds(0, size), across])

            @pl.when(helper & (skips(seat, mate) == bool(less)))
            def _():
                left_behind(sent_helper.at[0], right_far.at[pl.ds(0, (group - 1) * size + few)])


def prune(squared_ref, factor_ref, out_hbm, out_vmem, sem):
    tile = out_vmem.shape[0] // factor_ref.shape[0]
    size = tile // SLICES
    for i in range(factor_ref.shape[0] * SLICES):
        down = slice(i * size, (i + 1) * size)
        at = i // SLICES
        out_vmem[down] = squared_ref[down] * factor_ref[at:at + 1]
        pltpu.make_async_copy(out_vmem.at[down], out_hbm.at[down], sem.at[0]).start()
    pltpu.make_async_copy(out_vmem, out_hbm, sem.at[0]).wait()


def solution(mesh):
    n_row, n_col, n_fib = (mesh.shape[name] for name in ("row", "col", "fiber"))
    group = n_row // n_col
    helps = HELP if n_fib > 3 else 0

    def local(values, tile_mask, keep_mask):
        rows, unit = values.shape
        dma = pltpu.SemaphoreType.DMA
        parts = rows // unit
        few = rows // CHUNKS * HELP
        squared, factor = pl.pallas_call(
            functools.partial(kernel, n_row, n_col, n_fib, helps),
            out_shape=(
                pltpu.VMEM((rows, unit), jnp.float32),
                pltpu.VMEM((tile_mask.shape[0], unit), jnp.float32),
            ),
            in_specs=[
                pl.BlockSpec(memory_space=pltpu.HBM),
                pl.BlockSpec(memory_space=pltpu.HBM),
                pl.BlockSpec(memory_space=pltpu.HBM),
            ],
            out_specs=(
                pl.BlockSpec(memory_space=pltpu.VMEM),
                pl.BlockSpec(memory_space=pltpu.VMEM),
            ),
            scratch_shapes=[
                pltpu.SMEM(tile_mask.shape[::-1], jnp.int32),
                pltpu.SMEM(keep_mask.shape[::-1], jnp.int32),
                pltpu.VMEM((rows, unit), jnp.float32),
                pltpu.VMEM((n_fib, rows, unit), jnp.bfloat16),
                pltpu.VMEM((group * rows, n_col * unit), jnp.bfloat16),
                pltpu.VMEM((n_col, rows, unit), jnp.bfloat16),
                pltpu.VMEM((n_col, rows, unit), jnp.bfloat16),
                pltpu.VMEM((8, unit), jnp.float32),
                pltpu.VMEM((n_row, 1, unit), jnp.float32),
                pltpu.VMEM((rows // CHUNKS, n_col * unit), jnp.float32),
                pltpu.VMEM((group * rows, n_col * unit), jnp.bfloat16),
                pltpu.VMEM((few, unit), jnp.float32),
                pltpu.VMEM((n_col, few, unit), jnp.bfloat16),
                pltpu.VMEM((n_col, few, unit), jnp.bfloat16),
                pltpu.VMEM((few, unit), jnp.bfloat16),
                dma((3,)),
                dma((2,)),
                dma((1,)),
                dma((1,)),
                dma((1,)),
                dma((1,)),
                dma((1,)),
                dma((1,)),
                dma((n_fib - 1, CHUNKS)),
                dma((parts,)),
                dma((group,)),
                dma((n_col - 1, CHUNKS // 2)),
                dma((1,)),
                dma((parts,)),
                dma((group,)),
                dma((n_col - 1, max(HELP - TRAIL, 1))),
                dma((HELP,)),
            ],
            compiler_params=pltpu.CompilerParams(
                collective_id=0, has_side_effects=True, vmem_limit_bytes=VMEM_LIMIT
            ),
            name="expand",
        )(tile_mask.T, keep_mask.T, values)
        return pl.pallas_call(
            prune,
            out_shape=jax.ShapeDtypeStruct((rows, unit), jnp.float32),
            in_specs=[
                pl.BlockSpec(memory_space=pltpu.VMEM),
                pl.BlockSpec(memory_space=pltpu.VMEM),
            ],
            out_specs=pl.BlockSpec(memory_space=pl.ANY),
            scratch_shapes=[
                pltpu.VMEM((rows, unit), jnp.float32),
                dma((1,)),
            ],
            compiler_params=pltpu.CompilerParams(vmem_limit_bytes=8 * 1024 * 1024),
            name="prune",
        )(squared, factor)

    spec = P("row", ("col", "fiber"))
    return jax.shard_map(
        local, mesh=mesh, in_specs=(spec, spec, spec), out_specs=spec, check_vma=False
    )
```

```python
import functools

import jax
import jax.numpy as jnp
from jax import lax
from jax.experimental import pallas as pl
from jax.experimental.pallas import tpu as pltpu
from jax.sharding import PartitionSpec as P

MESH = pl.DeviceIdType.MESH
CHUNKS = 12
HELP = 3
TRAIL = 1
AHEAD = 4
FIRST_FETCH = 4
FETCH = 7
ANSWER = 9
LAG = 5
SLICES = 4
VMEM_LIMIT = 62 * 1024 * 1024


def kernel(
    n_row, n_col, n_fib, helps, tile_hbm, keep_hbm, values_hbm, own, factor_ref,
    tile_ref, keep_ref, values_ref, left, right, part_out, part_in, folded, sums, partial,
    right_far, help_own, help_out, help_in, helped, load_sem,
    sent_left, sent_right, sent_pair, sent_part, sent_sum, sent_far, sent_helper,
    recv_left, recv_right, recv_pair, recv_part, recv_sum,
    recv_far, recv_far_pair, recv_help, recv_done,
):
    r, c, f = lax.axis_index("row"), lax.axis_index("col"), lax.axis_index("fiber")
    rows, unit = values_ref.shape
    tile = unit // tile_ref.shape[0]
    step = rows // CHUNKS
    parts = rows // unit
    group = n_row // n_col
    owner, seat = r // group, lax.rem(r, group)

    load = pltpu.make_async_copy(values_hbm, values_ref, load_sem.at[0])
    for i in range(rows // tile):
        down = pl.ds(i * tile, tile)
        pltpu.make_async_copy(values_hbm.at[down], values_ref.at[down], load_sem.at[0]).start()
    load_tile = pltpu.make_async_copy(tile_hbm, tile_ref, load_sem.at[1])
    load_tile.start()
    load_keep = pltpu.make_async_copy(keep_hbm, keep_ref, load_sem.at[2])
    load_keep.start()

    barrier = pltpu.get_barrier_semaphore()

    def greet(row, col):
        pl.semaphore_signal(barrier, inc=1, device_id=(row, col, f), device_id_type=MESH)

    for t in range(n_row // group):
        @pl.when((owner != c) & (owner != t))
        def _():
            greet(t * group + seat, owner)

    for dc in range(1, n_col):
        col = lax.rem(c + dc, n_col)

        @pl.when((owner != c) & (owner != col))
        def _():
            greet(c * group + seat, col)

        greet(r, col)

    for dr in range(1, n_row):
        greet(lax.rem(r + dr, n_row), c)

    peers = n_row + n_col - 2 + jnp.where(owner == c, 0, 2 * n_col - 3)

    has_down, has_up = f > 0, f < n_fib - 1
    outer = jnp.logical_not(has_down & has_up)
    helper = (f == 1) | (f == n_fib - 2)
    mate = jnp.where(outer, jnp.where(has_down, f - 1, 1), jnp.where(f == 1, 0, n_fib - 1))
    mine = owner == c

    @pl.when(has_down)
    def _():
        pl.semaphore_signal(barrier, inc=1, device_id=(r, c, f - 1), device_id_type=MESH)

    @pl.when(has_up)
    def _():
        pl.semaphore_signal(barrier, inc=1, device_id=(r, c, f + 1), device_id_type=MESH)

    load_tile.wait()
    load_keep.wait()
    load.wait()

    for i in range(rows // tile):
        for j in range(unit // tile):
            at = (pl.ds(i * tile, tile), pl.ds(j * tile, tile))
            masked = values_ref[at] * tile_ref[j, i].astype(jnp.float32)
            left[f, i * tile:(i + 1) * tile, j * tile:(j + 1) * tile] = masked.astype(jnp.bfloat16)

    neighbours = has_down.astype(jnp.int32) + has_up.astype(jnp.int32)
    pl.semaphore_wait(barrier, peers + neighbours)

    def chunk(i):
        return pl.ds(i * step if isinstance(i, int) else pl.multiple_of(i * step, step), step)

    def along(source, i, up):
        part = left.at[source, chunk(i)]
        return pltpu.make_async_remote_copy(
            src_ref=part, dst_ref=part,
            send_sem=sent_left.at[int(up)], recv_sem=recv_left.at[source if up else source - 1, i],
            device_id=(r, c, f + 1 if up else f - 1), device_id_type=MESH,
        )

    late = min(helps, TRAIL)
    lead = helps - late

    def kept(i):
        return (i >= lead) & (i < CHUNKS - late)

    def lent_at(h):
        return h if h < lead else h - helps + CHUNKS

    def sends_up(i):
        return has_up & (kept(i) | (f + 1 < n_fib - 1))

    def sends_down(i):
        return has_down & (kept(i) | (f - 1 > 0))

    def gets_up(i):
        return kept(i) | has_up

    def gets_down(i):
        return kept(i) | has_down

    def right_at(ref, col, place, b):
        return ref.at[
            pl.ds(pl.multiple_of(place * rows + b * unit, unit), unit),
            pl.ds(pl.multiple_of(col * unit, unit), unit),
        ]

    def block(source, b):
        return left.at[source, pl.ds(b * unit, unit)]

    def to_right(t, b):
        return pltpu.make_async_remote_copy(
            src_ref=block(f, b), dst_ref=right_at(right, c, seat, b),
            send_sem=sent_right.at[0], recv_sem=recv_right.at[b],
            device_id=(t * group + seat, owner, f), device_id_type=MESH,
        )

    def arrived(ref, recv, b):
        for less in range(2):
            if n_col > less:
                @pl.when(mine == bool(less))
                def _():
                    theirs = ref.at[pl.ds(0, unit), pl.ds(0, (n_col - less) * unit)]
                    pltpu.make_async_remote_copy(
                        src_ref=theirs, dst_ref=theirs, send_sem=sent_right.at[0],
                        recv_sem=recv.at[b], device_id=(r, c, f), device_id_type=MESH,
                    ).wait_recv()

    def to_far(col, b):
        return pltpu.make_async_remote_copy(
            src_ref=right_at(right, col, seat, b), dst_ref=right_at(right_far, col, seat, b),
            send_sem=sent_far.at[0], recv_sem=recv_far.at[b],
            device_id=(r, c, mate), device_id_type=MESH,
        )

    def to_side(t, b):
        return pltpu.make_async_remote_copy(
            src_ref=block(mate, b), dst_ref=right_at(right_far, c, seat, b),
            send_sem=sent_far.at[0], recv_sem=recv_far.at[b],
            device_id=(t * group + seat, c, f), device_id_type=MESH,
        )

    def pairing(ref, send, recv):
        def to_pair(col, b, other):
            return pltpu.make_async_remote_copy(
                src_ref=right_at(ref, col, seat, b), dst_ref=right_at(ref, col, seat, b),
                send_sem=send.at[0], recv_sem=recv.at[seat],
                device_id=(owner * group + other, c, f), device_id_type=MESH,
            )

        def came_pair(other, blocks):
            theirs = ref.at[pl.ds(other * rows, blocks * unit)]
            return pltpu.make_async_remote_copy(
                src_ref=theirs, dst_ref=theirs, send_sem=send.at[0], recv_sem=recv.at[other],
                device_id=(r, c, f), device_id_type=MESH,
            )

        return to_pair, came_pair

    to_pair, came_pair = pairing(right, sent_pair, recv_pair)
    to_far_pair, came_far_pair = pairing(right_far, sent_helper, recv_far_pair)

    def crossing(out, into, send, recv, share):
        def to_col(col, i):
            return pltpu.make_async_remote_copy(
                src_ref=out.at[col, chunk(i)], dst_ref=into.at[c, chunk(i)],
                send_sem=send.at[0],
                recv_sem=recv.at[lax.rem(c - col + n_col, n_col) - 1, i // share],
                device_id=(r, col, f), device_id_type=MESH,
            )

        def came_col(col, i):
            both = into.at[col, pl.ds(i * step, share * step)]
            return pltpu.make_async_remote_copy(
                src_ref=both, dst_ref=both, send_sem=send.at[0],
                recv_sem=recv.at[lax.rem(col - c + n_col, n_col) - 1, i // share],
                device_id=(r, col, f), device_id_type=MESH,
            )

        return to_col, came_col

    to_col, came_col = crossing(part_out, part_in, sent_part, recv_part, 2)
    to_help, came_help = crossing(help_out, help_in, sent_helper, recv_help, 1)

    def to_done(i):
        return pltpu.make_async_remote_copy(
            src_ref=helped.at[chunk(i)], dst_ref=helped.at[chunk(i)],
            send_sem=sent_helper.at[0], recv_sem=recv_done.at[i],
            device_id=(r, c, mate), device_id_type=MESH,
        )

    def skips(place, far):
        return (far >= place * parts) & (far < (place + 1) * parts)

    def to_owner(col, i):
        return pltpu.make_async_remote_copy(
            src_ref=help_out.at[col, chunk(i)], dst_ref=help_in.at[c, chunk(i)],
            send_sem=sent_helper.at[0], recv_sem=recv_done.at[i],
            device_id=(r, col, mate), device_id_type=MESH,
        )

    def came_owner(i):
        all_cols = help_in.at[pl.ds(0, n_col), chunk(i)]
        return pltpu.make_async_remote_copy(
            src_ref=all_cols, dst_ref=all_cols, send_sem=sent_helper.at[0], recv_sem=recv_done.at[i],
            device_id=(r, c, f), device_id_type=MESH,
        )

    def served(place, b):
        return place * parts + b != mate

    def to_serve(b):
        return seat * parts + b != f

    def send_own(i, now_down, now_up):
        @pl.when(sends_down(i) & now_down)
        def _():
            along(f, i, False).start()

        @pl.when(sends_up(i) & now_up)
        def _():
            along(f, i, True).start()

    low, high = f == 1, f == n_fib - 2
    inner = jnp.logical_not(outer)
    direct_down = outer | jnp.logical_not(high)
    direct_up = outer | jnp.logical_not(low)

    @pl.loop(0, CHUNKS)
    def _(i):
        send_own(i, direct_down | (i < AHEAD), direct_up | (i < AHEAD))

    for b in range(parts):
        for t in range(n_row // group):
            @pl.when(jnp.logical_not(mine & (owner == t)))
            def _():
                to_right(t, b).start()

    @pl.when(mine)
    def _():
        for b in range(parts):
            spot = right_at(right, c, seat, b)
            spot[...] = left[f, b * unit:(b + 1) * unit]

    def pass_up(d, i):
        @pl.when((f - d >= 0) & gets_up(i))
        def _():
            along(f - d, i, True).wait_recv()

            @pl.when(sends_up(i))
            def _():
                along(f - d, i, True).start()

    def pass_down(d, i):
        @pl.when((f + d < n_fib) & gets_down(i))
        def _():
            along(f + d, i, False).wait_recv()

            @pl.when(sends_down(i))
            def _():
                along(f + d, i, False).start()

    def feed(i):
        @pl.when(low)
        def _():
            pass_up(1, i)

        @pl.when(high)
        def _():
            pass_down(1, i)

        @pl.when(i + AHEAD < CHUNKS)
        def _():
            send_own(i + AHEAD, high, low)

    def near(i):
        @pl.when(jnp.logical_not(low))
        def _():
            pass_up(1, i)

        @pl.when(jnp.logical_not(high))
        def _():
            pass_down(1, i)

    def far(i):
        for d in range(2, n_fib - 1):
            pass_up(d, i)
            pass_down(d, i)

    def side(b):
        @pl.when(helper & mine & served(seat, b))
        def _():
            for t in range(n_row // group):
                @pl.when(owner != t)
                def _():
                    to_side(t, b).start()

            spot = right_at(right_far, c, seat, b)
            spot[...] = left[mate, b * unit:(b + 1) * unit]

    def gather(b):
        arrived(right, recv_right, b)
        for col in range(n_col):
            if helps:
                @pl.when(outer & (c != col) & to_serve(b))
                def _():
                    to_far(col, b).start()

            for other in range(group):
                @pl.when(seat != other)
                def _():
                    to_pair(col, b, other).start()

    half = CHUNKS // 2

    def approach(first, last):
        @pl.when(inner)
        def _():
            @pl.loop(first, last)
            def _(p):
                feed(2 * p)
                near(p)
                feed(2 * p + 1)

                @pl.when(p > 1)
                def _():
                    far(p - 2)

    for b in range(parts):
        approach(half * b // parts, half * (b + 1) // parts)
        if helps:
            side(b)
        if b < parts - 1:
            gather(b)

    @pl.when(inner)
    def _():
        near(half)

    gather(parts - 1)

    for other in range(group):
        @pl.when(seat != other)
        def _():
            came_pair(other, parts).wait_recv()

    def products(ref, part, first, count):
        return jnp.dot(
            jnp.concatenate([left[first + k, part, :] for k in range(count)], axis=1),
            ref[pl.ds(first * unit if isinstance(first, int) else pl.multiple_of(first * unit, unit), count * unit), :],
            preferred_element_type=jnp.float32,
        )

    def store(total, ours, part, out):
        kept_total = total[:, :unit]
        for col in range(n_col):
            piece = total[:, col * unit:(col + 1) * unit]
            out[col, part, :] = piece.astype(jnp.bfloat16)
            if col:
                kept_total = jnp.where(c == col, piece, kept_total)
        ours[part, :] = kept_total

    def col_at(shift):
        return lax.rem(c + shift, n_col)

    folded[...] = jnp.zeros((8, unit), jnp.float32)

    def combine(i, h=None):
        part = chunk(i)
        expanded = own[part, :]
        def await_two():
            for shift in range(1, n_col):
                came_col(col_at(shift), i).wait_recv()

        if not isinstance(i, int):
            pl.when(lax.rem(i, 2) == 0)(await_two)
        elif i % 2 == 0:
            await_two()

        for shift in range(1, n_col):
            expanded += part_in[col_at(shift), part, :].astype(jnp.float32)
        if h is not None and h >= lead:
            came_owner(h).wait_recv()
            for col in range(n_col):
                expanded += help_in[col, pl.ds(h * step, step), :].astype(jnp.float32)
        elif h is not None:
            to_done(h).wait_recv()
            expanded += helped[pl.ds(h * step, step), :].astype(jnp.float32)
        squared = expanded * expanded
        own[part, :] = squared
        folded[...] += jnp.sum(squared.reshape(step // 8, 8, unit), axis=0)

    def fetch(b):
        @pl.when(served(seat, b))
        def _():
            arrived(right_far, recv_far, b)
            for col in range(n_col):
                for other in range(group):
                    @pl.when(seat != other)
                    def _():
                        to_far_pair(col, b, other).start()

    def answer():
        for other in range(group):
            for skipped in range(2):
                @pl.when((seat != other) & (skips(other, mate) == bool(skipped)))
                def _():
                    came_far_pair(other, parts - skipped).wait_recv()

        if lead:
            reckon(0, lead)

    def reckon(h, count):
        part = pl.ds(lent_at(h) * step, count * step)
        total = products(right_far, part, jnp.where(mate == 0, 1, 0), n_fib - 1)
        store(total, help_own, pl.ds(h * step, count * step), help_out)
        for i in range(h, h + count):
            for shift in range(n_col):
                if h >= lead:
                    to_owner(col_at(shift), i).start()
                elif shift:
                    to_help(col_at(shift), i).start()

    if helps:
        @pl.when(outer)
        def _():
            for h in range(helps):
                i = lent_at(h)
                part = pl.ds(i * step, step)
                store(products(right, part, f, 1), own, part, part_out)
                for shift in range(1, n_col):
                    to_col(col_at(shift), i).start()

    def advance(i):
        odd = lax.rem(i, 2) == 1

        @pl.when(i == 0)
        def _():
            near(half + 1)

        @pl.when((i < CHUNKS - 5) & jnp.logical_not(odd))
        def _():
            far(half - 2 + i // 2)

        @pl.when((i <= CHUNKS - 5) & odd)
        def _():
            near(half + 2 + i // 2)

        @pl.when((i >= CHUNKS - 5) & (i < CHUNKS - 1))
        def _():
            far(i + 1)

    @pl.loop(0, CHUNKS)
    def _(i):
        part = chunk(i)
        full = kept(i) | jnp.logical_not(outer)

        @pl.when(outer & full)
        def _():
            for d in range(1, n_fib - 1):
                pass_up(d, i)
                pass_down(d, i)
            partial[...] = products(right, part, jnp.where(has_down, 1, 0), n_fib - 1)
            pass_up(n_fib - 1, i)
            pass_down(n_fib - 1, i)
            total = partial[...] + products(right, part, jnp.where(has_down, 0, n_fib - 1), 1)
            store(total, own, part, part_out)

        if helps:
            @pl.when(helper & (i == ANSWER))
            def _():
                answer()

        @pl.when(inner & (i >= ANSWER))
        def _():
            advance(i)

        for h in range(lead, helps):
            @pl.when(helper & (i == max(lent_at(h) - 1, ANSWER)))
            def _():
                reckon(h, 1)

        @pl.when(inner)
        def _():
            store(products(right, part, 0, n_fib), own, part, part_out)

        @pl.when(full)
        def _():
            for shift in range(1, n_col):
                to_col(col_at(shift), i).start()

        if helps:
            for b in range(parts):
                @pl.when(helper & (i == (FIRST_FETCH if b < parts - 1 else FETCH)))
                def _():
                    fetch(b)

        @pl.when(inner & (i < ANSWER))
        def _():
            advance(i)

        @pl.when((i >= LAG) & (kept(i - LAG) | jnp.logical_not(outer)))
        def _():
            combine(i - LAG)

    def reply(h):
        @pl.when(helper)
        def _():
            part = pl.ds(h * step, step)
            total = help_own[part, :]
            for shift in range(1, n_col):
                came_help(col_at(shift), h).wait_recv()
                total += help_in[col_at(shift), part, :].astype(jnp.float32)
            helped[part, :] = total.astype(jnp.bfloat16)
            to_done(h).start()

    for h in range(lead):
        reply(h)

    @pl.loop(CHUNKS - LAG, CHUNKS)
    def _(i):
        @pl.when(kept(i) | inner)
        def _():
            combine(i)

    if helps:
        @pl.when(outer)
        def _():
            for h in range(helps):
                combine(lent_at(h), h)

    def to_row(shift):
        return pltpu.make_async_remote_copy(
            src_ref=sums.at[r], dst_ref=sums.at[r],
            send_sem=sent_sum.at[0], recv_sem=recv_sum.at[0],
            device_id=(lax.rem(r + shift, n_row), c, f), device_id_type=MESH,
        )

    def came_rows():
        return pltpu.make_async_remote_copy(
            src_ref=sums.at[pl.ds(0, n_row - 1)], dst_ref=sums.at[pl.ds(0, n_row - 1)],
            send_sem=sent_sum.at[0], recv_sem=recv_sum.at[0],
            device_id=(r, c, f), device_id_type=MESH,
        )

    sums[r] = jnp.sum(folded[...], axis=0, keepdims=True)
    for shift in range(1, n_row):
        to_row(shift).start()
    came_rows().wait_recv()
    total = sums[0]
    for other in range(1, n_row):
        total += sums[other]
    scale = total / (rows * n_row) + 1e-6
    inverse = 1.0 / scale
    for i in range(rows // tile):
        for j in range(unit // tile):
            across = slice(j * tile, (j + 1) * tile)
            factor_ref[i:i + 1, across] = inverse[:, across] * keep_ref[j, i].astype(jnp.float32)

    def left_behind(sem, ref):
        pltpu.make_async_remote_copy(
            src_ref=ref, dst_ref=ref, send_sem=sem, recv_sem=recv_sum.at[0],
            device_id=(r, c, f), device_id_type=MESH,
        ).wait_send()

    few = helps * step
    for at in range(n_fib):
        @pl.when(f == at)
        def _():
            if at < n_fib - 1:
                less = few if at == n_fib - 2 else 0
                left_behind(sent_left.at[1], left.at[pl.ds(0, at + 1), pl.ds(0, rows - less)])
            if at > 0:
                less = few if at == 1 else 0
                left_behind(sent_left.at[0], left.at[pl.ds(0, n_fib - at), pl.ds(0, rows - less)])

    for less in range(2):
        if n_col > less:
            @pl.when(mine == bool(less))
            def _():
                left_behind(sent_right.at[0], part_out.at[pl.ds(0, n_col - less)])

    if group > 1:
        left_behind(sent_pair.at[0], right.at[pl.ds(0, (group - 1) * rows)])
    if n_col > 1:
        left_behind(sent_part.at[0], part_out.at[pl.ds(0, n_col - 1)])
    if n_row > 1:
        left_behind(sent_sum.at[0], sums.at[pl.ds(0, n_row - 1)])

    if helps:
        for less in range(2):
            size = (parts - less) * unit
            across = pl.ds(0, (n_col - 1) * unit)
            if size and n_col > 1:
                @pl.when(skips(seat, jnp.where(outer, f, mate)) == bool(less))
                def _():
                    @pl.when(outer | (helper & mine))
                    def _():
                        left_behind(sent_far.at[0], right.at[pl.ds(0, size), across])

            @pl.when(helper & (skips(seat, mate) == bool(less)))
            def _():
                left_behind(sent_helper.at[0], right_far.at[pl.ds(0, (group - 1) * size + few)])


def prune(squared_ref, factor_ref, out_hbm, out_vmem, sem):
    tile = out_vmem.shape[0] // factor_ref.shape[0]
    size = tile // SLICES
    for i in range(factor_ref.shape[0] * SLICES):
        down = slice(i * size, (i + 1) * size)
        at = i // SLICES
        out_vmem[down] = squared_ref[down] * factor_ref[at:at + 1]
        pltpu.make_async_copy(out_vmem.at[down], out_hbm.at[down], sem.at[0]).start()
    pltpu.make_async_copy(out_vmem, out_hbm, sem.at[0]).wait()


def solution(mesh):
    n_row, n_col, n_fib = (mesh.shape[name] for name in ("row", "col", "fiber"))
    group = n_row // n_col
    helps = HELP if n_fib > 3 else 0

    def local(values, tile_mask, keep_mask):
        rows, unit = values.shape
        dma = pltpu.SemaphoreType.DMA
        parts = rows // unit
        few = rows // CHUNKS * HELP
        squared, factor = pl.pallas_call(
            functools.partial(kernel, n_row, n_col, n_fib, helps),
            out_shape=(
                pltpu.VMEM((rows, unit), jnp.float32),
                pltpu.VMEM((tile_mask.shape[0], unit), jnp.float32),
            ),
            in_specs=[
                pl.BlockSpec(memory_space=pltpu.HBM),
                pl.BlockSpec(memory_space=pltpu.HBM),
                pl.BlockSpec(memory_space=pltpu.HBM),
            ],
            out_specs=(
                pl.BlockSpec(memory_space=pltpu.VMEM),
                pl.BlockSpec(memory_space=pltpu.VMEM),
            ),
            scratch_shapes=[
                pltpu.SMEM(tile_mask.shape[::-1], jnp.int32),
                pltpu.SMEM(keep_mask.shape[::-1], jnp.int32),
                pltpu.VMEM((rows, unit), jnp.float32),
                pltpu.VMEM((n_fib, rows, unit), jnp.bfloat16),
                pltpu.VMEM((group * rows, n_col * unit), jnp.bfloat16),
                pltpu.VMEM((n_col, rows, unit), jnp.bfloat16),
                pltpu.VMEM((n_col, rows, unit), jnp.bfloat16),
                pltpu.VMEM((8, unit), jnp.float32),
                pltpu.VMEM((n_row, 1, unit), jnp.float32),
                pltpu.VMEM((rows // CHUNKS, n_col * unit), jnp.float32),
                pltpu.VMEM((group * rows, n_col * unit), jnp.bfloat16),
                pltpu.VMEM((few, unit), jnp.float32),
                pltpu.VMEM((n_col, few, unit), jnp.bfloat16),
                pltpu.VMEM((n_col, few, unit), jnp.bfloat16),
                pltpu.VMEM((few, unit), jnp.bfloat16),
                dma((3,)),
                dma((2,)),
                dma((1,)),
                dma((1,)),
                dma((1,)),
                dma((1,)),
                dma((1,)),
                dma((1,)),
                dma((n_fib - 1, CHUNKS)),
                dma((parts,)),
                dma((group,)),
                dma((n_col - 1, CHUNKS // 2)),
                dma((1,)),
                dma((parts,)),
                dma((group,)),
                dma((n_col - 1, max(HELP - TRAIL, 1))),
                dma((HELP,)),
            ],
            compiler_params=pltpu.CompilerParams(
                collective_id=0, has_side_effects=True, vmem_limit_bytes=VMEM_LIMIT
            ),
            name="expand",
        )(tile_mask.T, keep_mask.T, values)
        return pl.pallas_call(
            prune,
            out_shape=jax.ShapeDtypeStruct((rows, unit), jnp.float32),
            in_specs=[
                pl.BlockSpec(memory_space=pltpu.VMEM),
                pl.BlockSpec(memory_space=pltpu.VMEM),
            ],
            out_specs=pl.BlockSpec(memory_space=pl.ANY),
            scratch_shapes=[
                pltpu.VMEM((rows, unit), jnp.float32),
                dma((1,)),
            ],
            compiler_params=pltpu.CompilerParams(vmem_limit_bytes=8 * 1024 * 1024),
            name="prune",
        )(squared, factor)

    spec = P("row", ("col", "fiber"))
    return jax.shard_map(
        local, mesh=mesh, in_specs=(spec, spec, spec), out_specs=spec, check_vma=False
    )
```

```python
import functools

import jax
import jax.numpy as jnp
from jax import lax
from jax.experimental import pallas as pl
from jax.experimental.pallas import tpu as pltpu
from jax.sharding import PartitionSpec as P

MESH = pl.DeviceIdType.MESH
CHUNKS = 12
HELP = 3
TRAIL = 1
AHEAD = 4
FIRST_FETCH = 3
FETCH = 7
ANSWER = 9
LAG = 6
SLICES = 4
VMEM_LIMIT = 62 * 1024 * 1024


def kernel(
    n_row, n_col, n_fib, helps, tile_hbm, keep_hbm, values_hbm, own, factor_ref,
    tile_ref, keep_ref, values_ref, left, right, part_out, part_in, folded, sums, partial,
    right_far, help_own, help_out, help_in, helped, load_sem,
    sent_left, sent_right, sent_pair, sent_part, sent_sum, sent_far, sent_helper,
    recv_left, recv_right, recv_pair, recv_part, recv_sum,
    recv_far, recv_far_pair, recv_help, recv_done,
):
    r, c, f = lax.axis_index("row"), lax.axis_index("col"), lax.axis_index("fiber")
    rows, unit = values_ref.shape
    tile = unit // tile_ref.shape[0]
    step = rows // CHUNKS
    parts = rows // unit
    group = n_row // n_col
    owner, seat = r // group, lax.rem(r, group)

    load = pltpu.make_async_copy(values_hbm, values_ref, load_sem.at[0])
    load.start()
    load_tile = pltpu.make_async_copy(tile_hbm, tile_ref, load_sem.at[1])
    load_tile.start()
    load_keep = pltpu.make_async_copy(keep_hbm, keep_ref, load_sem.at[2])
    load_keep.start()

    barrier = pltpu.get_barrier_semaphore()
    for dr in range(n_row):
        for dc in range(n_col):
            if dr or dc:
                pl.semaphore_signal(
                    barrier, inc=1, device_id_type=MESH,
                    device_id=(lax.rem(r + dr, n_row), lax.rem(c + dc, n_col), f),
                )

    has_down, has_up = f > 0, f < n_fib - 1
    outer = jnp.logical_not(has_down & has_up)
    helper = (f == 1) | (f == n_fib - 2)
    mate = jnp.where(outer, jnp.where(has_down, f - 1, 1), jnp.where(f == 1, 0, n_fib - 1))
    mine = owner == c

    @pl.when(has_down)
    def _():
        pl.semaphore_signal(barrier, inc=1, device_id=(r, c, f - 1), device_id_type=MESH)

    @pl.when(has_up)
    def _():
        pl.semaphore_signal(barrier, inc=1, device_id=(r, c, f + 1), device_id_type=MESH)

    load_tile.wait()
    load_keep.wait()
    load.wait()

    for i in range(rows // tile):
        for j in range(unit // tile):
            at = (pl.ds(i * tile, tile), pl.ds(j * tile, tile))
            masked = values_ref[at] * tile_ref[j, i].astype(jnp.float32)
            left[f, i * tile:(i + 1) * tile, j * tile:(j + 1) * tile] = masked.astype(jnp.bfloat16)

    neighbours = has_down.astype(jnp.int32) + has_up.astype(jnp.int32)
    pl.semaphore_wait(barrier, n_row * n_col - 1 + neighbours)

    def chunk(i):
        return pl.ds(i * step if isinstance(i, int) else pl.multiple_of(i * step, step), step)

    def along(source, i, up):
        part = left.at[source, chunk(i)]
        return pltpu.make_async_remote_copy(
            src_ref=part, dst_ref=part,
            send_sem=sent_left.at[int(up)], recv_sem=recv_left.at[source if up else source - 1, i],
            device_id=(r, c, f + 1 if up else f - 1), device_id_type=MESH,
        )

    late = min(helps, TRAIL)
    lead = helps - late

    def kept(i):
        return (i >= lead) & (i < CHUNKS - late)

    def lent_at(h):
        return h if h < lead else h - helps + CHUNKS

    def sends_up(i):
        return has_up & (kept(i) | (f + 1 < n_fib - 1))

    def sends_down(i):
        return has_down & (kept(i) | (f - 1 > 0))

    def gets_up(i):
        return kept(i) | has_up

    def gets_down(i):
        return kept(i) | has_down

    def right_at(ref, col, place, b):
        return ref.at[
            pl.ds(pl.multiple_of(place * rows + b * unit, unit), unit),
            pl.ds(pl.multiple_of(col * unit, unit), unit),
        ]

    def block(source, b):
        return left.at[source, pl.ds(b * unit, unit)]

    def to_right(t, b):
        return pltpu.make_async_remote_copy(
            src_ref=block(f, b), dst_ref=right_at(right, c, seat, b),
            send_sem=sent_right.at[0], recv_sem=recv_right.at[b],
            device_id=(t * group + seat, owner, f), device_id_type=MESH,
        )

    def arrived(ref, recv, b):
        for less in range(2):
            if n_col > less:
                @pl.when(mine == bool(less))
                def _():
                    theirs = ref.at[pl.ds(0, unit), pl.ds(0, (n_col - less) * unit)]
                    pltpu.make_async_remote_copy(
                        src_ref=theirs, dst_ref=theirs, send_sem=sent_right.at[0],
                        recv_sem=recv.at[b], device_id=(r, c, f), device_id_type=MESH,
                    ).wait_recv()

    def to_far(col, b):
        return pltpu.make_async_remote_copy(
            src_ref=right_at(right, col, seat, b), dst_ref=right_at(right_far, col, seat, b),
            send_sem=sent_far.at[0], recv_sem=recv_far.at[b],
            device_id=(r, c, mate), device_id_type=MESH,
        )

    def to_side(t, b):
        return pltpu.make_async_remote_copy(
            src_ref=block(mate, b), dst_ref=right_at(right_far, c, seat, b),
            send_sem=sent_far.at[0], recv_sem=recv_far.at[b],
            device_id=(t * group + seat, c, f), device_id_type=MESH,
        )

    def pairing(ref, send, recv):
        def to_pair(col, b, other):
            return pltpu.make_async_remote_copy(
                src_ref=right_at(ref, col, seat, b), dst_ref=right_at(ref, col, seat, b),
                send_sem=send.at[0], recv_sem=recv.at[seat],
                device_id=(owner * group + other, c, f), device_id_type=MESH,
            )

        def came_pair(other, blocks):
            theirs = ref.at[pl.ds(other * rows, blocks * unit)]
            return pltpu.make_async_remote_copy(
                src_ref=theirs, dst_ref=theirs, send_sem=send.at[0], recv_sem=recv.at[other],
                device_id=(r, c, f), device_id_type=MESH,
            )

        return to_pair, came_pair

    to_pair, came_pair = pairing(right, sent_pair, recv_pair)
    to_far_pair, came_far_pair = pairing(right_far, sent_helper, recv_far_pair)

    def crossing(out, into, send, recv, share):
        def to_col(col, i):
            return pltpu.make_async_remote_copy(
                src_ref=out.at[col, chunk(i)], dst_ref=into.at[c, chunk(i)],
                send_sem=send.at[0],
                recv_sem=recv.at[lax.rem(c - col + n_col, n_col) - 1, i // share],
                device_id=(r, col, f), device_id_type=MESH,
            )

        def came_col(col, i):
            both = into.at[col, pl.ds(i * step, share * step)]
            return pltpu.make_async_remote_copy(
                src_ref=both, dst_ref=both, send_sem=send.at[0],
                recv_sem=recv.at[lax.rem(col - c + n_col, n_col) - 1, i // share],
                device_id=(r, col, f), device_id_type=MESH,
            )

        return to_col, came_col

    to_col, came_col = crossing(part_out, part_in, sent_part, recv_part, 2)
    to_help, came_help = crossing(help_out, help_in, sent_helper, recv_help, 1)

    def to_done(i):
        return pltpu.make_async_remote_copy(
            src_ref=helped.at[chunk(i)], dst_ref=helped.at[chunk(i)],
            send_sem=sent_helper.at[0], recv_sem=recv_done.at[i],
            device_id=(r, c, mate), device_id_type=MESH,
        )

    def skips(place, far):
        return (far >= place * parts) & (far < (place + 1) * parts)

    def to_owner(col, i):
        return pltpu.make_async_remote_copy(
            src_ref=help_out.at[col, chunk(i)], dst_ref=help_in.at[c, chunk(i)],
            send_sem=sent_helper.at[0], recv_sem=recv_done.at[i],
            device_id=(r, col, mate), device_id_type=MESH,
        )

    def came_owner(i):
        all_cols = help_in.at[pl.ds(0, n_col), chunk(i)]
        return pltpu.make_async_remote_copy(
            src_ref=all_cols, dst_ref=all_cols, send_sem=sent_helper.at[0], recv_sem=recv_done.at[i],
            device_id=(r, c, f), device_id_type=MESH,
        )

    def served(place, b):
        return place * parts + b != mate

    def to_serve(b):
        return seat * parts + b != f

    def send_own(i, now_down, now_up):
        @pl.when(sends_down(i) & now_down)
        def _():
            along(f, i, False).start()

        @pl.when(sends_up(i) & now_up)
        def _():
            along(f, i, True).start()

    low, high = f == 1, f == n_fib - 2
    inner = jnp.logical_not(outer)
    direct_down = outer | jnp.logical_not(high)
    direct_up = outer | jnp.logical_not(low)

    @pl.loop(0, CHUNKS)
    def _(i):
        send_own(i, direct_down | (i < AHEAD), direct_up | (i < AHEAD))

    for b in range(parts):
        for t in range(n_row // group):
            @pl.when(jnp.logical_not(mine & (owner == t)))
            def _():
                to_right(t, b).start()

    @pl.when(mine)
    def _():
        for b in range(parts):
            spot = right_at(right, c, seat, b)
            spot[...] = left[f, b * unit:(b + 1) * unit]

    def pass_up(d, i):
        @pl.when((f - d >= 0) & gets_up(i))
        def _():
            along(f - d, i, True).wait_recv()

            @pl.when(sends_up(i))
            def _():
                along(f - d, i, True).start()

    def pass_down(d, i):
        @pl.when((f + d < n_fib) & gets_down(i))
        def _():
            along(f + d, i, False).wait_recv()

            @pl.when(sends_down(i))
            def _():
                along(f + d, i, False).start()

    def feed(i):
        @pl.when(low)
        def _():
            pass_up(1, i)

        @pl.when(high)
        def _():
            pass_down(1, i)

        @pl.when(i + AHEAD < CHUNKS)
        def _():
            send_own(i + AHEAD, high, low)

    def near(i):
        @pl.when(jnp.logical_not(low))
        def _():
            pass_up(1, i)

        @pl.when(jnp.logical_not(high))
        def _():
            pass_down(1, i)

    def far(i):
        for d in range(2, n_fib - 1):
            pass_up(d, i)
            pass_down(d, i)

    def side(b):
        @pl.when(helper & mine & served(seat, b))
        def _():
            for t in range(n_row // group):
                @pl.when(owner != t)
                def _():
                    to_side(t, b).start()

            spot = right_at(right_far, c, seat, b)
            spot[...] = left[mate, b * unit:(b + 1) * unit]

    def gather(b):
        arrived(right, recv_right, b)
        for col in range(n_col):
            if helps:
                @pl.when(outer & (c != col) & to_serve(b))
                def _():
                    to_far(col, b).start()

            for other in range(group):
                @pl.when(seat != other)
                def _():
                    to_pair(col, b, other).start()

    half = CHUNKS // 2

    def approach(first, last):
        @pl.when(inner)
        def _():
            @pl.loop(first, last)
            def _(p):
                feed(2 * p)
                near(p)
                feed(2 * p + 1)

                @pl.when(p > 1)
                def _():
                    far(p - 2)

    for b in range(parts):
        approach(half * b // parts, half * (b + 1) // parts)
        if helps:
            side(b)
        if b < parts - 1:
            gather(b)

    @pl.when(inner)
    def _():
        near(half)

    gather(parts - 1)

    for other in range(group):
        @pl.when(seat != other)
        def _():
            came_pair(other, parts).wait_recv()

    def products(ref, part, first, count):
        return jnp.dot(
            jnp.concatenate([left[first + k, part, :] for k in range(count)], axis=1),
            ref[pl.ds(first * unit if isinstance(first, int) else pl.multiple_of(first * unit, unit), count * unit), :],
            preferred_element_type=jnp.float32,
        )

    def store(total, ours, part, out):
        kept_total = total[:, :unit]
        for col in range(n_col):
            piece = total[:, col * unit:(col + 1) * unit]
            out[col, part, :] = piece.astype(jnp.bfloat16)
            if col:
                kept_total = jnp.where(c == col, piece, kept_total)
        ours[part, :] = kept_total

    def col_at(shift):
        return lax.rem(c + shift, n_col)

    folded[...] = jnp.zeros((8, unit), jnp.float32)

    def combine(i, h=None):
        part = chunk(i)
        expanded = own[part, :]
        def await_two():
            for shift in range(1, n_col):
                came_col(col_at(shift), i).wait_recv()

        if not isinstance(i, int):
            pl.when(lax.rem(i, 2) == 0)(await_two)
        elif i % 2 == 0:
            await_two()

        for shift in range(1, n_col):
            expanded += part_in[col_at(shift), part, :].astype(jnp.float32)
        if h is not None and h >= lead:
            came_owner(h).wait_recv()
            for col in range(n_col):
                expanded += help_in[col, pl.ds(h * step, step), :].astype(jnp.float32)
        elif h is not None:
            to_done(h).wait_recv()
            expanded += helped[pl.ds(h * step, step), :].astype(jnp.float32)
        squared = expanded * expanded
        own[part, :] = squared
        folded[...] += jnp.sum(squared.reshape(step // 8, 8, unit), axis=0)

    def fetch(b):
        @pl.when(served(seat, b))
        def _():
            arrived(right_far, recv_far, b)
            for col in range(n_col):
                for other in range(group):
                    @pl.when(seat != other)
                    def _():
                        to_far_pair(col, b, other).start()

    def answer():
        for other in range(group):
            for skipped in range(2):
                @pl.when((seat != other) & (skips(other, mate) == bool(skipped)))
                def _():
                    came_far_pair(other, parts - skipped).wait_recv()

        if lead:
            reckon(0, lead)

    def reckon(h, count):
        part = pl.ds(lent_at(h) * step, count * step)
        total = products(right_far, part, jnp.where(mate == 0, 1, 0), n_fib - 1)
        store(total, help_own, pl.ds(h * step, count * step), help_out)
        for i in range(h, h + count):
            for shift in range(n_col):
                if h >= lead:
                    to_owner(col_at(shift), i).start()
                elif shift:
                    to_help(col_at(shift), i).start()

    if helps:
        @pl.when(outer)
        def _():
            for h in range(helps):
                i = lent_at(h)
                part = pl.ds(i * step, step)
                store(products(right, part, f, 1), own, part, part_out)
                for shift in range(1, n_col):
                    to_col(col_at(shift), i).start()

    def advance(i):
        odd = lax.rem(i, 2) == 1

        @pl.when(i == 0)
        def _():
            near(half + 1)

        @pl.when((i < CHUNKS - 5) & jnp.logical_not(odd))
        def _():
            far(half - 2 + i // 2)

        @pl.when((i <= CHUNKS - 5) & odd)
        def _():
            near(half + 2 + i // 2)

        @pl.when((i >= CHUNKS - 5) & (i < CHUNKS - 1))
        def _():
            far(i + 1)

    @pl.loop(0, CHUNKS)
    def _(i):
        part = chunk(i)
        full = kept(i) | jnp.logical_not(outer)

        @pl.when(outer & full)
        def _():
            for d in range(1, n_fib - 1):
                pass_up(d, i)
                pass_down(d, i)
            partial[...] = products(right, part, jnp.where(has_down, 1, 0), n_fib - 1)
            pass_up(n_fib - 1, i)
            pass_down(n_fib - 1, i)
            total = partial[...] + products(right, part, jnp.where(has_down, 0, n_fib - 1), 1)
            store(total, own, part, part_out)

        if helps:
            @pl.when(helper & (i == ANSWER))
            def _():
                answer()

        @pl.when(inner & (i >= ANSWER))
        def _():
            advance(i)

        for h in range(lead, helps):
            @pl.when(helper & (i == max(lent_at(h) - 1, ANSWER)))
            def _():
                reckon(h, 1)

        @pl.when(inner)
        def _():
            store(products(right, part, 0, n_fib), own, part, part_out)

        @pl.when(full)
        def _():
            for shift in range(1, n_col):
                to_col(col_at(shift), i).start()

        if helps:
            for b in range(parts):
                @pl.when(helper & (i == (FIRST_FETCH if b < parts - 1 else FETCH)))
                def _():
                    fetch(b)

        @pl.when(inner & (i < ANSWER))
        def _():
            advance(i)

        @pl.when((i >= LAG) & (kept(i - LAG) | jnp.logical_not(outer)))
        def _():
            combine(i - LAG)

    def reply(h):
        @pl.when(helper)
        def _():
            part = pl.ds(h * step, step)
            total = help_own[part, :]
            for shift in range(1, n_col):
                came_help(col_at(shift), h).wait_recv()
                total += help_in[col_at(shift), part, :].astype(jnp.float32)
            helped[part, :] = total.astype(jnp.bfloat16)
            to_done(h).start()

    for h in range(lead):
        reply(h)

    @pl.loop(CHUNKS - LAG, CHUNKS)
    def _(i):
        @pl.when(kept(i) | inner)
        def _():
            combine(i)

    if helps:
        @pl.when(outer)
        def _():
            for h in range(helps):
                combine(lent_at(h), h)

    def to_row(shift):
        return pltpu.make_async_remote_copy(
            src_ref=sums.at[r], dst_ref=sums.at[r],
            send_sem=sent_sum.at[0], recv_sem=recv_sum.at[0],
            device_id=(lax.rem(r + shift, n_row), c, f), device_id_type=MESH,
        )

    def came_rows():
        return pltpu.make_async_remote_copy(
            src_ref=sums.at[pl.ds(0, n_row - 1)], dst_ref=sums.at[pl.ds(0, n_row - 1)],
            send_sem=sent_sum.at[0], recv_sem=recv_sum.at[0],
            device_id=(r, c, f), device_id_type=MESH,
        )

    sums[r] = jnp.sum(folded[...], axis=0, keepdims=True)
    for shift in range(1, n_row):
        to_row(shift).start()
    came_rows().wait_recv()
    total = sums[0]
    for other in range(1, n_row):
        total += sums[other]
    scale = total / (rows * n_row) + 1e-6
    inverse = 1.0 / scale
    for i in range(rows // tile):
        for j in range(unit // tile):
            across = slice(j * tile, (j + 1) * tile)
            factor_ref[i:i + 1, across] = inverse[:, across] * keep_ref[j, i].astype(jnp.float32)

    def left_behind(sem, ref):
        pltpu.make_async_remote_copy(
            src_ref=ref, dst_ref=ref, send_sem=sem, recv_sem=recv_sum.at[0],
            device_id=(r, c, f), device_id_type=MESH,
        ).wait_send()

    few = helps * step
    for at in range(n_fib):
        @pl.when(f == at)
        def _():
            if at < n_fib - 1:
                less = few if at == n_fib - 2 else 0
                left_behind(sent_left.at[1], left.at[pl.ds(0, at + 1), pl.ds(0, rows - less)])
            if at > 0:
                less = few if at == 1 else 0
                left_behind(sent_left.at[0], left.at[pl.ds(0, n_fib - at), pl.ds(0, rows - less)])

    for less in range(2):
        if n_col > less:
            @pl.when(mine == bool(less))
            def _():
                left_behind(sent_right.at[0], part_out.at[pl.ds(0, n_col - less)])

    if group > 1:
        left_behind(sent_pair.at[0], right.at[pl.ds(0, (group - 1) * rows)])
    if n_col > 1:
        left_behind(sent_part.at[0], part_out.at[pl.ds(0, n_col - 1)])
    if n_row > 1:
        left_behind(sent_sum.at[0], sums.at[pl.ds(0, n_row - 1)])

    if helps:
        for less in range(2):
            size = (parts - less) * unit
            across = pl.ds(0, (n_col - 1) * unit)
            if size and n_col > 1:
                @pl.when(skips(seat, jnp.where(outer, f, mate)) == bool(less))
                def _():
                    @pl.when(outer | (helper & mine))
                    def _():
                        left_behind(sent_far.at[0], right.at[pl.ds(0, size), across])

            @pl.when(helper & (skips(seat, mate) == bool(less)))
            def _():
                left_behind(sent_helper.at[0], right_far.at[pl.ds(0, (group - 1) * size + few)])


def prune(squared_ref, factor_ref, out_hbm, out_vmem, sem):
    tile = out_vmem.shape[0] // factor_ref.shape[0]
    size = tile // SLICES
    for i in range(factor_ref.shape[0] * SLICES):
        down = slice(i * size, (i + 1) * size)
        at = i // SLICES
        out_vmem[down] = squared_ref[down] * factor_ref[at:at + 1]
        pltpu.make_async_copy(out_vmem.at[down], out_hbm.at[down], sem.at[0]).start()
    pltpu.make_async_copy(out_vmem, out_hbm, sem.at[0]).wait()


def solution(mesh):
    n_row, n_col, n_fib = (mesh.shape[name] for name in ("row", "col", "fiber"))
    group = n_row // n_col
    helps = HELP if n_fib > 3 else 0

    def local(values, tile_mask, keep_mask):
        rows, unit = values.shape
        dma = pltpu.SemaphoreType.DMA
        parts = rows // unit
        few = rows // CHUNKS * HELP
        squared, factor = pl.pallas_call(
            functools.partial(kernel, n_row, n_col, n_fib, helps),
            out_shape=(
                pltpu.VMEM((rows, unit), jnp.float32),
                pltpu.VMEM((tile_mask.shape[0], unit), jnp.float32),
            ),
            in_specs=[
                pl.BlockSpec(memory_space=pltpu.HBM),
                pl.BlockSpec(memory_space=pltpu.HBM),
                pl.BlockSpec(memory_space=pltpu.HBM),
            ],
            out_specs=(
                pl.BlockSpec(memory_space=pltpu.VMEM),
                pl.BlockSpec(memory_space=pltpu.VMEM),
            ),
            scratch_shapes=[
                pltpu.SMEM(tile_mask.shape[::-1], jnp.int32),
                pltpu.SMEM(keep_mask.shape[::-1], jnp.int32),
                pltpu.VMEM((rows, unit), jnp.float32),
                pltpu.VMEM((n_fib, rows, unit), jnp.bfloat16),
                pltpu.VMEM((group * rows, n_col * unit), jnp.bfloat16),
                pltpu.VMEM((n_col, rows, unit), jnp.bfloat16),
                pltpu.VMEM((n_col, rows, unit), jnp.bfloat16),
                pltpu.VMEM((8, unit), jnp.float32),
                pltpu.VMEM((n_row, 1, unit), jnp.float32),
                pltpu.VMEM((rows // CHUNKS, n_col * unit), jnp.float32),
                pltpu.VMEM((group * rows, n_col * unit), jnp.bfloat16),
                pltpu.VMEM((few, unit), jnp.float32),
                pltpu.VMEM((n_col, few, unit), jnp.bfloat16),
                pltpu.VMEM((n_col, few, unit), jnp.bfloat16),
                pltpu.VMEM((few, unit), jnp.bfloat16),
                dma((3,)),
                dma((2,)),
                dma((1,)),
                dma((1,)),
                dma((1,)),
                dma((1,)),
                dma((1,)),
                dma((1,)),
                dma((n_fib - 1, CHUNKS)),
                dma((parts,)),
                dma((group,)),
                dma((n_col - 1, CHUNKS // 2)),
                dma((1,)),
                dma((parts,)),
                dma((group,)),
                dma((n_col - 1, max(HELP - TRAIL, 1))),
                dma((HELP,)),
            ],
            compiler_params=pltpu.CompilerParams(
                collective_id=0, has_side_effects=True, vmem_limit_bytes=VMEM_LIMIT
            ),
            name="expand",
        )(tile_mask.T, keep_mask.T, values)
        return pl.pallas_call(
            prune,
            out_shape=jax.ShapeDtypeStruct((rows, unit), jnp.float32),
            in_specs=[
                pl.BlockSpec(memory_space=pltpu.VMEM),
                pl.BlockSpec(memory_space=pltpu.VMEM),
            ],
            out_specs=pl.BlockSpec(memory_space=pl.ANY),
            scratch_shapes=[
                pltpu.VMEM((rows, unit), jnp.float32),
                dma((1,)),
            ],
            compiler_params=pltpu.CompilerParams(vmem_limit_bytes=8 * 1024 * 1024),
            name="prune",
        )(squared, factor)

    spec = P("row", ("col", "fiber"))
    return jax.shard_map(
        local, mesh=mesh, in_specs=(spec, spec, spec), out_specs=spec, check_vma=False
    )
```
